256 devices in a mesh: pipe: 8 (over y, core), expert: 32 (over x, z).
Axes of the slice: x: 4, y: 4, z: 8, core: 2. Of those that a mesh axis runs over, the one named last changes fastest.
Arguments:
- acts: bfloat16 [8, 2, 2048, 1440], P('pipe', None, 'expert'), may hold values from -6 to 6
- hidden: bfloat16 [8, 2, 2048, 4, 1440], P('pipe', None, 'expert'), may hold values from -6 to 6
- ids: int32 [8, 2, 2048, 4], P('pipe', None, 'expert'), may hold values from 0 to 31, all different within a row; in each aligned block of 64 rows (0 to 63, 64 to 127, ..., all dimensions but the last counted through in order) at most 12 rows name the same one
- version: int32 [8, 2], P('pipe'), may hold values from 0 to 1
- router: bfloat16 [8, 2, 1440, 32], P('pipe'), may hold values from -0.078125 to 0.078125
- down: bfloat16 [8, 32, 1440, 1440], P('pipe', 'expert'), may hold values from -0.15625 to 0.15625
- grad_top: bfloat16 [2, 2048, 1440], P(None, 'expert'), may hold values from -6 to 6
Outputs:
- grad_in: bfloat16 [8, 2, 2048, 1440], P('pipe', None, 'expert')
- grad_hidden: bfloat16 [8, 2, 2048, 4, 1440], P('pipe', None, 'expert')
- grad_router: float32 [8, 1440, 32], P('pipe', 'expert')
The draws below stay inside these ranges and needn't reach their ends.
Inputs may be any that keep to these rules, and one draw needn't show every extreme that they name: `ids`: each token names 4 different experts. In the rows of one device for one section and micro-batch (aligned blocks of 64 tokens) no expert is named by more than 12 slots, and some blocks reach 12.
All inputs are finite; a program needn't handle non-finite values.
Results may differ from the reference program's by a relative error of at most 0.019.
Values may be sent and summed in bfloat16 or wider, within the bound.
No kernel may reach another device: no remote copies, remote signals or barrier semaphores. Data moves between devices by JAX's collectives and lax.ppermute only.
A program may use at most 64 MiB of HBM per device.

```python
import math
import jax
import jax.numpy as jnp
import numpy as np
from jax import lax

D = 1440
FFW = 1440
TOP = 4
MB = 2
VERSIONS = 2
TOK_DEV = 64
SECTIONS = 8
EXPERTS = 32
TOKENS = 2048
SLOT = 12
N_EXPERT = 32


def place_ends(values, own_key, smallest, largest):
    shape = values.shape
    spot = [jax.random.randint(jax.random.fold_in(own_key, axis), (), 0, shape[axis]) for axis in range(len(shape))]
    values = values.at[tuple(spot)].set(smallest)
    longest = shape.index(max(shape))
    spot[longest] = (spot[longest] + 1) % shape[longest]
    return values.at[tuple(spot)].set(largest)


def with_spikes(entries, own_key, source, target, shards_of, factor):
    def block_of(axis_at):
        return (jnp.arange(entries.shape[axis_at]) // (entries.shape[axis_at] // shards_of)).reshape((-1,) + (1,) * (entries.ndim - 1 - axis_at))

    first = jax.random.permutation(own_key, shards_of)[block_of(target)]
    other_side = (block_of(target) + shards_of // 2) % shards_of
    return jnp.where((block_of(source) == first) | (block_of(source) == other_side), factor * entries, entries)


def level_of(own_key, shape, split, low, top_value):
    factor_of = 1.0
    for dim, shards_of in split:
        draws = jax.random.uniform(jax.random.fold_in(jax.random.fold_in(own_key, 6), dim), (shards_of,), jnp.float32, low / len(split), top_value / len(split))
        factor_of = factor_of * jnp.repeat(jnp.exp(draws), shape[dim] // shards_of).reshape((-1,) + (1,) * (len(shape) - 1 - dim))
    return factor_of


def shared_out(own_key, own, number, rows, amount, top, limit, lean):
    sequence = jax.random.permutation(own_key, amount)
    packed, usual = portions_of(amount, rows * top, limit, lean, True), portions_of(amount, rows * top, limit, lean, False)
    places = jnp.arange(amount)

    def named(sizes, offset_by):
        used = int((sizes > 0).sum())
        fixed = max(1, used // 4)
        moved = fixed + (places - fixed + offset_by * (used - fixed)) % max(1, amount - fixed)
        return jnp.zeros((amount,), jnp.int32).at[sequence[jnp.where(places < fixed, places, moved)]].set(jnp.asarray(sizes, jnp.int32))

    sizes = jnp.where(number % 4 == 0, named(packed, number // 4), named(usual, number - number // 4 - 1))
    mixed = jax.random.permutation(jax.random.fold_in(own, 3), amount)
    giver, receiver = mixed[0:amount // 2 * 2:2], mixed[1:amount // 2 * 2:2]
    slack = jnp.minimum(sizes[giver] - 1, limit - sizes[receiver]) // 2
    slack = jnp.where((giver == sequence[0]) | (receiver == sequence[0]) | (sizes[receiver] == 0), 0, jnp.maximum(slack, 0))
    moved = jax.random.randint(jax.random.fold_in(own, 4), (amount // 2,), 0, 1 << 20) % (slack + 1)
    sizes = sizes.at[giver].add(-moved).at[receiver].add(moved)
    items = jnp.searchsorted(jnp.cumsum(sizes), jnp.arange(rows * top), side="right").astype(jnp.int32)
    table = items.reshape(top, rows).T
    table = table[jax.random.permutation(jax.random.fold_in(own, 1), rows)]
    offset_by = jax.random.randint(jax.random.fold_in(own, 2), (rows, 1), 0, top)
    return jnp.take_along_axis(table, (jnp.arange(top)[None, :] + offset_by) % top, axis=1)


def portions_of(count, total, bound, lean, full):
    weights = [(1 << 20) // math.isqrt(standing ** lean) + 1 for standing in range(1, count + 1)]
    largest = bound if full else min(bound, max(-(-total // count), total * weights[0] // sum(weights)))
    least = 1 if total - largest >= count - 1 else 0
    counts, spare = [largest] + [least] * (count - 1), total - largest - least * (count - 1)
    while spare > 0:
        candidates = [i for i in range(1, count) if counts[i] < largest] or [i for i in range(1, count) if counts[i] < bound]
        pool, left = sum([weights[i] for i in candidates]), spare
        for i in candidates:
            addition = min(bound - counts[i], max(1, left * weights[i] // pool), spare)
            counts[i] = counts[i] + addition
            spare = spare - addition
    return np.array(counts)


def scatter_about(rng, shape, width, bound, pieces=(), held_as=jnp.bfloat16):
    values = width * jax.random.normal(rng, shape, jnp.float32)
    if pieces:
        values = values * level_of(rng, shape, pieces, -0.22, 0.18)
    return jnp.clip(values, -bound, bound).astype(held_as)


def bell_draw_with(key, dims, width, reach, pieces, heavy, held_as=jnp.bfloat16):
    drawn = width * jax.random.normal(key, dims, jnp.float32)
    if pieces:
        drawn = drawn * level_of(key, dims, pieces, -0.22, 0.18)
    return jnp.clip(with_spikes(drawn, jax.random.fold_in(key, 3), *heavy), -reach, reach).astype(held_as)


def setup_inputs(seed: int = 0) -> dict:
    streams_of = jax.random.split(jax.random.key(seed), 8)
    acts = bell_draw_with(streams_of[0], (SECTIONS, MB, TOKENS, D), 1.0, 6.0, ((0, 8), (2, 32)), (2, 3, 32, 2.75))
    hidden = scatter_about(streams_of[1], (SECTIONS, MB, TOKENS, TOP, FFW), 1.0, 6.0, ((0, 8), (2, 32)))
    ids_keys = jax.random.split(jax.random.fold_in(streams_of[2], 1), SECTIONS * MB * TOKENS // TOK_DEV)
    ids_turns = jax.random.permutation(jax.random.fold_in(streams_of[2], 3), SECTIONS * MB * TOKENS // TOK_DEV)
    ids = jax.vmap(lambda own, number: shared_out(jax.random.fold_in(streams_of[2], 2), own, number, TOK_DEV, EXPERTS, TOP, SLOT, 2))(ids_keys, ids_turns).reshape((SECTIONS, MB, TOKENS, TOP))
    version = place_ends(jax.random.randint(streams_of[3], (SECTIONS, MB), 0, VERSIONS), jax.random.fold_in(streams_of[3], 1), 0, VERSIONS - 1).astype(jnp.int32)
    router = scatter_about(streams_of[4], (SECTIONS, VERSIONS, D, EXPERTS), (4 * D) ** -0.5, 0.078125, ((0, 8),))
    down = scatter_about(streams_of[5], (SECTIONS, EXPERTS, FFW, D), FFW ** -0.5, 0.15625, ((0, 8), (1, 32)))
    grad_top = scatter_about(streams_of[6], (MB, TOKENS, D), 1.0, 6.0, ((1, 32),))
    return dict(acts=acts, hidden=hidden, ids=ids, version=version, router=router, down=down, grad_top=grad_top)


def slot_places(flat_ids):
    labels = jnp.arange(EXPERTS, dtype=jnp.int32)
    markers = (flat_ids[:, None] == labels[None, :]).astype(jnp.int32)
    ranking = jnp.cumsum(markers, axis=0) - 1
    return jnp.sum(ranking * markers, axis=1).astype(jnp.int32)


def expert_apply(row_data, flat_ids, places, matrices, transposed):
    capacity = N_EXPERT * SLOT
    buffer = jnp.zeros((EXPERTS, capacity, row_data.shape[1]), jnp.float32)
    buffer = buffer.at[flat_ids, places].set(row_data.astype(jnp.float32))
    if transposed:
        result = jnp.einsum("erd,efd->erf", buffer, matrices, precision=lax.Precision.HIGHEST)
    else:
        result = jnp.einsum("erf,efd->erd", buffer, matrices, precision=lax.Precision.HIGHEST)
    return result[flat_ids, places]


def reference(acts, hidden, ids, version, router, down, grad_top):
    labels = jnp.arange(EXPERTS, dtype=jnp.int32)
    upstream = [grad_top[micro_batch] for micro_batch in range(MB)]
    grad_in = [None] * SECTIONS
    grad_hidden = [None] * SECTIONS
    grad_router = [None] * SECTIONS
    for section_id in range(SECTIONS - 1, -1, -1):
        matrices = down[section_id].astype(jnp.float32)
        router_sum = jnp.zeros((D, EXPERTS), jnp.float32)
        input_list = []
        hidden_list = []
        for micro_batch in range(MB):
            router_table = jnp.take(router[section_id], version[section_id, micro_batch], axis=0)
            picked = ids[section_id, micro_batch][:, :, None] == labels[None, None, :]
            logits = jnp.dot(acts[section_id, micro_batch], router_table, preferred_element_type=jnp.float32)
            chosen = jnp.sum(jnp.where(picked, logits[:, None, :], 0.0), axis=2)
            scores = jnp.exp(chosen)
            gating = scores / jnp.sum(scores, axis=1, keepdims=True)
            flat_ids = ids[section_id, micro_batch].reshape(-1)
            places = slot_places(flat_ids)
            outputs = expert_apply(hidden[section_id, micro_batch].reshape(-1, FFW), flat_ids, places, matrices, False)
            outputs = outputs.astype(jnp.bfloat16).reshape(TOKENS, TOP, D)
            incoming = upstream[micro_batch]
            grad_gating = jnp.einsum("tkd,td->tk", outputs.astype(jnp.float32), incoming.astype(jnp.float32), precision=lax.Precision.HIGHEST)
            grad_chosen = gating * (grad_gating - jnp.sum(gating * grad_gating, axis=1, keepdims=True))
            grad_logits = jnp.sum(jnp.where(picked, grad_chosen[:, :, None], 0.0), axis=1).astype(jnp.bfloat16)
            passed = incoming.astype(jnp.float32) + jnp.dot(grad_logits, router_table.T, preferred_element_type=jnp.float32)
            passed = passed.astype(jnp.bfloat16)
            scaled = (gating[:, :, None] * incoming[:, None, :].astype(jnp.float32)).astype(jnp.bfloat16)
            hidden_grads = expert_apply(scaled.reshape(-1, D), flat_ids, places, matrices, True)
            hidden_grads = hidden_grads.astype(jnp.bfloat16).reshape(TOKENS, TOP, FFW)
            router_sum = router_sum + jnp.dot(acts[section_id, micro_batch].T, grad_logits, preferred_element_type=jnp.float32)
            upstream[micro_batch] = passed
            input_list.append(passed)
            hidden_list.append(hidden_grads)
        grad_in[section_id] = jnp.stack(input_list)
        grad_hidden[section_id] = jnp.stack(hidden_list)
        grad_router[section_id] = router_sum / TOK_DEV
    return jnp.stack(grad_in), jnp.stack(grad_hidden), jnp.stack(grad_router)
```

```python
import functools

import jax
import jax.numpy as jnp
from jax import lax
from jax.experimental import pallas as pl
from jax.experimental.pallas import tpu as pltpu
from jax.sharding import PartitionSpec as P

BF = jnp.bfloat16
F32 = jnp.float32
I32 = jnp.int32
NN = (((1,), (0,)), ((), ()))
NT = (((1,), (1,)), ((), ()))
TN = (((0,), (0,)), ((), ()))
VM = pl.BlockSpec(memory_space=pltpu.VMEM)
SM = pl.BlockSpec(memory_space=pltpu.SMEM)

N, T, K, E, HALF = 128, 64, 4, 32, 12
ROWS = 2 * HALF
ALL = E * ROWS
W = 256
LATER = 224


def dot(a, b, dims):
    return lax.dot_general(a, b, dims, preferred_element_type=F32)


def iota(shape, dim):
    return lax.broadcasted_iota(I32, shape, dim)


def one(mask):
    return jnp.where(mask, 1.0, 0.0).astype(BF)


def divided(x, by):
    return ((x.astype(F32) + 0.5) * (1.0 / by)).astype(I32)


def split(x):
    high = x.astype(BF)
    return high, (x - high.astype(F32)).astype(BF)


def slot_matrix(ids_row, token_major):
    lane = iota((N, N * K), 1)
    owner = (lane >> 2) if token_major else (lane & (N - 1))
    spread = one(owner == iota((N, N * K), 0))
    named = ids_row == iota((E, N * K), 0)
    marks = dot(one(named), spread, NT)
    first, second = iota((N, N), 0), iota((N, N), 1)
    earlier = one((first < second) & ((first >> 6) == (second >> 6)))
    place = dot(marks.astype(BF), earlier, NN) + (HALF * (iota((E, N), 1) >> 6)).astype(F32)
    code = jnp.where(named, dot(place.astype(BF), spread, NN), -1.0).astype(BF)
    row = iota((ALL, E), 0)
    expand = one(divided(row, ROWS) == iota((ALL, E), 1))
    wide = iota((ALL, N * K), 0)
    inner = (wide - ROWS * divided(wide, ROWS)).astype(F32)
    return one(dot(expand, code, NN) == inner), spread


def first_half(rows, width, start=0):
    row = iota((rows, width), 0) + start
    return (row - ROWS * divided(row, ROWS)) < HALF


def dispatch_kernel(ids_ref, hid_ref, grad_ref, out_ref):
    pick, spread = slot_matrix(ids_ref[...], True)
    tokens = dot(pick, spread, NT).astype(BF)
    step = 8
    for c in range(E // step):
        rows = slice(c * step * ROWS, (c + 1) * step * ROWS)
        to = slice(c * step, (c + 1) * step)
        own = dot(tokens[rows], grad_ref[...], NN).astype(BF)
        out_ref[to, 0:ROWS, :] = own.reshape(step, ROWS, own.shape[1])
        own = dot(pick[rows], hid_ref[...], NN).astype(BF)
        out_ref[to, ROWS : 2 * ROWS, :] = own.reshape(step, ROWS, own.shape[1])


def tables_kernel(*refs):
    held, down_ref, tab_ref, back_ref, ids_ref = refs[:8], refs[8], refs[9], refs[10], refs[11]
    for b in range(8):
        for m in range(2):
            tab_ref[m * W + b * E : m * W + (b + 1) * E, :] = held[b][m * E : (m + 1) * E, :]
    rows = jnp.concatenate([held[b][2 * E : 2 * E + 8, 0:N].astype(F32) for b in range(8)], axis=0)
    for j in range(K):
        for b in range(8):
            ids_ref[8 * j + b : 8 * j + b + 1, :] = rows[8 * b + j : 8 * b + j + 1, :]
    for m in range(2):
        back_ref[m * W : (m + 1) * W, :] = dot(
            tab_ref[m * W : (m + 1) * W, :], down_ref[...], NT
        ).astype(BF)


def expert_kernel(got_ref, down_ref, back_ref, base_ref, out_ref):
    step = 8
    size = step * ROWS
    for c in range(E // step):
        to = slice(c * step, (c + 1) * step)
        grad = got_ref[to, 0:ROWS, :].reshape(size, got_ref.shape[2])
        hid = got_ref[to, ROWS : 2 * ROWS, :].reshape(size, got_ref.shape[2])
        base = dot(grad, down_ref[...], NT)
        base_ref[c * size : (c + 1) * size, :] = base
        high, low = split(jnp.sum(hid.astype(F32) * base, axis=1, keepdims=True))
        both = dot(hid, back_ref[...], NT)
        proj = jnp.where(first_half(size, W), both[:, :W], both[:, W:])
        lane = iota((size, W), 1)
        tail = jnp.where(lane == LATER, high.astype(F32), low.astype(F32))
        tail = jnp.where(lane < LATER + 2, tail, 0.0)
        out_ref[c * size : (c + 1) * size, :] = jnp.where(lane < LATER, proj, tail).astype(BF)


def id_masks(ids_ref):
    spread = one(divided(iota((8, W), 1), E) == iota((8, W), 0))
    lane = iota((N, W), 1) & (E - 1)
    masks = []
    for j in range(K):
        wide = dot(ids_ref[8 * j : 8 * j + 8, :].astype(BF), spread, TN)
        masks.append(wide == lane.astype(F32))
    return masks, spread


def blocks_kernel(got_ref, row_ref, ids_ref, gate_ref, out_ref):
    pick, _ = slot_matrix(row_ref[...], False)
    slots = dot(pick, got_ref[...], TN)
    gates = [gate_ref[:, k : k + 1] for k in range(K)]
    parts = [slots[k * N : (k + 1) * N] for k in range(K)]
    lane = iota((N, W), 1)
    full = []
    for part in parts:
        dots = part[:, LATER : LATER + 1] + part[:, LATER + 1 : LATER + 2]
        full.append(jnp.where(lane < LATER, part, dots))
    mean = sum(gates[k] * full[k] for k in range(K))
    masks, spread = id_masks(ids_ref)
    rows = []
    for k in range(K):
        value = gates[k] * (full[k] - mean)
        high, low = split(value)
        for j in range(K):
            source = jnp.where(masks[j] & (lane < LATER), high.astype(F32), 0.0)
            if j < 2:
                extra = high if j == 0 else low
                source = jnp.where(lane == LATER, extra.astype(F32), source)
            rows.append(source.astype(BF))
    packed = dot(spread, jnp.concatenate(rows, axis=0), NT).astype(BF)
    for d in range(8):
        out_ref[d] = packed


def solve_kernel(at_ref, got_ref, row_ref, ids_ref, gate_ref, out_ref, coef_ref):
    at = at_ref[0]
    depth = iota((8, K * N), 0)
    found = jnp.zeros((8, K * N), F32)
    for back in range(7, -1, -1):
        where = jnp.minimum(at + back, 7)
        valid = (at + back <= 7).astype(F32)
        block = got_ref[where].astype(F32)
        fresh = []
        for k in range(K):
            part = block[:, k * K * N : (k + 1) * K * N]
            fixed = part[7:8, 0:N] + part[7:8, N : 2 * N]
            terms = jnp.sum(part * found, axis=0, keepdims=True)
            total = fixed
            for j in range(K):
                total = total + terms[:, j * N : (j + 1) * N]
            fresh.append(total * valid)
        fresh = jnp.concatenate(fresh, axis=1)
        if back:
            found = jnp.where(depth == 0, fresh, pltpu.roll(found, 1, 0))
        else:
            found = jnp.where(depth == 7, fresh, found)
    masks, spread = id_masks(ids_ref)
    high, low = split(found)
    coef = jnp.zeros((N, W), F32)
    for j in range(K):
        cut = slice(j * N, (j + 1) * N)
        wide = dot(high[:, cut], spread, TN) + dot(low[:, cut], spread, TN)
        coef = jnp.where(masks[j], wide, coef)
    coef_ref[...] = coef.astype(BF)
    lane = iota((N, W), 1)
    rows = []
    for k in range(K):
        gate = gate_ref[:, k : k + 1]
        up, rest = split(gate)
        tail = jnp.where(lane == LATER, up.astype(F32), rest.astype(F32))
        tail = jnp.where(lane < LATER + 2, tail, 0.0)
        rows.append(jnp.where(lane < LATER, gate * coef, tail).astype(BF))
    pick, _ = slot_matrix(row_ref[...], False)
    out_ref[...] = dot(pick, jnp.concatenate(rows, axis=0), NN).astype(BF)


def passed_kernel(coef_ref, tab_ref, grad_ref, acts_ref, pass_ref, part_ref):
    for m in range(2):
        rows = slice(m * T, (m + 1) * T)
        moved = dot(coef_ref[rows, :], tab_ref[m * W : (m + 1) * W, :], NN)
        pass_ref[rows, :] = (grad_ref[rows, :].astype(F32) + moved).astype(BF)
    own = coef_ref[:, LATER:W]
    width = acts_ref.shape[1]
    router = (dot(acts_ref[...], own, TN) / T).astype(BF)
    each = width // E
    row, col = iota((ALL, width), 0), iota((ALL, width), 1)
    peer = divided(row, ROWS)
    inner = row - ROWS * peer
    source = peer * each + inner
    first = dot(one(source == col), router, NN)
    second = dot(one((source + ROWS == col) & (inner + ROWS < each)), router, NN)
    part_ref[:, 0:E] = first.astype(BF)
    part_ref[:, E : 2 * E] = second.astype(BF)


def answer_kernel(got_ref, base_ref, back_ref, part_ref, out_ref):
    step = 8
    size = step * ROWS
    width = base_ref.shape[1]
    for c in range(E // step):
        rows = slice(c * size, (c + 1) * size)
        got = got_ref[rows, :].astype(F32)
        gate = got[:, LATER : LATER + 1] + got[:, LATER + 1 : LATER + 2]
        lane = iota((size, W), 1)
        coef = jnp.where(lane < LATER, got, 0.0)
        half = first_half(size, W)
        left = jnp.where(half, coef, 0.0).astype(BF)
        right = jnp.where(half, 0.0, coef).astype(BF)
        value = gate * base_ref[rows, :]
        value = value + dot(left, back_ref[0:W, :], NN) + dot(right, back_ref[W : 2 * W, :], NN)
        out_ref[rows, 0:width] = value.astype(BF)
        out_ref[rows, width : width + 2 * E] = part_ref[rows, :]
        out_ref[rows, width + 2 * E :] = jnp.zeros((size, out_ref.shape[1] - width - 2 * E), BF)


def combine_kernel(got_ref, row_ref, out_ref, router_ref):
    pick, _ = slot_matrix(row_ref[...], True)
    width = out_ref.shape[1]
    step = 128
    for c in range(N * K // step):
        cut = slice(c * step, (c + 1) * step)
        out_ref[cut, :] = dot(pick[:, cut], got_ref[:, 0:width], TN).astype(BF)
    parts = got_ref[:, width : width + 2 * E].astype(F32).reshape(E, ROWS, 2 * E)
    total = jnp.sum(parts, axis=0)
    each = width // E
    router_ref[0:ROWS, :] = total[:, 0:E]
    router_ref[ROWS:each, :] = total[0 : each - ROWS, E : 2 * E]


def call(body, shapes, args, smem=0):
    return pl.pallas_call(
        body,
        out_shape=[jax.ShapeDtypeStruct(s, d) for s, d in shapes],
        in_specs=[SM] * smem + [VM] * (len(args) - smem),
        out_specs=[VM] * len(shapes),
        compiler_params=pltpu.CompilerParams(vmem_limit_bytes=60000 * 1024),
    )(*args)


def exchange(x, axis):
    return lax.all_to_all(x, axis, split_axis=0, concat_axis=0, tiled=True)


def on_device(acts, hidden, ids, version, router, down, grad_top):
    pipe = lax.axis_size("pipe")
    section = lax.axis_index("pipe")
    width = acts.shape[-1]
    inner = hidden.shape[-1]
    inputs = acts[0]
    routes = ids[0]
    mats = down[0, 0]
    grads = grad_top.reshape(N, width)
    row_nk = routes.reshape(1, N * K)
    row_kn = routes.reshape(N, K).T.reshape(1, N * K)

    (sent,) = call(
        dispatch_kernel,
        [((E, 2 * ROWS, width), BF)],
        (row_nk, hidden[0].reshape(N * K, inner), grads),
    )
    arrived = exchange(sent, "expert")

    picked_version = version[0][:, None, None] == 1
    tables = jnp.where(picked_version, router[0, 1][None], router[0, 0][None])
    flipped = tables.transpose(0, 2, 1).reshape(2 * E, width)
    id_rows = jnp.pad(row_kn.reshape(K, N).astype(BF), ((0, 8 - K), (0, width - N)))
    own = jnp.concatenate([flipped, id_rows], axis=0)
    held = [
        lax.ppermute(own, "pipe", [(i, i - by) for i in range(by, pipe)]) for by in range(1, pipe)
    ] + [own]
    table_rows, back, id_all = call(
        tables_kernel,
        [((2 * W, width), BF), ((2 * W, inner), BF), ((K * 8, N), F32)],
        (*held, mats),
    )

    logits = jnp.einsum("mtd,mde->mte", inputs, tables, preferred_element_type=F32)
    labels = jnp.arange(E, dtype=I32)
    picked = routes[:, :, :, None] == labels
    chosen = jnp.sum(jnp.where(picked, logits[:, :, None, :], 0.0), axis=3)
    scores = jnp.exp(chosen)
    gating = (scores / jnp.sum(scores, axis=2, keepdims=True)).reshape(N, K)

    base, proj = call(
        expert_kernel, [((ALL, inner), F32), ((ALL, W), BF)], (arrived, mats, back)
    )
    returned = exchange(proj.reshape(E, ROWS, W), "expert").reshape(ALL, W)
    (blocks,) = call(
        blocks_kernel, [((8, 8, K * K * N), BF)], (returned, row_kn, id_all, gating)
    )
    gathered = exchange(blocks, "pipe")
    coef_sent, coef = call(
        solve_kernel,
        [((ALL, W), BF), ((N, W), BF)],
        (section.reshape(1), gathered, row_kn, id_all, gating),
        smem=1,
    )
    coef_got = exchange(coef_sent.reshape(E, ROWS, W), "expert").reshape(ALL, W)
    passed, parts = call(
        passed_kernel,
        [((N, width), BF), ((ALL, 2 * E), BF)],
        (coef, table_rows, grads, inputs.reshape(N, width)),
    )
    wide = 128 * pl.cdiv(inner + 2 * E, 128)
    (answer,) = call(answer_kernel, [((ALL, wide), BF)], (coef_got, base, back, parts))
    answered = exchange(answer.reshape(E, ROWS, wide), "expert").reshape(ALL, wide)
    hidden_grads, grad_router = call(
        combine_kernel, [((N * K, inner), BF), ((width // E, E), F32)], (answered, row_nk)
    )
    return (
        passed.reshape(1, 2, T, width),
        hidden_grads.reshape(1, 2, T, K, inner),
        grad_router[None],
    )


def solution(mesh):
    placed = (
        P("pipe", None, "expert", None),
        P("pipe", None, "expert", None, None),
        P("pipe", None, "expert", None),
        P("pipe", None),
        P("pipe", None, None, None),
        P("pipe", "expert", None, None),
        P(None, "expert", None),
    )
    return jax.shard_map(
        on_device,
        mesh=mesh,
        in_specs=placed,
        out_specs=(
            P("pipe", None, "expert", None),
            P("pipe", None, "expert", None, None),
            P("pipe", "expert", None),
        ),
        check_vma=False,
    )
```

```python
import functools

import jax
import jax.numpy as jnp
from jax import lax
from jax.experimental import pallas as pl
from jax.experimental.pallas import tpu as pltpu
from jax.sharding import PartitionSpec as P

BF = jnp.bfloat16
F32 = jnp.float32
I32 = jnp.int32
NN = (((1,), (0,)), ((), ()))
NT = (((1,), (1,)), ((), ()))
TN = (((0,), (0,)), ((), ()))
VM = pl.BlockSpec(memory_space=pltpu.VMEM)
SM = pl.BlockSpec(memory_space=pltpu.SMEM)

N, T, K, E, HALF = 128, 64, 4, 32, 12
ROWS = 2 * HALF
ALL = E * ROWS
W = 256
MIBS = (20, 20, 32, 12, 12, 20, 24, 20)
LATER = 224


def dot(a, b, dims):
    return lax.dot_general(a, b, dims, preferred_element_type=F32)


def iota(shape, dim):
    return lax.broadcasted_iota(I32, shape, dim)


def one(mask):
    return jnp.where(mask, 1.0, 0.0).astype(BF)


def divided(x, by):
    return ((x.astype(F32) + 0.5) * (1.0 / by)).astype(I32)


def split(x):
    high = x.astype(BF)
    return high, (x - high.astype(F32)).astype(BF)


def slot_codes(ids_ref):
    named = []
    for k in range(K):
        row = jnp.concatenate([ids_ref[0, k : k + 1, :], ids_ref[1, k : k + 1, :]], axis=1)
        named.append(row == iota((E, N), 0))
    marks = sum(jnp.where(hit, 1.0, 0.0) for hit in named).astype(BF)
    first, second = iota((N, N), 0), iota((N, N), 1)
    earlier = one((first < second) & ((first >> 6) == (second >> 6)))
    place = dot(marks, earlier, NN) + (HALF * (iota((E, N), 1) >> 6)).astype(F32)
    return [jnp.where(hit, place, -1.0) for hit in named]


def token_major(codes):
    lane = iota((N, N * K), 1)
    spread = one((lane >> 2) == iota((N, N * K), 0))
    which = iota((E, N * K), 1) & (K - 1)
    out = jnp.zeros((E, N * K), F32)
    for k in range(K):
        out = jnp.where(which == k, dot(codes[k].astype(BF), spread, NN), out)
    return out


def rows_by_slots(code):
    expand = one(divided(iota((ALL, E), 0), ROWS) == iota((ALL, E), 1))
    row = iota((ALL, code.shape[1]), 0)
    inner = (row - ROWS * divided(row, ROWS)).astype(F32)
    return one(dot(expand, code.astype(BF), NN) == inner)


def slots_by_rows(code):
    expand = one(divided(iota((E, ALL), 1), ROWS) == iota((E, ALL), 0))
    row = iota((code.shape[1], ALL), 1)
    inner = (row - ROWS * divided(row, ROWS)).astype(F32)
    return one(dot(code.astype(BF), expand, TN) == inner)


def first_half(rows, width, start=0):
    row = iota((rows, width), 0) + start
    return (row - ROWS * divided(row, ROWS)) < HALF


def dispatch_kernel(ids_ref, hid_ref, grad_ref, out_ref):
    codes = slot_codes(ids_ref)
    pick = rows_by_slots(token_major(codes))
    tokens = rows_by_slots(functools.reduce(jnp.maximum, codes))
    width = grad_ref.shape[1]
    for start in range(0, width, 256):
        cols = slice(start, min(start + 256, width))
        size = cols.stop - start
        grad = dot(tokens, grad_ref[:, cols], NN)
        hid = dot(pick, hid_ref[:, :, cols].reshape(N * K, size), NN)
        for lanes in range(0, size, 128):
            at = 2 * ROWS * ((start + lanes) // 128)
            cut = min(lanes + 128, size)
            left = grad[:, lanes:cut].reshape(E, ROWS, cut - lanes)
            right = hid[:, lanes:cut].reshape(E, ROWS, cut - lanes)
            if cut - lanes == 128:
                out_ref[:, at : at + ROWS, :] = left.astype(BF)
                out_ref[:, at + ROWS : at + 2 * ROWS, :] = right.astype(BF)
            else:
                tail = [
                    left[:, 0:16],
                    jnp.concatenate([left[:, 16:24], right[:, 0:8]], axis=1),
                    right[:, 8:24],
                    jnp.zeros((E, 16, 32), F32),
                ]
                out_ref[:, at : at + 16, :] = jnp.concatenate(tail, axis=2).astype(BF)


def tables_kernel(*refs):
    held, down_ref, tab_ref, back_ref, ids_ref = refs[:8], refs[8], refs[9], refs[10], refs[11]
    for b in range(8):
        for m in range(2):
            tab_ref[m * W + b * E : m * W + (b + 1) * E, :] = held[b][m * E : (m + 1) * E, :]
    rows = jnp.concatenate([held[b][2 * E : 2 * E + 8, 0:N].astype(F32) for b in range(8)], axis=0)
    for j in range(K):
        for b in range(8):
            ids_ref[8 * j + b : 8 * j + b + 1, :] = rows[8 * b + j : 8 * b + j + 1, :]
    for m in range(2):
        back_ref[m * W : (m + 1) * W, :] = dot(
            tab_ref[m * W : (m + 1) * W, :], down_ref[...], NT
        ).astype(BF)


def expert_kernel(got_ref, down_ref, back_ref, base_ref, out_ref, grad_ref, hid_ref):
    inner = down_ref.shape[0]
    full = 128 * (inner // 128)
    for lanes in range(0, full, 128):
        at = 2 * ROWS * (lanes // 128)
        cols = slice(lanes, lanes + 128)
        grad_ref[:, cols] = got_ref[:, at : at + ROWS, :].reshape(ALL, 128)
        hid_ref[:, cols] = got_ref[:, at + ROWS : at + 2 * ROWS, :].reshape(ALL, 128)
    at = 2 * ROWS * (full // 128)
    tail = got_ref[:, at : at + 16, :].astype(F32)
    middle = tail[:, :, 32:64]
    grad = jnp.concatenate([tail[:, :, 0:32], middle[:, 0:8]], axis=1)
    hid = jnp.concatenate([middle[:, 8:16], tail[:, :, 64:96]], axis=1)
    grad_ref[:, full:inner] = grad.astype(BF).reshape(ALL, 32)
    hid_ref[:, full:inner] = hid.astype(BF).reshape(ALL, 32)
    total = jnp.zeros((ALL, 1), F32)
    for start in range(0, inner, 256):
        cols = slice(start, min(start + 256, inner))
        base = dot(grad_ref[...], down_ref[cols, :], NT)
        base_ref[:, cols] = base
        total = total + jnp.sum(hid_ref[:, cols].astype(F32) * base, axis=1, keepdims=True)
    high, low = split(total)
    left = dot(hid_ref[...], back_ref[0:W, :], NT)
    right = dot(hid_ref[...], back_ref[W : 2 * W, :], NT)
    proj = jnp.where(first_half(ALL, W), left, right)
    lane = iota((ALL, W), 1)
    tail = jnp.where(lane == LATER, high.astype(F32), low.astype(F32))
    tail = jnp.where(lane < LATER + 2, tail, 0.0)
    out_ref[...] = jnp.where(lane < LATER, proj, tail).astype(BF)


def id_masks(ids_ref):
    spread = one(divided(iota((8, W), 1), E) == iota((8, W), 0))
    lane = iota((N, W), 1) & (E - 1)
    masks = []
    for j in range(K):
        wide = dot(ids_ref[8 * j : 8 * j + 8, :].astype(BF), spread, TN)
        masks.append(wide == lane.astype(F32))
    return masks, spread


def blocks_kernel(got_ref, row_ref, ids_ref, gate_ref, out_ref):
    pick = slots_by_rows(jnp.concatenate(slot_codes(row_ref), axis=1))
    slots = dot(pick, got_ref[...], NN)
    gates = [gate_ref[:, k : k + 1] for k in range(K)]
    parts = [slots[k * N : (k + 1) * N] for k in range(K)]
    lane = iota((N, W), 1)
    full = []
    for part in parts:
        dots = part[:, LATER : LATER + 1] + part[:, LATER + 1 : LATER + 2]
        full.append(jnp.where(lane < LATER, part, dots))
    mean = sum(gates[k] * full[k] for k in range(K))
    masks, spread = id_masks(ids_ref)
    rows = []
    for k in range(K):
        value = gates[k] * (full[k] - mean)
        high, low = split(value)
        for j in range(K):
            source = jnp.where(masks[j] & (lane < LATER), high.astype(F32), 0.0)
            if j < 2:
                extra = high if j == 0 else low
                source = jnp.where(lane == LATER, extra.astype(F32), source)
            rows.append(source.astype(BF))
    packed = dot(spread, jnp.concatenate(rows, axis=0), NT).astype(BF)
    for d in range(8):
        out_ref[d] = packed


def solve_kernel(at_ref, got_ref, row_ref, ids_ref, gate_ref, out_ref, coef_ref):
    at = at_ref[0]
    depth = iota((8, K * N), 0)
    found = jnp.zeros((8, K * N), F32)
    for back in range(7, -1, -1):
        where = jnp.minimum(at + back, 7)
        valid = (at + back <= 7).astype(F32)
        block = got_ref[where].astype(F32)
        fresh = []
        for k in range(K):
            part = block[:, k * K * N : (k + 1) * K * N]
            fixed = part[7:8, 0:N] + part[7:8, N : 2 * N]
            terms = jnp.sum(part * found, axis=0, keepdims=True)
            total = fixed
            for j in range(K):
                total = total + terms[:, j * N : (j + 1) * N]
            fresh.append(total * valid)
        fresh = jnp.concatenate(fresh, axis=1)
        if back:
            found = jnp.where(depth == 0, fresh, pltpu.roll(found, 1, 0))
        else:
            found = jnp.where(depth == 7, fresh, found)
    masks, spread = id_masks(ids_ref)
    high, low = split(found)
    coef = jnp.zeros((N, W), F32)
    for j in range(K):
        cut = slice(j * N, (j + 1) * N)
        wide = dot(high[:, cut], spread, TN) + dot(low[:, cut], spread, TN)
        coef = jnp.where(masks[j], wide, coef)
    coef_ref[...] = coef.astype(BF)
    lane = iota((N, W), 1)
    rows = []
    for k in range(K):
        gate = gate_ref[:, k : k + 1]
        up, rest = split(gate)
        tail = jnp.where(lane == LATER, up.astype(F32), rest.astype(F32))
        tail = jnp.where(lane < LATER + 2, tail, 0.0)
        rows.append(jnp.where(lane < LATER, gate * coef, tail).astype(BF))
    pick = rows_by_slots(jnp.concatenate(slot_codes(row_ref), axis=1))
    out_ref[...] = dot(pick, jnp.concatenate(rows, axis=0), NN).astype(BF)


def passed_kernel(coef_ref, tab_ref, grad_ref, acts_ref, pass_ref, part_ref):
    for m in range(2):
        rows = slice(m * T, (m + 1) * T)
        moved = dot(coef_ref[rows, :], tab_ref[m * W : (m + 1) * W, :], NN)
        pass_ref[rows, :] = (grad_ref[rows, :].astype(F32) + moved).astype(BF)
    own = coef_ref[:, LATER:W]
    width = acts_ref.shape[1]
    router = (dot(acts_ref[...], own, TN) / T).astype(BF)
    each = width // E
    row, col = iota((ALL, width), 0), iota((ALL, width), 1)
    peer = divided(row, ROWS)
    inner = row - ROWS * peer
    source = peer * each + inner
    first = dot(one(source == col), router, NN)
    second = dot(one((source + ROWS == col) & (inner + ROWS < each)), router, NN)
    part_ref[:, 0:E] = first.astype(BF)
    part_ref[:, E : 2 * E] = second.astype(BF)


def answer_kernel(got_ref, base_ref, back_ref, part_ref, out_ref):
    width = base_ref.shape[1]
    got = got_ref[...].astype(F32)
    gate = got[:, LATER : LATER + 1] + got[:, LATER + 1 : LATER + 2]
    coef = jnp.where(iota((ALL, W), 1) < LATER, got, 0.0)
    half = first_half(ALL, W)
    left = jnp.where(half, coef, 0.0).astype(BF)
    right = jnp.where(half, 0.0, coef).astype(BF)
    for start in range(0, width, 256):
        cols = slice(start, min(start + 256, width))
        moved = dot(left, back_ref[0:W, cols], NN) + dot(right, back_ref[W : 2 * W, cols], NN)
        out_ref[:, cols] = (gate * base_ref[:, cols] + moved).astype(BF)
    out_ref[:, width : width + 2 * E] = part_ref[...]
    out_ref[:, width + 2 * E :] = jnp.zeros((ALL, out_ref.shape[1] - width - 2 * E), BF)


def combine_kernel(got_ref, ids_ref, out_ref, router_ref):
    pick = slots_by_rows(token_major(slot_codes(ids_ref)))
    width = out_ref.shape[2]
    for start in range(0, width, 256):
        cols = slice(start, min(start + 256, width))
        own = dot(pick, got_ref[:, cols], NN).astype(BF)
        out_ref[:, :, cols] = own.reshape(N, K, cols.stop - start)
    parts = got_ref[:, width : width + 2 * E].astype(F32).reshape(E, ROWS, 2 * E)
    total = jnp.sum(parts, axis=0)
    each = width // E
    turn = iota((E, 2 * E), 1) - iota((E, 2 * E), 0)
    flipped = [jnp.zeros((E, ROWS), F32)] * 2
    for _ in range(3):
        piece = total.astype(BF)
        total = total - piece.astype(F32)
        flipped = [flipped[q] + dot(one(turn == q * E), piece, NT) for q in range(2)]
    router_ref[:, 0:ROWS] = flipped[0]
    router_ref[:, ROWS:each] = flipped[1][:, 0 : each - ROWS]


def call(body, shapes, args, mib, smem=0, scratch=()):
    return pl.pallas_call(
        body,
        out_shape=[jax.ShapeDtypeStruct(s, d) for s, d in shapes],
        in_specs=[SM] * smem + [VM] * (len(args) - smem),
        out_specs=[VM] * len(shapes),
        scratch_shapes=list(scratch),
        compiler_params=pltpu.CompilerParams(vmem_limit_bytes=mib << 20),
    )(*args)


def exchange(x, axis):
    return lax.all_to_all(x, axis, split_axis=0, concat_axis=0, tiled=True)


def on_device(acts, hidden, ids, version, router, down, grad_top):
    pipe = lax.axis_size("pipe")
    section = lax.axis_index("pipe")
    width = acts.shape[-1]
    inner = hidden.shape[-1]
    inputs = acts[0]
    routes = ids[0]
    mats = down[0, 0]
    grads = grad_top.reshape(N, width)
    turned = routes.transpose(0, 2, 1)
    tall = 2 * ROWS * (inner // 128) + 16

    (sent,) = call(
        dispatch_kernel,
        [((E, tall, 128), BF)],
        (turned, hidden[0].reshape(N, K, inner), grads),
        MIBS[0],
    )
    arrived = exchange(sent, "expert")

    picked_version = version[0][:, None, None] == 1
    tables = jnp.where(picked_version, router[0, 1][None], router[0, 0][None])
    flipped = tables.transpose(0, 2, 1).reshape(2 * E, width)
    id_rows = jnp.pad(
        turned.transpose(1, 0, 2).reshape(K, N).astype(BF), ((0, 8 - K), (0, width - N))
    )
    own = jnp.concatenate([flipped, id_rows], axis=0)
    held = [
        lax.ppermute(own, "pipe", [(i, i - by) for i in range(by, pipe)]) for by in range(1, pipe)
    ] + [own]
    table_rows, back, id_all = call(
        tables_kernel,
        [((2 * W, width), BF), ((2 * W, inner), BF), ((K * 8, N), F32)],
        (*held, mats),
        MIBS[1],
    )

    logits = jnp.einsum("mtd,mde->mte", inputs, tables, preferred_element_type=F32)
    labels = jnp.arange(E, dtype=I32)
    picked = routes[:, :, :, None] == labels
    chosen = jnp.sum(jnp.where(picked, logits[:, :, None, :], 0.0), axis=3)
    scores = jnp.exp(chosen)
    gating = (scores / jnp.sum(scores, axis=2, keepdims=True)).reshape(N, K)

    base, proj = call(
        expert_kernel,
        [((ALL, inner), F32), ((ALL, W), BF)],
        (arrived, mats, back),
        MIBS[2],
        scratch=[pltpu.VMEM((ALL, inner), BF)] * 2,
    )
    proj, gating = lax.optimization_barrier((proj, gating))
    returned = exchange(proj.reshape(E, ROWS, W), "expert").reshape(ALL, W)
    (blocks,) = call(
        blocks_kernel,
        [((8, 8, K * K * N), BF)],
        (returned, turned, id_all, gating),
        MIBS[3],
    )
    gathered = exchange(blocks, "pipe")
    coef_sent, coef = call(
        solve_kernel,
        [((ALL, W), BF), ((N, W), BF)],
        (section.reshape(1), gathered, turned, id_all, gating),
        MIBS[4],
        smem=1,
    )
    coef_got = exchange(coef_sent.reshape(E, ROWS, W), "expert").reshape(ALL, W)
    passed, parts = call(
        passed_kernel,
        [((N, width), BF), ((ALL, 2 * E), BF)],
        (coef, table_rows, grads, inputs.reshape(N, width)),
        MIBS[5],
    )
    wide = 128 * pl.cdiv(inner + 2 * E, 128)
    (answer,) = call(
        answer_kernel, [((ALL, wide), BF)], (coef_got, base, back, parts), MIBS[6]
    )
    answered = exchange(answer.reshape(E, ROWS, wide), "expert").reshape(ALL, wide)
    hidden_grads, grad_router = call(
        combine_kernel, [((N, K, inner), BF), ((E, width // E), F32)], (answered, turned), MIBS[7]
    )
    return (
        passed.reshape(1, 2, T, width),
        hidden_grads.reshape(1, 2, T, K, inner),
        grad_router.T[None],
    )


def solution(mesh):
    placed = (
        P("pipe", None, "expert", None),
        P("pipe", None, "expert", None, None),
        P("pipe", None, "expert", None),
        P("pipe", None),
        P("pipe", None, None, None),
        P("pipe", "expert", None, None),
        P(None, "expert", None),
    )
    return jax.shard_map(
        on_device,
        mesh=mesh,
        in_specs=placed,
        out_specs=(
            P("pipe", None, "expert", None),
            P("pipe", None, "expert", None, None),
            P("pipe", "expert", None),
        ),
        check_vma=False,
    )
```

```python
import functools

import jax
import jax.numpy as jnp
from jax import lax
from jax.experimental import pallas as pl
from jax.experimental.pallas import tpu as pltpu
from jax.sharding import PartitionSpec as P

BF = jnp.bfloat16
F32 = jnp.float32
I32 = jnp.int32
NN = (((1,), (0,)), ((), ()))
NT = (((1,), (1,)), ((), ()))
TN = (((0,), (0,)), ((), ()))
VM = pl.BlockSpec(memory_space=pltpu.VMEM)
SM = pl.BlockSpec(memory_space=pltpu.SMEM)

N, T, K, E, HALF = 128, 64, 4, 32, 12
ROWS = 2 * HALF
ALL = E * ROWS
W = 256
MIBS = (58, 20, 58, 12, 12, 20, 62, 58)
LATER = 224


def dot(a, b, dims):
    return lax.dot_general(a, b, dims, preferred_element_type=F32)


def iota(shape, dim):
    return lax.broadcasted_iota(I32, shape, dim)


def one(mask):
    return jnp.where(mask, 1.0, 0.0).astype(BF)


def divided(x, by):
    return ((x.astype(F32) + 0.5) * (1.0 / by)).astype(I32)


def split(x):
    high = x.astype(BF)
    return high, (x - high.astype(F32)).astype(BF)


def slot_codes(ids_ref):
    named = []
    for k in range(K):
        row = jnp.concatenate([ids_ref[0, k : k + 1, :], ids_ref[1, k : k + 1, :]], axis=1)
        named.append(row == iota((E, N), 0))
    marks = sum(jnp.where(hit, 1.0, 0.0) for hit in named).astype(BF)
    first, second = iota((N, N), 0), iota((N, N), 1)
    earlier = one((first < second) & ((first >> 6) == (second >> 6)))
    place = dot(marks, earlier, NN) + (HALF * (iota((E, N), 1) >> 6)).astype(F32)
    return [jnp.where(hit, place, -1.0) for hit in named]


def token_major(codes):
    lane = iota((N, N * K), 1)
    spread = one((lane >> 2) == iota((N, N * K), 0))
    which = iota((E, N * K), 1) & (K - 1)
    out = jnp.zeros((E, N * K), F32)
    for k in range(K):
        out = jnp.where(which == k, dot(codes[k].astype(BF), spread, NN), out)
    return out


def rows_by_slots(code):
    expand = one(divided(iota((ALL, E), 0), ROWS) == iota((ALL, E), 1))
    row = iota((ALL, code.shape[1]), 0)
    inner = (row - ROWS * divided(row, ROWS)).astype(F32)
    return one(dot(expand, code.astype(BF), NN) == inner)


def slots_by_rows(code):
    expand = one(divided(iota((E, ALL), 1), ROWS) == iota((E, ALL), 0))
    row = iota((code.shape[1], ALL), 1)
    inner = (row - ROWS * divided(row, ROWS)).astype(F32)
    return one(dot(code.astype(BF), expand, TN) == inner)


def first_half(rows, width, start=0):
    row = iota((rows, width), 0) + start
    return (row - ROWS * divided(row, ROWS)) < HALF


def dispatch_kernel(ids_ref, hid_ref, grad_ref, out_ref, pick_ref, token_ref):
    step = pl.program_id(0)

    @pl.when(step == 0)
    def _():
        codes = slot_codes(ids_ref)
        pick_ref[...] = rows_by_slots(token_major(codes))
        token_ref[...] = rows_by_slots(functools.reduce(jnp.maximum, codes))

    size = grad_ref.shape[1]
    grad = dot(token_ref[...], grad_ref[...], NN).reshape(E, ROWS, size)
    hid = dot(pick_ref[...], hid_ref[...].reshape(N * K, size), NN).reshape(E, ROWS, size)
    out_ref[:, 0:ROWS, :] = grad[:, :, 0:128].astype(BF)
    out_ref[:, ROWS : 2 * ROWS, :] = hid[:, :, 0:128].astype(BF)

    @pl.when(step < pl.num_programs(0) - 1)
    def _():
        out_ref[:, 2 * ROWS : 3 * ROWS, :] = grad[:, :, 128:256].astype(BF)
        out_ref[:, 3 * ROWS : 4 * ROWS, :] = hid[:, :, 128:256].astype(BF)

    @pl.when(step == pl.num_programs(0) - 1)
    def _():
        left, right = grad[:, :, 128:160], hid[:, :, 128:160]
        tail = [
            left[:, 0:16],
            jnp.concatenate([left[:, 16:24], right[:, 0:8]], axis=1),
            right[:, 8:24],
            jnp.zeros((E, 16, 32), F32),
        ]
        out_ref[:, 2 * ROWS : 2 * ROWS + 16, :] = jnp.concatenate(tail, axis=2).astype(BF)


def tables_kernel(*refs):
    held, down_ref, tab_ref, back_ref, ids_ref = refs[:8], refs[8], refs[9], refs[10], refs[11]
    for b in range(8):
        for m in range(2):
            tab_ref[m * W + b * E : m * W + (b + 1) * E, :] = held[b][m * E : (m + 1) * E, :]
    rows = jnp.concatenate([held[b][2 * E : 2 * E + 8, 0:N].astype(F32) for b in range(8)], axis=0)
    for j in range(K):
        for b in range(8):
            ids_ref[8 * j + b : 8 * j + b + 1, :] = rows[8 * b + j : 8 * b + j + 1, :]
    for m in range(2):
        back_ref[m * W : (m + 1) * W, :] = dot(
            tab_ref[m * W : (m + 1) * W, :], down_ref[...], NT
        ).astype(BF)


def expert_kernel(got_ref, down_ref, back_ref, base_ref, out_ref, grad_ref, hid_ref, sum_ref):
    step = pl.program_id(0)
    inner = grad_ref.shape[1]
    full = 128 * (inner // 128)

    @pl.when(step == 0)
    def _():
        for lanes in range(0, full, 128):
            at = 2 * ROWS * (lanes // 128)
            cols = slice(lanes, lanes + 128)
            grad_ref[:, cols] = got_ref[:, at : at + ROWS, :].reshape(ALL, 128)
            hid_ref[:, cols] = got_ref[:, at + ROWS : at + 2 * ROWS, :].reshape(ALL, 128)
        at = 2 * ROWS * (full // 128)
        tail = got_ref[:, at : at + 16, :].astype(F32)
        middle = tail[:, :, 32:64]
        grad = jnp.concatenate([tail[:, :, 0:32], middle[:, 0:8]], axis=1)
        hid = jnp.concatenate([middle[:, 8:16], tail[:, :, 64:96]], axis=1)
        grad_ref[:, full:inner] = grad.astype(BF).reshape(ALL, 32)
        hid_ref[:, full:] = jnp.zeros((ALL, hid_ref.shape[1] - full), BF)
        hid_ref[:, full:inner] = hid.astype(BF).reshape(ALL, 32)
        sum_ref[...] = jnp.zeros((ALL, 1), F32)

    base = dot(grad_ref[...], down_ref[...], NT)
    base = jnp.where(iota((ALL, 256), 1) < inner - 256 * step, base, 0.0)
    base_ref[...] = base.astype(BF)
    hid = hid_ref[:, pl.ds(pl.multiple_of(256 * step, 256), 256)].astype(F32)
    sum_ref[...] += jnp.sum(hid * base, axis=1, keepdims=True)

    @pl.when(step == 1)
    def _():
        left = dot(hid_ref[:, 0:inner], back_ref[0:W, :], NT)
        right = dot(hid_ref[:, 0:inner], back_ref[W : 2 * W, :], NT)
        out_ref[...] = jnp.where(first_half(ALL, W), left, right).astype(BF)

    @pl.when(step == pl.num_programs(0) - 1)
    def _():
        high, low = split(sum_ref[...])
        lane = iota((ALL, 128), 1) + 128
        tail = jnp.where(lane == LATER, high.astype(F32), low.astype(F32))
        tail = jnp.where(lane < LATER + 2, tail, 0.0)
        proj = out_ref[:, 128:256].astype(F32)
        out_ref[:, 128:256] = jnp.where(lane < LATER, proj, tail).astype(BF)


def id_masks(ids_ref):
    spread = one(divided(iota((8, W), 1), E) == iota((8, W), 0))
    lane = iota((N, W), 1) & (E - 1)
    masks = []
    for j in range(K):
        wide = dot(ids_ref[8 * j : 8 * j + 8, :].astype(BF), spread, TN)
        masks.append(wide == lane.astype(F32))
    return masks, spread


def blocks_kernel(got_ref, row_ref, ids_ref, gate_ref, out_ref):
    pick = slots_by_rows(jnp.concatenate(slot_codes(row_ref), axis=1))
    slots = dot(pick, got_ref[...], NN)
    gates = [gate_ref[:, k : k + 1] for k in range(K)]
    parts = [slots[k * N : (k + 1) * N] for k in range(K)]
    lane = iota((N, W), 1)
    full = []
    for part in parts:
        dots = part[:, LATER : LATER + 1] + part[:, LATER + 1 : LATER + 2]
        full.append(jnp.where(lane < LATER, part, dots))
    mean = sum(gates[k] * full[k] for k in range(K))
    masks, spread = id_masks(ids_ref)
    rows = []
    for k in range(K):
        value = gates[k] * (full[k] - mean)
        high, low = split(value)
        for j in range(K):
            source = jnp.where(masks[j] & (lane < LATER), high.astype(F32), 0.0)
            if j < 2:
                extra = high if j == 0 else low
                source = jnp.where(lane == LATER, extra.astype(F32), source)
            rows.append(source.astype(BF))
    packed = dot(spread, jnp.concatenate(rows, axis=0), NT).astype(BF)
    for d in range(8):
        out_ref[d] = packed


def solve_kernel(at_ref, got_ref, row_ref, ids_ref, gate_ref, out_ref, coef_ref):
    at = at_ref[0]
    depth = iota((8, K * N), 0)
    found = jnp.zeros((8, K * N), F32)
    for back in range(7, -1, -1):
        where = jnp.minimum(at + back, 7)
        valid = (at + back <= 7).astype(F32)
        block = got_ref[where].astype(F32)
        fresh = []
        for k in range(K):
            part = block[:, k * K * N : (k + 1) * K * N]
            fixed = part[7:8, 0:N] + part[7:8, N : 2 * N]
            terms = jnp.sum(part * found, axis=0, keepdims=True)
            total = fixed
            for j in range(K):
                total = total + terms[:, j * N : (j + 1) * N]
            fresh.append(total * valid)
        fresh = jnp.concatenate(fresh, axis=1)
        if back:
            found = jnp.where(depth == 0, fresh, pltpu.roll(found, 1, 0))
        else:
            found = jnp.where(depth == 7, fresh, found)
    masks, spread = id_masks(ids_ref)
    high, low = split(found)
    coef = jnp.zeros((N, W), F32)
    for j in range(K):
        cut = slice(j * N, (j + 1) * N)
        wide = dot(high[:, cut], spread, TN) + dot(low[:, cut], spread, TN)
        coef = jnp.where(masks[j], wide, coef)
    coef_ref[...] = coef.astype(BF)
    lane = iota((N, W), 1)
    rows = []
    for k in range(K):
        gate = gate_ref[:, k : k + 1]
        up, rest = split(gate)
        tail = jnp.where(lane == LATER, up.astype(F32), rest.astype(F32))
        tail = jnp.where(lane < LATER + 2, tail, 0.0)
        rows.append(jnp.where(lane < LATER, gate * coef, tail).astype(BF))
    pick = rows_by_slots(jnp.concatenate(slot_codes(row_ref), axis=1))
    out_ref[...] = dot(pick, jnp.concatenate(rows, axis=0), NN).astype(BF)


def passed_kernel(coef_ref, tab_ref, grad_ref, acts_ref, pass_ref, part_ref):
    for m in range(2):
        rows = slice(m * T, (m + 1) * T)
        moved = dot(coef_ref[rows, :], tab_ref[m * W : (m + 1) * W, :], NN)
        pass_ref[rows, :] = (grad_ref[rows, :].astype(F32) + moved).astype(BF)
    own = coef_ref[:, LATER:W]
    width = acts_ref.shape[1]
    router = (dot(acts_ref[...], own, TN) / T).astype(BF)
    each = width // E
    row, col = iota((ALL, width), 0), iota((ALL, width), 1)
    peer = divided(row, ROWS)
    inner = row - ROWS * peer
    source = peer * each + inner
    first = dot(one(source == col), router, NN)
    second = dot(one((source + ROWS == col) & (inner + ROWS < each)), router, NN)
    part_ref[:, 0:E] = first.astype(BF)
    part_ref[:, E : 2 * E] = second.astype(BF)


def answer_kernel(got_ref, base_ref, back_ref, part_ref, out_ref, left_ref, right_ref, gate_ref):
    step = pl.program_id(0)

    @pl.when(step == 0)
    def _():
        got = got_ref[...].astype(F32)
        gate = got[:, LATER : LATER + 1] + got[:, LATER + 1 : LATER + 2]
        gate_ref[...] = jnp.broadcast_to(gate, (ALL, W))
        coef = jnp.where(iota((ALL, W), 1) < LATER, got, 0.0)
        half = first_half(ALL, W)
        left_ref[...] = jnp.where(half, coef, 0.0).astype(BF)
        right_ref[...] = jnp.where(half, 0.0, coef).astype(BF)

    moved = dot(left_ref[...], back_ref[0:W, :], NN) + dot(right_ref[...], back_ref[W : 2 * W, :], NN)
    out_ref[...] = (gate_ref[...] * base_ref[...].astype(F32) + moved).astype(BF)

    @pl.when(step == pl.num_programs(0) - 1)
    def _():
        out_ref[:, 160 : 160 + 2 * E] = part_ref[...]
        out_ref[:, 160 + 2 * E :] = jnp.zeros((ALL, 96 - 2 * E), BF)


def combine_kernel(got_ref, ids_ref, out_ref, router_ref, pick_ref):
    step = pl.program_id(0)

    @pl.when(step == 0)
    def _():
        pick_ref[...] = slots_by_rows(token_major(slot_codes(ids_ref)))

    own = dot(pick_ref[...], got_ref[...], NN).astype(BF)
    out_ref[...] = own.reshape(N, K, got_ref.shape[1])

    @pl.when(step == pl.num_programs(0) - 1)
    def _():
        parts = got_ref[:, 160 : 160 + 2 * E].astype(F32).reshape(E, ROWS, 2 * E)
        total = jnp.sum(parts, axis=0)
        each = router_ref.shape[1]
        turn = iota((E, 2 * E), 1) - iota((E, 2 * E), 0)
        flipped = [jnp.zeros((E, ROWS), F32)] * 2
        for _ in range(3):
            piece = total.astype(BF)
            total = total - piece.astype(F32)
            flipped = [flipped[q] + dot(one(turn == q * E), piece, NT) for q in range(2)]
        router_ref[:, 0:ROWS] = flipped[0]
        router_ref[:, ROWS:each] = flipped[1][:, 0 : each - ROWS]


def call(body, shapes, args, mib, smem=0, scratch=()):
    return pl.pallas_call(
        body,
        out_shape=[jax.ShapeDtypeStruct(s, d) for s, d in shapes],
        in_specs=[SM] * smem + [VM] * (len(args) - smem),
        out_specs=[VM] * len(shapes),
        scratch_shapes=list(scratch),
        compiler_params=pltpu.CompilerParams(vmem_limit_bytes=mib << 20),
    )(*args)


def fixed(shape, once=False):
    at = (0,) * len(shape)
    if once:
        return pl.BlockSpec(shape, lambda i: at, pipeline_mode=pl.Buffered(1))
    return pl.BlockSpec(shape, lambda i: at)


def along(shape, dim):
    return pl.BlockSpec(shape, lambda i: tuple(i if d == dim else 0 for d in range(len(shape))))


def looped(body, steps, shapes, ins, outs, args, mib, scratch):
    return pl.pallas_call(
        body,
        grid=(steps,),
        out_shape=[jax.ShapeDtypeStruct(s, d) for s, d in shapes],
        in_specs=ins,
        out_specs=outs,
        scratch_shapes=[pltpu.VMEM(s, d) for s, d in scratch],
        compiler_params=pltpu.CompilerParams(
            vmem_limit_bytes=mib << 20, dimension_semantics=("arbitrary",)
        ),
    )(*args)


def exchange(x, axis):
    return lax.all_to_all(x, axis, split_axis=0, concat_axis=0, tiled=True)


def on_device(acts, hidden, ids, version, router, down, grad_top):
    pipe = lax.axis_size("pipe")
    section = lax.axis_index("pipe")
    width = acts.shape[-1]
    inner = hidden.shape[-1]
    inputs = acts[0]
    routes = ids[0]
    mats = down[0, 0]
    grads = grad_top.reshape(N, width)
    turned = routes.transpose(0, 2, 1)
    tall = 2 * ROWS * (inner // 128) + 16

    steps = pl.cdiv(inner, 256)

    (sent,) = looped(
        dispatch_kernel,
        steps,
        [((E, tall, 128), BF)],
        [fixed((2, K, T)), along((N, K, 256), 2), along((N, 256), 1)],
        [along((E, 4 * ROWS, 128), 1)],
        (turned, hidden[0].reshape(N, K, inner), grads),
        MIBS[0],
        [((ALL, N * K), BF), ((ALL, N), BF)],
    )
    arrived = exchange(sent, "expert")

    picked_version = version[0][:, None, None] == 1
    tables = jnp.where(picked_version, router[0, 1][None], router[0, 0][None])
    flipped = tables.transpose(0, 2, 1).reshape(2 * E, width)
    id_rows = jnp.pad(
        turned.transpose(1, 0, 2).reshape(K, N).astype(BF), ((0, 8 - K), (0, width - N))
    )
    own = jnp.concatenate([flipped, id_rows], axis=0)
    held = [
        lax.ppermute(own, "pipe", [(i, i - by) for i in range(by, pipe)]) for by in range(1, pipe)
    ] + [own]
    table_rows, back, id_all = call(
        tables_kernel,
        [((2 * W, width), BF), ((2 * W, inner), BF), ((K * 8, N), F32)],
        (*held, mats),
        MIBS[1],
    )

    logits = jnp.einsum("mtd,mde->mte", inputs, tables, preferred_element_type=F32)
    labels = jnp.arange(E, dtype=I32)
    picked = routes[:, :, :, None] == labels
    chosen = jnp.sum(jnp.where(picked, logits[:, :, None, :], 0.0), axis=3)
    scores = jnp.exp(chosen)
    gating = (scores / jnp.sum(scores, axis=2, keepdims=True)).reshape(N, K)

    base, proj = looped(
        expert_kernel,
        steps,
        [((ALL, 256 * steps), BF), ((ALL, W), BF)],
        [
            fixed((E, tall, 128), True),
            along((256, width), 0),
            fixed((2 * W, inner), True),
        ],
        [along((ALL, 256), 1), fixed((ALL, W))],
        (arrived, mats, back),
        MIBS[2],
        [((ALL, inner), BF), ((ALL, 256 * steps), BF), ((ALL, 1), F32)],
    )
    proj, gating = lax.optimization_barrier((proj, gating))
    returned = exchange(proj.reshape(E, ROWS, W), "expert").reshape(ALL, W)
    (blocks,) = call(
        blocks_kernel,
        [((8, 8, K * K * N), BF)],
        (returned, turned, id_all, gating),
        MIBS[3],
    )
    blocks, where = lax.optimization_barrier((blocks, section.reshape(1)))
    gathered = exchange(blocks, "pipe")
    coef_sent, coef = call(
        solve_kernel,
        [((ALL, W), BF), ((N, W), BF)],
        (where, gathered, turned, id_all, gating),
        MIBS[4],
        smem=1,
    )
    coef_got = exchange(coef_sent.reshape(E, ROWS, W), "expert").reshape(ALL, W)
    passed, parts = call(
        passed_kernel,
        [((N, width), BF), ((ALL, 2 * E), BF)],
        (coef, table_rows, grads, inputs.reshape(N, width)),
        MIBS[5],
    )
    wide = 256 * steps
    (answer,) = looped(
        answer_kernel,
        steps,
        [((ALL, wide), BF)],
        [fixed((ALL, W)), along((ALL, 256), 1), along((2 * W, 256), 1), fixed((ALL, 2 * E))],
        [along((ALL, 256), 1)],
        (coef_got, base, back, parts),
        MIBS[6],
        [((ALL, W), BF), ((ALL, W), BF), ((ALL, W), F32)],
    )
    answered = exchange(answer.reshape(E, ROWS, wide), "expert").reshape(ALL, wide)
    hidden_grads, grad_router = looped(
        combine_kernel,
        steps,
        [((N, K, inner), BF), ((E, width // E), F32)],
        [along((ALL, 256), 1), fixed((2, K, T))],
        [along((N, K, 256), 2), fixed((E, width // E))],
        (answered, turned),
        MIBS[7],
        [((N * K, ALL), BF)],
    )
    return (
        passed.reshape(1, 2, T, width),
        hidden_grads.reshape(1, 2, T, K, inner),
        grad_router.T[None],
    )


def solution(mesh):
    placed = (
        P("pipe", None, "expert", None),
        P("pipe", None, "expert", None, None),
        P("pipe", None, "expert", None),
        P("pipe", None),
        P("pipe", None, None, None),
        P("pipe", "expert", None, None),
        P(None, "expert", None),
    )
    return jax.shard_map(
        on_device,
        mesh=mesh,
        in_specs=placed,
        out_specs=(
            P("pipe", None, "expert", None),
            P("pipe", None, "expert", None, None),
            P("pipe", "expert", None),
        ),
        check_vma=False,
    )
```

```python
import functools

import jax
import jax.numpy as jnp
from jax import lax
from jax.experimental import pallas as pl
from jax.experimental.pallas import tpu as pltpu
from jax.sharding import PartitionSpec as P

BF = jnp.bfloat16
F32 = jnp.float32
I32 = jnp.int32
NN = (((1,), (0,)), ((), ()))
NT = (((1,), (1,)), ((), ()))
TN = (((0,), (0,)), ((), ()))
VM = pl.BlockSpec(memory_space=pltpu.VMEM)
HB = pl.BlockSpec(memory_space=pltpu.HBM)
SM = pl.BlockSpec(memory_space=pltpu.SMEM)

N, T, K, E, HALF = 128, 64, 4, 32, 12
ROWS = 2 * HALF
ALL = E * ROWS
W = 256
MIBS = (62, 20, 62, 12, 12, 20, 62, 20)
LATER = 224


def dot(a, b, dims):
    return lax.dot_general(a, b, dims, preferred_element_type=F32)


def iota(shape, dim):
    return lax.broadcasted_iota(I32, shape, dim)


def one(mask):
    return jnp.where(mask, 1.0, 0.0).astype(BF)


def divided(x, by):
    return ((x.astype(F32) + 0.5) * (1.0 / by)).astype(I32)


def split(x):
    high = x.astype(BF)
    return high, (x - high.astype(F32)).astype(BF)


def slot_codes(ids_ref):
    named = []
    for k in range(K):
        row = jnp.concatenate([ids_ref[0, k : k + 1, :], ids_ref[1, k : k + 1, :]], axis=1)
        named.append(row == iota((E, N), 0))
    marks = sum(jnp.where(hit, 1.0, 0.0) for hit in named).astype(BF)
    first, second = iota((N, N), 0), iota((N, N), 1)
    earlier = one((first < second) & ((first >> 6) == (second >> 6)))
    place = dot(marks, earlier, NN) + (HALF * (iota((E, N), 1) >> 6)).astype(F32)
    return [jnp.where(hit, place, -1.0) for hit in named]


def token_major(codes):
    lane = iota((N, N * K), 1)
    spread = one((lane >> 2) == iota((N, N * K), 0))
    which = iota((E, N * K), 1) & (K - 1)
    out = jnp.zeros((E, N * K), F32)
    for k in range(K):
        out = jnp.where(which == k, dot(codes[k].astype(BF), spread, NN), out)
    return out


def rows_by_slots(code):
    expand = one(divided(iota((ALL, E), 0), ROWS) == iota((ALL, E), 1))
    row = iota((ALL, code.shape[1]), 0)
    inner = (row - ROWS * divided(row, ROWS)).astype(F32)
    return one(dot(expand, code.astype(BF), NN) == inner)


def slots_by_rows(code):
    expand = one(divided(iota((E, ALL), 1), ROWS) == iota((E, ALL), 0))
    row = iota((code.shape[1], ALL), 1)
    inner = (row - ROWS * divided(row, ROWS)).astype(F32)
    return one(dot(code.astype(BF), expand, TN) == inner)


def first_half(rows, width, start=0):
    row = iota((rows, width), 0) + start
    return (row - ROWS * divided(row, ROWS)) < HALF


def dispatch_kernel(ids_ref, hid_hbm, grad_hbm, out_hbm, hid_ref, grad_ref, out_ref, sems):
    loads = [
        pltpu.make_async_copy(grad_hbm, grad_ref, sems.at[0]),
        pltpu.make_async_copy(hid_hbm, hid_ref, sems.at[1]),
    ]
    for load in loads:
        load.start()
    codes = slot_codes(ids_ref)
    tokens = rows_by_slots(functools.reduce(jnp.maximum, codes))
    pick = rows_by_slots(token_major(codes))
    for load in loads:
        load.wait()
    width = grad_ref.shape[1]
    stores = []
    for start in range(0, width, 256):
        cols = slice(start, min(start + 256, width))
        size = cols.stop - start
        grad = dot(tokens, grad_ref[:, cols], NN)
        hid = dot(pick, hid_ref[:, :, cols].reshape(N * K, size), NN)
        first = 2 * ROWS * (start // 128)
        for lanes in range(0, size, 128):
            at = 2 * ROWS * ((start + lanes) // 128)
            cut = min(lanes + 128, size)
            left = grad[:, lanes:cut].reshape(E, ROWS, cut - lanes)
            right = hid[:, lanes:cut].reshape(E, ROWS, cut - lanes)
            if cut - lanes == 128:
                out_ref[:, at : at + ROWS, :] = left.astype(BF)
                out_ref[:, at + ROWS : at + 2 * ROWS, :] = right.astype(BF)
                last = at + 2 * ROWS
            else:
                tail = [
                    left[:, 0:16],
                    jnp.concatenate([left[:, 16:24], right[:, 0:8]], axis=1),
                    right[:, 8:24],
                    jnp.zeros((E, 16, 32), F32),
                ]
                out_ref[:, at : at + 16, :] = jnp.concatenate(tail, axis=2).astype(BF)
                last = at + 16
        part = pl.ds(first, last - first)
        store = pltpu.make_async_copy(
            out_ref.at[:, part, :], out_hbm.at[:, part, :], sems.at[2 + len(stores)]
        )
        store.start()
        stores.append(store)
    for store in stores:
        store.wait()


def tables_kernel(*refs):
    held, down_ref, tab_ref, back_ref, ids_ref = refs[:8], refs[8], refs[9], refs[10], refs[11]
    for b in range(8):
        for m in range(2):
            tab_ref[m * W + b * E : m * W + (b + 1) * E, :] = held[b][m * E : (m + 1) * E, :]
    rows = jnp.concatenate([held[b][2 * E : 2 * E + 8, 0:N].astype(F32) for b in range(8)], axis=0)
    for j in range(K):
        for b in range(8):
            ids_ref[8 * j + b : 8 * j + b + 1, :] = rows[8 * b + j : 8 * b + j + 1, :]
    for m in range(2):
        back_ref[m * W : (m + 1) * W, :] = dot(
            tab_ref[m * W : (m + 1) * W, :], down_ref[...], NT
        ).astype(BF)


def expert_kernel(
    got_hbm, down_hbm, back_hbm, base_hbm, out_ref,
    got_ref, down_ref, back_ref, base_ref, grad_ref, hid_ref, sems,
):
    inner = down_ref.shape[0]
    starts = range(0, inner, 256)
    load = pltpu.make_async_copy(got_hbm, got_ref, sems.at[0])
    load.start()
    mats = []
    for start in starts:
        rows = pl.ds(start, min(256, inner - start))
        mats.append(
            pltpu.make_async_copy(
                down_hbm.at[rows, :], down_ref.at[rows, :], sems.at[2 + len(mats)]
            )
        )
    for copy in mats:
        copy.start()
    backs = pltpu.make_async_copy(back_hbm, back_ref, sems.at[1])
    backs.start()
    load.wait()
    full = 128 * (inner // 128)
    for lanes in range(0, full, 128):
        at = 2 * ROWS * (lanes // 128)
        cols = slice(lanes, lanes + 128)
        grad_ref[:, cols] = got_ref[:, at : at + ROWS, :].reshape(ALL, 128)
        hid_ref[:, cols] = got_ref[:, at + ROWS : at + 2 * ROWS, :].reshape(ALL, 128)
    at = 2 * ROWS * (full // 128)
    tail = got_ref[:, at : at + 16, :].astype(F32)
    middle = tail[:, :, 32:64]
    grad = jnp.concatenate([tail[:, :, 0:32], middle[:, 0:8]], axis=1)
    hid = jnp.concatenate([middle[:, 8:16], tail[:, :, 64:96]], axis=1)
    grad_ref[:, full:inner] = grad.astype(BF).reshape(ALL, 32)
    hid_ref[:, full:inner] = hid.astype(BF).reshape(ALL, 32)
    total = jnp.zeros((ALL, 1), F32)
    stores = []
    for c, start in enumerate(starts):
        cols = slice(start, min(start + 256, inner))
        size = cols.stop - start
        mats[c].wait()
        base = dot(grad_ref[...], down_ref[cols, :], NT)
        base_ref[c, :, 0:size] = base.astype(BF)
        if size < 256:
            base_ref[c, :, size:] = jnp.zeros((ALL, 256 - size), BF)
        store = pltpu.make_async_copy(base_ref.at[c], base_hbm.at[c], sems.at[2 + len(mats) + c])
        store.start()
        stores.append(store)
        total = total + jnp.sum(hid_ref[:, cols].astype(F32) * base, axis=1, keepdims=True)
    high, low = split(total)
    backs.wait()
    left = dot(hid_ref[...], back_ref[0:W, :], NT)
    right = dot(hid_ref[...], back_ref[W : 2 * W, :], NT)
    proj = jnp.where(first_half(ALL, W), left, right)
    lane = iota((ALL, W), 1)
    tail = jnp.where(lane == LATER, high.astype(F32), low.astype(F32))
    tail = jnp.where(lane < LATER + 2, tail, 0.0)
    out_ref[...] = jnp.where(lane < LATER, proj, tail).astype(BF)
    for store in stores:
        store.wait()


def id_masks(ids_ref):
    spread = one(divided(iota((8, W), 1), E) == iota((8, W), 0))
    lane = iota((N, W), 1) & (E - 1)
    masks = []
    for j in range(K):
        wide = dot(ids_ref[8 * j : 8 * j + 8, :].astype(BF), spread, TN)
        masks.append(wide == lane.astype(F32))
    return masks, spread


def blocks_kernel(got_ref, row_ref, ids_ref, gate_ref, out_ref):
    pick = slots_by_rows(jnp.concatenate(slot_codes(row_ref), axis=1))
    slots = dot(pick, got_ref[...], NN)
    gates = [gate_ref[:, k : k + 1] for k in range(K)]
    parts = [slots[k * N : (k + 1) * N] for k in range(K)]
    lane = iota((N, W), 1)
    full = []
    for part in parts:
        dots = part[:, LATER : LATER + 1] + part[:, LATER + 1 : LATER + 2]
        full.append(jnp.where(lane < LATER, part, dots))
    mean = sum(gates[k] * full[k] for k in range(K))
    masks, spread = id_masks(ids_ref)
    rows = []
    for k in range(K):
        value = gates[k] * (full[k] - mean)
        high, low = split(value)
        for j in range(K):
            source = jnp.where(masks[j] & (lane < LATER), high.astype(F32), 0.0)
            if j < 2:
                extra = high if j == 0 else low
                source = jnp.where(lane == LATER, extra.astype(F32), source)
            rows.append(source.astype(BF))
    packed = dot(spread, jnp.concatenate(rows, axis=0), NT).astype(BF)
    for d in range(8):
        out_ref[d] = packed


def solve_kernel(at_ref, got_ref, row_ref, ids_ref, gate_ref, out_ref, coef_ref):
    at = at_ref[0]
    depth = iota((8, K * N), 0)
    found = jnp.zeros((8, K * N), F32)
    for back in range(7, -1, -1):
        where = jnp.minimum(at + back, 7)
        valid = (at + back <= 7).astype(F32)
        block = got_ref[where].astype(F32)
        fresh = []
        for k in range(K):
            part = block[:, k * K * N : (k + 1) * K * N]
            fixed = part[7:8, 0:N] + part[7:8, N : 2 * N]
            terms = jnp.sum(part * found, axis=0, keepdims=True)
            total = fixed
            for j in range(K):
                total = total + terms[:, j * N : (j + 1) * N]
            fresh.append(total * valid)
        fresh = jnp.concatenate(fresh, axis=1)
        if back:
            found = jnp.where(depth == 0, fresh, pltpu.roll(found, 1, 0))
        else:
            found = jnp.where(depth == 7, fresh, found)
    masks, spread = id_masks(ids_ref)
    high, low = split(found)
    coef = jnp.zeros((N, W), F32)
    for j in range(K):
        cut = slice(j * N, (j + 1) * N)
        wide = dot(high[:, cut], spread, TN) + dot(low[:, cut], spread, TN)
        coef = jnp.where(masks[j], wide, coef)
    coef_ref[...] = coef.astype(BF)
    lane = iota((N, W), 1)
    rows = []
    for k in range(K):
        gate = gate_ref[:, k : k + 1]
        up, rest = split(gate)
        tail = jnp.where(lane == LATER, up.astype(F32), rest.astype(F32))
        tail = jnp.where(lane < LATER + 2, tail, 0.0)
        rows.append(jnp.where(lane < LATER, gate * coef, tail).astype(BF))
    pick = rows_by_slots(jnp.concatenate(slot_codes(row_ref), axis=1))
    out_ref[...] = dot(pick, jnp.concatenate(rows, axis=0), NN).astype(BF)


def passed_kernel(coef_ref, tab_ref, grad_ref, acts_ref, pass_ref, part_ref):
    for m in range(2):
        rows = slice(m * T, (m + 1) * T)
        moved = dot(coef_ref[rows, :], tab_ref[m * W : (m + 1) * W, :], NN)
        pass_ref[rows, :] = (grad_ref[rows, :].astype(F32) + moved).astype(BF)
    own = coef_ref[:, LATER:W]
    width = acts_ref.shape[1]
    router = (dot(acts_ref[...], own, TN) / T).astype(BF)
    each = width // E
    row, col = iota((ALL, width), 0), iota((ALL, width), 1)
    peer = divided(row, ROWS)
    inner = row - ROWS * peer
    source = peer * each + inner
    first = dot(one(source == col), router, NN)
    second = dot(one((source + ROWS == col) & (inner + ROWS < each)), router, NN)
    part_ref[:, 0:E] = first.astype(BF)
    part_ref[:, E : 2 * E] = second.astype(BF)


def answer_kernel(got_ref, base_hbm, back_hbm, part_ref, out_hbm, base_ref, back_ref, out_ref, sems):
    width = back_ref.shape[1]
    count = base_ref.shape[0]
    backs = pltpu.make_async_copy(back_hbm, back_ref, sems.at[0])
    backs.start()
    loads = []
    for c in range(count):
        load = pltpu.make_async_copy(base_hbm.at[c], base_ref.at[c], sems.at[1 + c])
        load.start()
        loads.append(load)
    got = got_ref[...].astype(F32)
    gate = got[:, LATER : LATER + 1] + got[:, LATER + 1 : LATER + 2]
    coef = jnp.where(iota((ALL, W), 1) < LATER, got, 0.0)
    half = first_half(ALL, W)
    left = jnp.where(half, coef, 0.0).astype(BF)
    right = jnp.where(half, 0.0, coef).astype(BF)
    backs.wait()
    stores = []
    for c in range(count):
        cols = slice(256 * c, min(256 * c + 256, width))
        moved = dot(left, back_ref[0:W, cols], NN) + dot(right, back_ref[W : 2 * W, cols], NN)
        loads[c].wait()
        base = base_ref[c, :, 0 : cols.stop - cols.start].astype(F32)
        value = gate * base + moved
        if c == count - 1:
            spare = jnp.zeros((ALL, 96 - 2 * E), F32)
            value = jnp.concatenate([value, part_ref[...].astype(F32), spare], axis=1)
        for half_at in range(2):
            tile = value[:, 128 * half_at : 128 * half_at + 128].astype(BF)
            at = ROWS * (2 * c + half_at)
            out_ref[:, at : at + ROWS, :] = tile.reshape(E, ROWS, 128)
        part = pl.ds(2 * ROWS * c, 2 * ROWS)
        store = pltpu.make_async_copy(
            out_ref.at[:, part, :], out_hbm.at[:, part, :], sems.at[1 + count + c]
        )
        store.start()
        stores.append(store)
    for store in stores:
        store.wait()


def combine_kernel(got_ref, ids_ref, out_ref, router_ref):
    pick = slots_by_rows(token_major(slot_codes(ids_ref)))
    width = out_ref.shape[2]

    def tile(t):
        return got_ref[:, ROWS * t : ROWS * t + ROWS, :].reshape(ALL, 128)

    for start in range(0, width, 256):
        cols = slice(start, min(start + 256, width))
        t = start // 128
        both = jnp.concatenate([tile(t), tile(t + 1)], axis=1)
        own = dot(pick, both, NN).astype(BF)[:, 0 : cols.stop - start]
        out_ref[:, :, cols] = own.reshape(N, K, cols.stop - start)
    parts = tile(width // 128).astype(F32)[:, 32 : 32 + 2 * E].reshape(E, ROWS, 2 * E)
    total = jnp.sum(parts, axis=0)
    each = width // E
    turn = iota((E, 2 * E), 1) - iota((E, 2 * E), 0)
    flipped = [jnp.zeros((E, ROWS), F32)] * 2
    for _ in range(3):
        piece = total.astype(BF)
        total = total - piece.astype(F32)
        flipped = [flipped[q] + dot(one(turn == q * E), piece, NT) for q in range(2)]
    router_ref[:, 0:ROWS] = flipped[0]
    router_ref[:, ROWS:each] = flipped[1][:, 0 : each - ROWS]


def call(body, shapes, args, mib, smem=0, scratch=(), sems=0, far=(), far_out=()):
    ins = [SM] * smem + [VM] * (len(args) - smem)
    ins = [HB if i in far else spec for i, spec in enumerate(ins)]
    held = [pltpu.VMEM(s, d) for s, d in scratch]
    if sems:
        held.append(pltpu.SemaphoreType.DMA((sems,)))
    return pl.pallas_call(
        body,
        out_shape=[jax.ShapeDtypeStruct(s, d) for s, d in shapes],
        in_specs=ins,
        out_specs=[HB if i in far_out else VM for i in range(len(shapes))],
        scratch_shapes=held,
        compiler_params=pltpu.CompilerParams(vmem_limit_bytes=mib << 20),
    )(*args)


def exchange(x, axis):
    return lax.all_to_all(x, axis, split_axis=0, concat_axis=0, tiled=True)


def on_device(acts, hidden, ids, version, router, down, grad_top):
    pipe = lax.axis_size("pipe")
    section = lax.axis_index("pipe")
    width = acts.shape[-1]
    inner = hidden.shape[-1]
    inputs = acts[0]
    routes = ids[0]
    mats = down[0, 0]
    grads = grad_top.reshape(N, width)
    turned = routes.transpose(0, 2, 1)
    tall = 2 * ROWS * (inner // 128) + 16

    steps = pl.cdiv(inner, 256)

    (sent,) = call(
        dispatch_kernel,
        [((E, tall, 128), BF)],
        (turned, hidden[0].reshape(N, K, inner), grads),
        MIBS[0],
        scratch=[((N, K, inner), BF), ((N, width), BF), ((E, tall, 128), BF)],
        sems=2 + steps,
        far=(1, 2),
        far_out=(0,),
    )
    arrived = exchange(sent, "expert")

    picked_version = version[0][:, None, None] == 1
    tables = jnp.where(picked_version, router[0, 1][None], router[0, 0][None])
    flipped = tables.transpose(0, 2, 1).reshape(2 * E, width)
    id_rows = jnp.pad(
        turned.transpose(1, 0, 2).reshape(K, N).astype(BF), ((0, 8 - K), (0, width - N))
    )
    own = jnp.concatenate([flipped, id_rows], axis=0)
    held = [
        lax.ppermute(own, "pipe", [(i, i - by) for i in range(by, pipe)]) for by in range(1, pipe)
    ] + [own]
    table_rows, back, id_all = call(
        tables_kernel,
        [((2 * W, width), BF), ((2 * W, inner), BF), ((K * 8, N), F32)],
        (*held, mats),
        MIBS[1],
    )

    logits = jnp.einsum("mtd,mde->mte", inputs, tables, preferred_element_type=F32)
    labels = jnp.arange(E, dtype=I32)
    picked = routes[:, :, :, None] == labels
    chosen = jnp.sum(jnp.where(picked, logits[:, :, None, :], 0.0), axis=3)
    scores = jnp.exp(chosen)
    gating = (scores / jnp.sum(scores, axis=2, keepdims=True)).reshape(N, K)

    base, proj = call(
        expert_kernel,
        [((steps, ALL, 256), BF), ((ALL, W), BF)],
        (arrived, mats, back),
        MIBS[2],
        scratch=[
            ((E, tall, 128), BF),
            ((inner, width), BF),
            ((2 * W, inner), BF),
            ((steps, ALL, 256), BF),
            ((ALL, width), BF),
            ((ALL, inner), BF),
        ],
        sems=2 + 2 * steps,
        far=(0, 1, 2),
        far_out=(0,),
    )
    proj, gating = lax.optimization_barrier((proj, gating))
    returned = exchange(proj.reshape(E, ROWS, W), "expert").reshape(ALL, W)
    (blocks,) = call(
        blocks_kernel,
        [((8, 8, K * K * N), BF)],
        (returned, turned, id_all, gating),
        MIBS[3],
    )
    blocks, where = lax.optimization_barrier((blocks, section.reshape(1)))
    gathered = exchange(blocks, "pipe")
    coef_sent, coef = call(
        solve_kernel,
        [((ALL, W), BF), ((N, W), BF)],
        (where, gathered, turned, id_all, gating),
        MIBS[4],
        smem=1,
    )
    coef_got = exchange(coef_sent.reshape(E, ROWS, W), "expert").reshape(ALL, W)
    passed, parts = call(
        passed_kernel,
        [((N, width), BF), ((ALL, 2 * E), BF)],
        (coef, table_rows, grads, inputs.reshape(N, width)),
        MIBS[5],
    )
    back_tall = 2 * ROWS * steps
    (answer,) = call(
        answer_kernel,
        [((E, back_tall, 128), BF)],
        (coef_got, base, back, parts),
        MIBS[6],
        scratch=[((steps, ALL, 256), BF), ((2 * W, inner), BF), ((E, back_tall, 128), BF)],
        sems=1 + 2 * steps,
        far=(1, 2),
        far_out=(0,),
    )
    answered = exchange(answer, "expert")
    hidden_grads, grad_router = call(
        combine_kernel, [((N, K, inner), BF), ((E, width // E), F32)], (answered, turned), MIBS[7]
    )
    return (
        passed.reshape(1, 2, T, width),
        hidden_grads.reshape(1, 2, T, K, inner),
        grad_router.T[None],
    )


def solution(mesh):
    placed = (
        P("pipe", None, "expert", None),
        P("pipe", None, "expert", None, None),
        P("pipe", None, "expert", None),
        P("pipe", None),
        P("pipe", None, None, None),
        P("pipe", "expert", None, None),
        P(None, "expert", None),
    )
    return jax.shard_map(
        on_device,
        mesh=mesh,
        in_specs=placed,
        out_specs=(
            P("pipe", None, "expert", None),
            P("pipe", None, "expert", None, None),
            P("pipe", "expert", None),
        ),
        check_vma=False,
    )
```

```python
import functools

import jax
import jax.numpy as jnp
from jax import lax
from jax.experimental import pallas as pl
from jax.experimental.pallas import tpu as pltpu
from jax.sharding import PartitionSpec as P

BF = jnp.bfloat16
F32 = jnp.float32
I32 = jnp.int32
NN = (((1,), (0,)), ((), ()))
NT = (((1,), (1,)), ((), ()))
TN = (((0,), (0,)), ((), ()))
VM = pl.BlockSpec(memory_space=pltpu.VMEM)
HB = pl.BlockSpec(memory_space=pltpu.HBM)
SM = pl.BlockSpec(memory_space=pltpu.SMEM)

N, T, K, E, HALF = 128, 64, 4, 32, 12
ROWS = 2 * HALF
ALL = E * ROWS
W = 256
MIBS = (62, 20, 24, 12, 12, 16, 16, 20)
LATER = 224


def dot(a, b, dims):
    return lax.dot_general(a, b, dims, preferred_element_type=F32)


def iota(shape, dim):
    return lax.broadcasted_iota(I32, shape, dim)


def one(mask):
    return jnp.where(mask, 1.0, 0.0).astype(BF)


def divided(x, by):
    return ((x.astype(F32) + 0.5) * (1.0 / by)).astype(I32)


def split(x):
    high = x.astype(BF)
    return high, (x - high.astype(F32)).astype(BF)


def slot_codes(ids_ref):
    named = []
    for k in range(K):
        row = jnp.concatenate([ids_ref[0, k : k + 1, :], ids_ref[1, k : k + 1, :]], axis=1)
        named.append(row == iota((E, N), 0))
    marks = sum(jnp.where(hit, 1.0, 0.0) for hit in named).astype(BF)
    first, second = iota((N, N), 0), iota((N, N), 1)
    earlier = one((first < second) & ((first >> 6) == (second >> 6)))
    place = dot(marks, earlier, NN) + (HALF * (iota((E, N), 1) >> 6)).astype(F32)
    return [jnp.where(hit, place, -1.0) for hit in named]


def token_major(codes):
    lane = iota((N, N * K), 1)
    spread = one((lane >> 2) == iota((N, N * K), 0))
    which = iota((E, N * K), 1) & (K - 1)
    out = jnp.zeros((E, N * K), F32)
    for k in range(K):
        out = jnp.where(which == k, dot(codes[k].astype(BF), spread, NN), out)
    return out


def rows_by_slots(code):
    expand = one(divided(iota((ALL, E), 0), ROWS) == iota((ALL, E), 1))
    row = iota((ALL, code.shape[1]), 0)
    inner = (row - ROWS * divided(row, ROWS)).astype(F32)
    return one(dot(expand, code.astype(BF), NN) == inner)


def slots_by_rows(code):
    expand = one(divided(iota((E, ALL), 1), ROWS) == iota((E, ALL), 0))
    row = iota((code.shape[1], ALL), 1)
    inner = (row - ROWS * divided(row, ROWS)).astype(F32)
    return one(dot(code.astype(BF), expand, TN) == inner)


def first_half(rows, width, start=0):
    row = iota((rows, width), 0) + start
    return (row - ROWS * divided(row, ROWS)) < HALF


def dispatch_kernel(ids_ref, hid_hbm, grad_hbm, out_hbm, hid_ref, grad_ref, out_ref, sems):
    loads = [
        pltpu.make_async_copy(grad_hbm, grad_ref, sems.at[0]),
        pltpu.make_async_copy(hid_hbm, hid_ref, sems.at[1]),
    ]
    for load in loads:
        load.start()
    codes = slot_codes(ids_ref)
    tokens = rows_by_slots(functools.reduce(jnp.maximum, codes))
    pick = rows_by_slots(token_major(codes))
    for load in loads:
        load.wait()
    width = grad_ref.shape[1]
    stores = []
    for start in range(0, width, 256):
        cols = slice(start, min(start + 256, width))
        size = cols.stop - start
        grad = dot(tokens, grad_ref[:, cols], NN)
        hid = dot(pick, hid_ref[:, :, cols].reshape(N * K, size), NN)
        first = 2 * ROWS * (start // 128)
        for lanes in range(0, size, 128):
            at = 2 * ROWS * ((start + lanes) // 128)
            cut = min(lanes + 128, size)
            left = grad[:, lanes:cut].reshape(E, ROWS, cut - lanes)
            right = hid[:, lanes:cut].reshape(E, ROWS, cut - lanes)
            if cut - lanes == 128:
                out_ref[:, at : at + ROWS, :] = left.astype(BF)
                out_ref[:, at + ROWS : at + 2 * ROWS, :] = right.astype(BF)
                last = at + 2 * ROWS
            else:
                tail = [
                    left[:, 0:16],
                    jnp.concatenate([left[:, 16:24], right[:, 0:8]], axis=1),
                    right[:, 8:24],
                    jnp.zeros((E, 16, 32), F32),
                ]
                out_ref[:, at : at + 16, :] = jnp.concatenate(tail, axis=2).astype(BF)
                last = at + 16
        part = pl.ds(first, last - first)
        store = pltpu.make_async_copy(
            out_ref.at[:, part, :], out_hbm.at[:, part, :], sems.at[2 + len(stores)]
        )
        store.start()
        stores.append(store)
    for store in stores:
        store.wait()


def tables_kernel(*refs):
    held, down_ref, tab_ref, back_ref, ids_ref = refs[:8], refs[8], refs[9], refs[10], refs[11]
    for b in range(8):
        for m in range(2):
            tab_ref[m * W + b * E : m * W + (b + 1) * E, :] = held[b][m * E : (m + 1) * E, :]
    rows = jnp.concatenate([held[b][2 * E : 2 * E + 8, 0:N].astype(F32) for b in range(8)], axis=0)
    for j in range(K):
        for b in range(8):
            ids_ref[8 * j + b : 8 * j + b + 1, :] = rows[8 * b + j : 8 * b + j + 1, :]
    for m in range(2):
        back_ref[m * W : (m + 1) * W, :] = dot(
            tab_ref[m * W : (m + 1) * W, :], down_ref[...], NT
        ).astype(BF)


def expert_kernel(got_ref, down_ref, back_ref, base_ref, out_ref, grad_ref, hid_ref):
    inner = down_ref.shape[0]
    full = 128 * (inner // 128)
    for lanes in range(0, full, 128):
        at = 2 * ROWS * (lanes // 128)
        cols = slice(lanes, lanes + 128)
        grad_ref[:, cols] = got_ref[:, at : at + ROWS, :].reshape(ALL, 128)
        hid_ref[:, cols] = got_ref[:, at + ROWS : at + 2 * ROWS, :].reshape(ALL, 128)
    at = 2 * ROWS * (full // 128)
    tail = got_ref[:, at : at + 16, :].astype(F32)
    middle = tail[:, :, 32:64]
    grad = jnp.concatenate([tail[:, :, 0:32], middle[:, 0:8]], axis=1)
    hid = jnp.concatenate([middle[:, 8:16], tail[:, :, 64:96]], axis=1)
    grad_ref[:, full:inner] = grad.astype(BF).reshape(ALL, 32)
    hid_ref[:, full:inner] = hid.astype(BF).reshape(ALL, 32)
    total = jnp.zeros((ALL, 1), F32)
    for start in range(0, inner, 256):
        cols = slice(start, min(start + 256, inner))
        base = dot(grad_ref[...], down_ref[cols, :], NT)
        base_ref[:, cols] = base.astype(BF)
        total = total + jnp.sum(hid_ref[:, cols].astype(F32) * base, axis=1, keepdims=True)
    high, low = split(total)
    left = dot(hid_ref[...], back_ref[0:W, :], NT)
    right = dot(hid_ref[...], back_ref[W : 2 * W, :], NT)
    proj = jnp.where(first_half(ALL, W), left, right)
    lane = iota((ALL, W), 1)
    tail = jnp.where(lane == LATER, high.astype(F32), low.astype(F32))
    tail = jnp.where(lane < LATER + 2, tail, 0.0)
    out_ref[...] = jnp.where(lane < LATER, proj, tail).astype(BF)


def id_masks(ids_ref):
    spread = one(divided(iota((8, W), 1), E) == iota((8, W), 0))
    lane = iota((N, W), 1) & (E - 1)
    masks = []
    for j in range(K):
        wide = dot(ids_ref[8 * j : 8 * j + 8, :].astype(BF), spread, TN)
        masks.append(wide == lane.astype(F32))
    return masks, spread


def blocks_kernel(got_ref, row_ref, ids_ref, gate_ref, out_ref):
    pick = slots_by_rows(jnp.concatenate(slot_codes(row_ref), axis=1))
    slots = dot(pick, got_ref[...], NN)
    gates = [gate_ref[:, k : k + 1] for k in range(K)]
    parts = [slots[k * N : (k + 1) * N] for k in range(K)]
    lane = iota((N, W), 1)
    full = []
    for part in parts:
        dots = part[:, LATER : LATER + 1] + part[:, LATER + 1 : LATER + 2]
        full.append(jnp.where(lane < LATER, part, dots))
    mean = sum(gates[k] * full[k] for k in range(K))
    masks, spread = id_masks(ids_ref)
    rows = []
    for k in range(K):
        value = gates[k] * (full[k] - mean)
        high, low = split(value)
        for j in range(K):
            source = jnp.where(masks[j] & (lane < LATER), high.astype(F32), 0.0)
            if j < 2:
                extra = high if j == 0 else low
                source = jnp.where(lane == LATER, extra.astype(F32), source)
            rows.append(source.astype(BF))
    packed = dot(spread, jnp.concatenate(rows, axis=0), NT).astype(BF)
    for d in range(8):
        out_ref[d] = packed


def solve_kernel(at_ref, got_ref, row_ref, ids_ref, gate_ref, out_ref, coef_ref):
    at = at_ref[0]
    depth = iota((8, K * N), 0)
    found = jnp.zeros((8, K * N), F32)
    for back in range(7, -1, -1):
        where = jnp.minimum(at + back, 7)
        valid = (at + back <= 7).astype(F32)
        block = got_ref[where].astype(F32)
        fresh = []
        for k in range(K):
            part = block[:, k * K * N : (k + 1) * K * N]
            fixed = part[7:8, 0:N] + part[7:8, N : 2 * N]
            terms = jnp.sum(part * found, axis=0, keepdims=True)
            total = fixed
            for j in range(K):
                total = total + terms[:, j * N : (j + 1) * N]
            fresh.append(total * valid)
        fresh = jnp.concatenate(fresh, axis=1)
        if back:
            found = jnp.where(depth == 0, fresh, pltpu.roll(found, 1, 0))
        else:
            found = jnp.where(depth == 7, fresh, found)
    masks, spread = id_masks(ids_ref)
    high, low = split(found)
    coef = jnp.zeros((N, W), F32)
    for j in range(K):
        cut = slice(j * N, (j + 1) * N)
        wide = dot(high[:, cut], spread, TN) + dot(low[:, cut], spread, TN)
        coef = jnp.where(masks[j], wide, coef)
    coef_ref[...] = coef.astype(BF)
    lane = iota((N, W), 1)
    rows = []
    for k in range(K):
        gate = gate_ref[:, k : k + 1]
        up, rest = split(gate)
        tail = jnp.where(lane == LATER, up.astype(F32), rest.astype(F32))
        tail = jnp.where(lane < LATER + 2, tail, 0.0)
        rows.append(jnp.where(lane < LATER, gate * coef, tail).astype(BF))
    pick = rows_by_slots(jnp.concatenate(slot_codes(row_ref), axis=1))
    out_ref[...] = dot(pick, jnp.concatenate(rows, axis=0), NN).astype(BF)


def passed_kernel(coef_ref, tab_ref, grad_ref, acts_ref, pass_ref, part_ref):
    for m in range(2):
        rows = slice(m * T, (m + 1) * T)
        moved = dot(coef_ref[rows, :], tab_ref[m * W : (m + 1) * W, :], NN)
        pass_ref[rows, :] = (grad_ref[rows, :].astype(F32) + moved).astype(BF)
    own = coef_ref[:, LATER:W]
    width = acts_ref.shape[1]
    router = (dot(acts_ref[...], own, TN) / T).astype(BF)
    each = width // E
    row, col = iota((ALL, width), 0), iota((ALL, width), 1)
    peer = divided(row, ROWS)
    inner = row - ROWS * peer
    source = peer * each + inner
    first = dot(one(source == col), router, NN)
    second = dot(one((source + ROWS == col) & (inner + ROWS < each)), router, NN)
    part_ref[:, 0:E] = first.astype(BF)
    part_ref[:, E : 2 * E] = second.astype(BF)


def answer_kernel(got_ref, base_ref, back_ref, part_ref, out_ref):
    width = base_ref.shape[1]
    got = got_ref[...].astype(F32)
    gate = got[:, LATER : LATER + 1] + got[:, LATER + 1 : LATER + 2]
    coef = jnp.where(iota((ALL, W), 1) < LATER, got, 0.0)
    half = first_half(ALL, W)
    left = jnp.where(half, coef, 0.0).astype(BF)
    right = jnp.where(half, 0.0, coef).astype(BF)
    for start in range(0, width, 256):
        cols = slice(start, min(start + 256, width))
        moved = dot(left, back_ref[0:W, cols], NN) + dot(right, back_ref[W : 2 * W, cols], NN)
        out_ref[:, cols] = (gate * base_ref[:, cols].astype(F32) + moved).astype(BF)
    out_ref[:, width : width + 2 * E] = part_ref[...]
    out_ref[:, width + 2 * E :] = jnp.zeros((ALL, out_ref.shape[1] - width - 2 * E), BF)


def combine_kernel(got_ref, ids_ref, out_ref, router_ref):
    pick = slots_by_rows(token_major(slot_codes(ids_ref)))
    width = out_ref.shape[2]
    for start in range(0, width, 256):
        cols = slice(start, min(start + 256, width))
        own = dot(pick, got_ref[:, cols], NN).astype(BF)
        out_ref[:, :, cols] = own.reshape(N, K, cols.stop - start)
    parts = got_ref[:, width : width + 2 * E].astype(F32).reshape(E, ROWS, 2 * E)
    total = jnp.sum(parts, axis=0)
    each = width // E
    turn = iota((E, 2 * E), 1) - iota((E, 2 * E), 0)
    flipped = [jnp.zeros((E, ROWS), F32)] * 2
    for _ in range(3):
        piece = total.astype(BF)
        total = total - piece.astype(F32)
        flipped = [flipped[q] + dot(one(turn == q * E), piece, NT) for q in range(2)]
    router_ref[:, 0:ROWS] = flipped[0]
    router_ref[:, ROWS:each] = flipped[1][:, 0 : each - ROWS]


def call(body, shapes, args, mib, smem=0, scratch=(), sems=0, far=(), far_out=()):
    ins = [SM] * smem + [VM] * (len(args) - smem)
    ins = [HB if i in far else spec for i, spec in enumerate(ins)]
    held = [pltpu.VMEM(s, d) for s, d in scratch]
    if sems:
        held.append(pltpu.SemaphoreType.DMA((sems,)))
    return pl.pallas_call(
        body,
        out_shape=[jax.ShapeDtypeStruct(s, d) for s, d in shapes],
        in_specs=ins,
        out_specs=[HB if i in far_out else VM for i in range(len(shapes))],
        scratch_shapes=held,
        compiler_params=pltpu.CompilerParams(vmem_limit_bytes=mib << 20),
    )(*args)


def exchange(x, axis):
    return lax.all_to_all(x, axis, split_axis=0, concat_axis=0, tiled=True)


def on_device(acts, hidden, ids, version, router, down, grad_top):
    pipe = lax.axis_size("pipe")
    section = lax.axis_index("pipe")
    width = acts.shape[-1]
    inner = hidden.shape[-1]
    inputs = acts[0]
    routes = ids[0]
    mats = down[0, 0]
    grads = grad_top.reshape(N, width)
    turned = routes.transpose(0, 2, 1)
    tall = 2 * ROWS * (inner // 128) + 16

    steps = pl.cdiv(inner, 256)

    (sent,) = call(
        dispatch_kernel,
        [((E, tall, 128), BF)],
        (turned, hidden[0].reshape(N, K, inner), grads),
        MIBS[0],
        scratch=[((N, K, inner), BF), ((N, width), BF), ((E, tall, 128), BF)],
        sems=2 + steps,
        far=(1, 2),
        far_out=(0,),
    )
    arrived = exchange(sent, "expert")

    picked_version = version[0][:, None, None] == 1
    tables = jnp.where(picked_version, router[0, 1][None], router[0, 0][None])
    flipped = tables.transpose(0, 2, 1).reshape(2 * E, width)
    id_rows = jnp.pad(
        turned.transpose(1, 0, 2).reshape(K, N).astype(BF), ((0, 8 - K), (0, width - N))
    )
    own = jnp.concatenate([flipped, id_rows], axis=0)
    held = [
        lax.ppermute(own, "pipe", [(i, i - by) for i in range(by, pipe)]) for by in range(1, pipe)
    ] + [own]
    table_rows, back, id_all = call(
        tables_kernel,
        [((2 * W, width), BF), ((2 * W, inner), BF), ((K * 8, N), F32)],
        (*held, mats),
        MIBS[1],
    )

    logits = jnp.einsum("mtd,mde->mte", inputs, tables, preferred_element_type=F32)
    labels = jnp.arange(E, dtype=I32)
    picked = routes[:, :, :, None] == labels
    chosen = jnp.sum(jnp.where(picked, logits[:, :, None, :], 0.0), axis=3)
    scores = jnp.exp(chosen)
    gating = (scores / jnp.sum(scores, axis=2, keepdims=True)).reshape(N, K)

    base, proj = call(
        expert_kernel,
        [((ALL, inner), BF), ((ALL, W), BF)],
        (arrived, mats, back),
        MIBS[2],
        scratch=[((ALL, width), BF), ((ALL, inner), BF)],
    )
    rest = (gating, turned, id_all, section.reshape(1), grads, inputs, table_rows, back, base)
    proj, rest = lax.optimization_barrier((proj, rest))
    returned = exchange(proj.reshape(E, ROWS, W), "expert").reshape(ALL, W)
    returned, rest = lax.optimization_barrier((returned, rest))
    gating, turned, id_all, where, grads, inputs, table_rows, back, base = rest
    (blocks,) = call(
        blocks_kernel,
        [((8, 8, K * K * N), BF)],
        (returned, turned, id_all, gating),
        MIBS[3],
    )
    blocks, rest = lax.optimization_barrier((blocks, rest))
    gathered = exchange(blocks, "pipe")
    gathered, rest = lax.optimization_barrier((gathered, rest))
    gating, turned, id_all, where, grads, inputs, table_rows, back, base = rest
    coef_sent, coef = call(
        solve_kernel,
        [((ALL, W), BF), ((N, W), BF)],
        (where, gathered, turned, id_all, gating),
        MIBS[4],
        smem=1,
    )
    coef_sent, coef, rest = lax.optimization_barrier((coef_sent, coef, rest))
    coef_got = exchange(coef_sent.reshape(E, ROWS, W), "expert").reshape(ALL, W)
    coef_got, coef, rest = lax.optimization_barrier((coef_got, coef, rest))
    gating, turned, id_all, where, grads, inputs, table_rows, back, base = rest
    passed, parts = call(
        passed_kernel,
        [((N, width), BF), ((ALL, 2 * E), BF)],
        (coef, table_rows, grads, inputs.reshape(N, width)),
        MIBS[5],
    )
    wide = 256 * steps
    (answer,) = call(
        answer_kernel, [((ALL, wide), BF)], (coef_got, base, back, parts), MIBS[6]
    )
    answered = exchange(answer.reshape(E, ROWS, wide), "expert").reshape(ALL, wide)
    hidden_grads, grad_router = call(
        combine_kernel, [((N, K, inner), BF), ((E, width // E), F32)], (answered, turned), MIBS[7]
    )
    return (
        passed.reshape(1, 2, T, width),
        hidden_grads.reshape(1, 2, T, K, inner),
        grad_router.T[None],
    )


def solution(mesh):
    placed = (
        P("pipe", None, "expert", None),
        P("pipe", None, "expert", None, None),
        P("pipe", None, "expert", None),
        P("pipe", None),
        P("pipe", None, None, None),
        P("pipe", "expert", None, None),
        P(None, "expert", None),
    )
    return jax.shard_map(
        on_device,
        mesh=mesh,
        in_specs=placed,
        out_specs=(
            P("pipe", None, "expert", None),
            P("pipe", None, "expert", None, None),
            P("pipe", "expert", None),
        ),
        check_vma=False,
    )
```

```python
import functools

import jax
import jax.numpy as jnp
from jax import lax
from jax.experimental import pallas as pl
from jax.experimental.pallas import tpu as pltpu
from jax.sharding import PartitionSpec as P

BF = jnp.bfloat16
F32 = jnp.float32
I32 = jnp.int32
NN = (((1,), (0,)), ((), ()))
NT = (((1,), (1,)), ((), ()))
TN = (((0,), (0,)), ((), ()))
VM = pl.BlockSpec(memory_space=pltpu.VMEM)
HB = pl.BlockSpec(memory_space=pltpu.HBM)
SM = pl.BlockSpec(memory_space=pltpu.SMEM)

N, T, K, E, HALF = 128, 64, 4, 32, 12
ROWS = 2 * HALF
ALL = E * ROWS
W = 256
MIBS = (62, 20, 24, 12, 12, 16, 16, 20)
LATER = 224


def dot(a, b, dims):
    return lax.dot_general(a, b, dims, preferred_element_type=F32)


def iota(shape, dim):
    return lax.broadcasted_iota(I32, shape, dim)


def one(mask):
    return jnp.where(mask, 1.0, 0.0).astype(BF)


def divided(x, by):
    return ((x.astype(F32) + 0.5) * (1.0 / by)).astype(I32)


def split(x):
    high = x.astype(BF)
    return high, (x - high.astype(F32)).astype(BF)


def slot_codes(ids_ref):
    named = []
    for k in range(K):
        row = jnp.concatenate([ids_ref[0, k : k + 1, :], ids_ref[1, k : k + 1, :]], axis=1)
        named.append(row == iota((E, N), 0))
    marks = sum(jnp.where(hit, 1.0, 0.0) for hit in named).astype(BF)
    first, second = iota((N, N), 0), iota((N, N), 1)
    earlier = one((first < second) & ((first >> 6) == (second >> 6)))
    place = dot(marks, earlier, NN) + (HALF * (iota((E, N), 1) >> 6)).astype(F32)
    return [jnp.where(hit, place, -1.0) for hit in named]


def token_major(codes):
    lane = iota((N, N * K), 1)
    spread = one((lane >> 2) == iota((N, N * K), 0))
    which = iota((E, N * K), 1) & (K - 1)
    out = jnp.zeros((E, N * K), F32)
    for k in range(K):
        out = jnp.where(which == k, dot(codes[k].astype(BF), spread, NN), out)
    return out


def rows_by_slots(code):
    expand = one(divided(iota((ALL, E), 0), ROWS) == iota((ALL, E), 1))
    row = iota((ALL, code.shape[1]), 0)
    inner = (row - ROWS * divided(row, ROWS)).astype(F32)
    return one(dot(expand, code.astype(BF), NN) == inner)


def slots_by_rows(code):
    expand = one(divided(iota((E, ALL), 1), ROWS) == iota((E, ALL), 0))
    row = iota((code.shape[1], ALL), 1)
    inner = (row - ROWS * divided(row, ROWS)).astype(F32)
    return one(dot(code.astype(BF), expand, TN) == inner)


def first_half(rows, width, start=0):
    row = iota((rows, width), 0) + start
    return (row - ROWS * divided(row, ROWS)) < HALF


def dispatch_kernel(ids_ref, hid_hbm, grad_hbm, out_hbm, hid_ref, grad_ref, out_ref, sems):
    loads = [
        pltpu.make_async_copy(grad_hbm, grad_ref, sems.at[0]),
        pltpu.make_async_copy(hid_hbm, hid_ref, sems.at[1]),
    ]
    for load in loads:
        load.start()
    codes = slot_codes(ids_ref)
    tokens = rows_by_slots(functools.reduce(jnp.maximum, codes))
    pick = rows_by_slots(token_major(codes))
    for load in loads:
        load.wait()
    width = grad_ref.shape[1]
    stores = []
    for start in range(0, width, 256):
        cols = slice(start, min(start + 256, width))
        size = cols.stop - start
        grad = dot(tokens, grad_ref[:, cols], NN)
        hid = dot(pick, hid_ref[:, :, cols].reshape(N * K, size), NN)
        first = 2 * ROWS * (start // 128)
        for lanes in range(0, size, 128):
            at = 2 * ROWS * ((start + lanes) // 128)
            cut = min(lanes + 128, size)
            left = grad[:, lanes:cut].reshape(E, ROWS, cut - lanes)
            right = hid[:, lanes:cut].reshape(E, ROWS, cut - lanes)
            if cut - lanes == 128:
                out_ref[:, at : at + ROWS, :] = left.astype(BF)
                out_ref[:, at + ROWS : at + 2 * ROWS, :] = right.astype(BF)
                last = at + 2 * ROWS
            else:
                tail = [
                    left[:, 0:16],
                    jnp.concatenate([left[:, 16:24], right[:, 0:8]], axis=1),
                    right[:, 8:24],
                    jnp.zeros((E, 16, 32), F32),
                ]
                out_ref[:, at : at + 16, :] = jnp.concatenate(tail, axis=2).astype(BF)
                last = at + 16
        part = pl.ds(first, last - first)
        store = pltpu.make_async_copy(
            out_ref.at[:, part, :], out_hbm.at[:, part, :], sems.at[2 + len(stores)]
        )
        store.start()
        stores.append(store)
    for store in stores:
        store.wait()


def tables_kernel(*refs):
    held, down_ref, tab_ref, back_ref = refs[:8], refs[8], refs[9], refs[10]
    for b in range(8):
        for m in range(2):
            tab_ref[m * W + b * E : m * W + (b + 1) * E, :] = held[b][m * E : (m + 1) * E, :]
    for m in range(2):
        back_ref[m * W : (m + 1) * W, :] = dot(
            tab_ref[m * W : (m + 1) * W, :], down_ref[...], NT
        ).astype(BF)


def names_kernel(me_ref, all_ref, out_ref):
    me = me_ref[0].astype(F32)
    blocks = all_ref[...].astype(F32).reshape(E, K * 8, N)
    marks = jnp.zeros((E, N), F32)
    for j in range(K):
        marks = jnp.where(blocks[:, 8 * j + 7, :] == me, 1.0, marks)
    first, second = iota((N, N), 0), iota((N, N), 1)
    earlier = one((first < second) & ((first >> 6) == (second >> 6)))
    place = dot(marks.astype(BF), earlier, NN) + (HALF * (iota((E, N), 1) >> 6)).astype(F32)
    pick = rows_by_slots(jnp.where(marks > 0.5, place, -1.0))
    for e in range(E):
        rows = slice(e * ROWS, (e + 1) * ROWS)
        block = all_ref[e * 8 * K : (e + 1) * 8 * K, :]
        out_ref[rows, :] = dot(pick[rows], block, NT).astype(BF)


def packed(x):
    x = x.reshape(E, ROWS, 32)
    parts = [x[:, 0:8], x[:, 8:16], x[:, 16:24], jnp.zeros((E, 8, 32), x.dtype)]
    return jnp.concatenate(parts, axis=2).astype(BF)


def unpacked(ref):
    x = ref[...].astype(F32)
    parts = [x[:, :, 32 * q : 32 * q + 32] for q in range(3)]
    return jnp.concatenate(parts, axis=1).reshape(ALL, 32)


def row_masks(names_ref):
    spread = one((iota((8, W), 1) >> 5) == iota((8, W), 0))
    lane = (iota((ALL, W), 1) & (E - 1)).astype(F32)
    return [dot(names_ref[:, 8 * j : 8 * j + 8], spread, NN) == lane for j in range(K)]


def section_columns(j):
    row, col = iota((W, 32), 0), iota((W, 32), 1)
    return one((row < LATER) & ((row >> 5) + 8 * j == col))


def expert_kernel(
    got_ref, down_ref, back_ref, names_ref, base_ref, out_ref, grad_ref, hid_ref
):
    inner = down_ref.shape[0]
    full = 128 * (inner // 128)
    for lanes in range(0, full, 128):
        at = 2 * ROWS * (lanes // 128)
        cols = slice(lanes, lanes + 128)
        grad_ref[:, cols] = got_ref[:, at : at + ROWS, :].reshape(ALL, 128)
        hid_ref[:, cols] = got_ref[:, at + ROWS : at + 2 * ROWS, :].reshape(ALL, 128)
    at = 2 * ROWS * (full // 128)
    tail = got_ref[:, at : at + 16, :].astype(F32)
    middle = tail[:, :, 32:64]
    grad = jnp.concatenate([tail[:, :, 0:32], middle[:, 0:8]], axis=1)
    hid = jnp.concatenate([middle[:, 8:16], tail[:, :, 64:96]], axis=1)
    grad_ref[:, full:inner] = grad.astype(BF).reshape(ALL, 32)
    hid_ref[:, full:inner] = hid.astype(BF).reshape(ALL, 32)
    total = jnp.zeros((ALL, 1), F32)
    for start in range(0, inner, 256):
        cols = slice(start, min(start + 256, inner))
        base = dot(grad_ref[...], down_ref[cols, :], NT)
        base_ref[:, cols] = base.astype(BF)
        total = total + jnp.sum(hid_ref[:, cols].astype(F32) * base, axis=1, keepdims=True)
    high, low = split(total)
    left = dot(hid_ref[...], back_ref[0:W, :], NT)
    right = dot(hid_ref[...], back_ref[W : 2 * W, :], NT)
    proj = jnp.where(first_half(ALL, W), left, right)
    chosen = jnp.zeros((ALL, 32), F32)
    for j, mask in enumerate(row_masks(names_ref)):
        kept = jnp.where(mask, proj, 0.0).astype(BF)
        chosen = chosen + dot(kept, section_columns(j), NN)
    col = iota((ALL, 32), 1)
    chosen = jnp.where(col == 7, high.astype(F32), chosen)
    chosen = jnp.where(col == 15, low.astype(F32), chosen)
    out_ref[...] = packed(chosen)


def id_masks(ids_ref):
    spread = one(divided(iota((8, W), 1), E) == iota((8, W), 0))
    lane = iota((N, W), 1) & (E - 1)
    masks = []
    for j in range(K):
        wide = dot(ids_ref[8 * j : 8 * j + 8, :].astype(BF), spread, TN)
        masks.append(wide == lane.astype(F32))
    return masks, spread


def blocks_kernel(got_ref, row_ref, gate_ref, out_ref):
    pick = slots_by_rows(jnp.concatenate(slot_codes(row_ref), axis=1))
    slots = dot(pick, unpacked(got_ref).astype(BF), NN)
    gates = [gate_ref[:, k : k + 1] for k in range(K)]
    col = iota((N, 32), 1)
    full = []
    for k in range(K):
        part = slots[k * N : (k + 1) * N]
        dots = part[:, 7:8] + part[:, 15:16]
        full.append(jnp.where(col == 7, dots, part))
    mean = sum(gates[k] * full[k] for k in range(K))
    same = one(iota((32, 32), 0) == iota((32, 32), 1))
    cells = []
    for k in range(K):
        value = gates[k] * (full[k] - mean)
        high, low = split(value[:, 7:8])
        value = jnp.where(col == 7, high.astype(F32), value)
        value = jnp.where(col == 15, low.astype(F32), value).astype(BF)
        turned = dot(same, value, NT).astype(BF)
        cells += [turned[8 * j : 8 * j + 8, :] for j in range(K)]
    block = jnp.concatenate(cells, axis=1)
    for d in range(8):
        out_ref[d] = block


def solve_kernel(at_ref, got_ref, row_ref, ids_ref, gate_ref, out_ref, coef_ref):
    at = at_ref[0]
    depth = iota((8, K * N), 0)
    found = jnp.zeros((8, K * N), F32)
    for back in range(7, -1, -1):
        where = jnp.minimum(at + back, 7)
        valid = (at + back <= 7).astype(F32)
        block = got_ref[where].astype(F32)
        fresh = []
        for k in range(K):
            part = block[:, k * K * N : (k + 1) * K * N]
            fixed = part[7:8, 0:N] + part[7:8, N : 2 * N]
            terms = jnp.sum(part * found, axis=0, keepdims=True)
            total = fixed
            for j in range(K):
                total = total + terms[:, j * N : (j + 1) * N]
            fresh.append(total * valid)
        fresh = jnp.concatenate(fresh, axis=1)
        if back:
            found = jnp.where(depth == 0, fresh, pltpu.roll(found, 1, 0))
        else:
            found = jnp.where(depth == 7, fresh, found)
    masks, spread = id_masks(ids_ref)
    high, low = split(found)
    coef = jnp.zeros((N, W), F32)
    for j in range(K):
        cut = slice(j * N, (j + 1) * N)
        wide = dot(high[:, cut], spread, TN) + dot(low[:, cut], spread, TN)
        coef = jnp.where(masks[j], wide, coef)
    coef_ref[...] = coef.astype(BF)
    same = one(iota((32, 32), 0) == iota((32, 32), 1))
    tall_high = jnp.concatenate([high[:, j * N : (j + 1) * N] for j in range(K)], axis=0)
    tall_low = jnp.concatenate([low[:, j * N : (j + 1) * N] for j in range(K)], axis=0)
    short = dot(tall_high, same, TN) + dot(tall_low, same, TN)
    col = iota((N, 32), 1)
    rows = []
    for k in range(K):
        gate = gate_ref[:, k : k + 1]
        up, rest = split(gate)
        value = jnp.where(col == 7, up.astype(F32), gate * short)
        rows.append(jnp.where(col == 15, rest.astype(F32), value).astype(BF))
    pick = rows_by_slots(jnp.concatenate(slot_codes(row_ref), axis=1))
    out_ref[...] = packed(dot(pick, jnp.concatenate(rows, axis=0), NN))


def passed_kernel(coef_ref, tab_ref, grad_ref, acts_ref, pass_ref, part_ref):
    for m in range(2):
        rows = slice(m * T, (m + 1) * T)
        moved = dot(coef_ref[rows, :], tab_ref[m * W : (m + 1) * W, :], NN)
        pass_ref[rows, :] = (grad_ref[rows, :].astype(F32) + moved).astype(BF)
    own = coef_ref[:, LATER:W]
    width = acts_ref.shape[1]
    router = (dot(acts_ref[...], own, TN) / T).astype(BF)
    each = width // E
    row, col = iota((ALL, width), 0), iota((ALL, width), 1)
    peer = divided(row, ROWS)
    inner = row - ROWS * peer
    source = peer * each + inner
    first = dot(one(source == col), router, NN)
    second = dot(one((source + ROWS == col) & (inner + ROWS < each)), router, NN)
    part_ref[:, 0:E] = first.astype(BF)
    part_ref[:, E : 2 * E] = second.astype(BF)


def answer_kernel(got_ref, base_ref, back_ref, part_ref, names_ref, out_ref):
    width = base_ref.shape[1]
    got = unpacked(got_ref)
    gate = got[:, 7:8] + got[:, 15:16]
    coef = jnp.zeros((ALL, W), F32)
    for j, mask in enumerate(row_masks(names_ref)):
        coef = jnp.where(mask, coef + dot(got.astype(BF), section_columns(j), NT), coef)
    half = first_half(ALL, W)
    left = jnp.where(half, coef, 0.0).astype(BF)
    right = jnp.where(half, 0.0, coef).astype(BF)
    for start in range(0, width, 256):
        cols = slice(start, min(start + 256, width))
        moved = dot(left, back_ref[0:W, cols], NN) + dot(right, back_ref[W : 2 * W, cols], NN)
        out_ref[:, cols] = (gate * base_ref[:, cols].astype(F32) + moved).astype(BF)
    out_ref[:, width : width + 2 * E] = part_ref[...]
    out_ref[:, width + 2 * E :] = jnp.zeros((ALL, out_ref.shape[1] - width - 2 * E), BF)


def combine_kernel(got_ref, ids_ref, out_ref, router_ref):
    pick = slots_by_rows(token_major(slot_codes(ids_ref)))
    width = out_ref.shape[2]
    for start in range(0, width, 256):
        cols = slice(start, min(start + 256, width))
        own = dot(pick, got_ref[:, cols], NN).astype(BF)
        out_ref[:, :, cols] = own.reshape(N, K, cols.stop - start)
    parts = got_ref[:, width : width + 2 * E].astype(F32).reshape(E, ROWS, 2 * E)
    total = jnp.sum(parts, axis=0)
    each = width // E
    turn = iota((E, 2 * E), 1) - iota((E, 2 * E), 0)
    flipped = [jnp.zeros((E, ROWS), F32)] * 2
    for _ in range(3):
        piece = total.astype(BF)
        total = total - piece.astype(F32)
        flipped = [flipped[q] + dot(one(turn == q * E), piece, NT) for q in range(2)]
    router_ref[:, 0:ROWS] = flipped[0]
    router_ref[:, ROWS:each] = flipped[1][:, 0 : each - ROWS]


def call(body, shapes, args, mib, smem=0, scratch=(), sems=0, far=(), far_out=()):
    ins = [SM] * smem + [VM] * (len(args) - smem)
    ins = [HB if i in far else spec for i, spec in enumerate(ins)]
    held = [pltpu.VMEM(s, d) for s, d in scratch]
    if sems:
        held.append(pltpu.SemaphoreType.DMA((sems,)))
    return pl.pallas_call(
        body,
        out_shape=[jax.ShapeDtypeStruct(s, d) for s, d in shapes],
        in_specs=ins,
        out_specs=[HB if i in far_out else VM for i in range(len(shapes))],
        scratch_shapes=held,
        compiler_params=pltpu.CompilerParams(vmem_limit_bytes=mib << 20),
    )(*args)


def exchange(x, axis):
    return lax.all_to_all(x, axis, split_axis=0, concat_axis=0, tiled=True)


def on_device(acts, hidden, ids, version, router, down, grad_top):
    pipe = lax.axis_size("pipe")
    section = lax.axis_index("pipe")
    width = acts.shape[-1]
    inner = hidden.shape[-1]
    inputs = acts[0]
    routes = ids[0]
    mats = down[0, 0]
    grads = grad_top.reshape(N, width)
    turned = routes.transpose(0, 2, 1)
    tall = 2 * ROWS * (inner // 128) + 16

    steps = pl.cdiv(inner, 256)

    (sent,) = call(
        dispatch_kernel,
        [((E, tall, 128), BF)],
        (turned, hidden[0].reshape(N, K, inner), grads),
        MIBS[0],
        scratch=[((N, K, inner), BF), ((N, width), BF), ((E, tall, 128), BF)],
        sems=2 + steps,
        far=(1, 2),
        far_out=(0,),
    )
    arrived = exchange(sent, "expert")

    picked_version = version[0][:, None, None] == 1
    tables = jnp.where(picked_version, router[0, 1][None], router[0, 0][None])
    flipped = tables.transpose(0, 2, 1).reshape(2 * E, width)
    id_rows = jnp.pad(
        turned.transpose(1, 0, 2).reshape(K, N).astype(BF), ((0, 8 - K), (0, width - N))
    )
    own = jnp.concatenate([flipped, id_rows], axis=0)
    held = [
        lax.ppermute(own, "pipe", [(i, i - by) for i in range(by, pipe)]) for by in range(1, pipe)
    ] + [own]
    near = jnp.stack([h[2 * E : 2 * E + K, 0:N] for h in held], axis=1).reshape(K * 8, N)
    id_all = near.astype(F32)
    place = lax.axis_index("expert")
    for bit in range(5):
        other = lax.ppermute(near, "expert", [(i, i ^ (1 << bit)) for i in range(E)])
        upper = ((place >> bit) & 1) == 1
        near = jnp.where(
            upper,
            jnp.concatenate([other, near], axis=0),
            jnp.concatenate([near, other], axis=0),
        )
    (names,) = call(names_kernel, [((ALL, K * 8), BF)], (place.reshape(1), near), 12, smem=1)
    table_rows, back = call(
        tables_kernel,
        [((2 * W, width), BF), ((2 * W, inner), BF)],
        (*held, mats),
        MIBS[1],
    )

    logits = jnp.einsum("mtd,mde->mte", inputs, tables, preferred_element_type=F32)
    labels = jnp.arange(E, dtype=I32)
    picked = routes[:, :, :, None] == labels
    chosen = jnp.sum(jnp.where(picked, logits[:, :, None, :], 0.0), axis=3)
    scores = jnp.exp(chosen)
    gating = (scores / jnp.sum(scores, axis=2, keepdims=True)).reshape(N, K)

    base, proj = call(
        expert_kernel,
        [((ALL, inner), BF), ((E, 8, 128), BF)],
        (arrived, mats, back, names),
        MIBS[2],
        scratch=[((ALL, width), BF), ((ALL, inner), BF)],
    )
    rest = (gating, turned, id_all, section.reshape(1), grads, inputs, table_rows, back, base, names)
    proj, rest = lax.optimization_barrier((proj, rest))
    returned = exchange(proj, "expert")
    returned, rest = lax.optimization_barrier((returned, rest))
    gating, turned, id_all, where, grads, inputs, table_rows, back, base, names = rest
    (blocks,) = call(
        blocks_kernel,
        [((8, 8, K * K * N), BF)],
        (returned, turned, gating),
        MIBS[3],
    )
    blocks, rest = lax.optimization_barrier((blocks, rest))
    gathered = exchange(blocks, "pipe")
    gathered, rest = lax.optimization_barrier((gathered, rest))
    gating, turned, id_all, where, grads, inputs, table_rows, back, base, names = rest
    coef_sent, coef = call(
        solve_kernel,
        [((E, 8, 128), BF), ((N, W), BF)],
        (where, gathered, turned, id_all, gating),
        MIBS[4],
        smem=1,
    )
    coef_sent, coef, rest = lax.optimization_barrier((coef_sent, coef, rest))
    coef_got = exchange(coef_sent, "expert")
    coef_got, coef, rest = lax.optimization_barrier((coef_got, coef, rest))
    gating, turned, id_all, where, grads, inputs, table_rows, back, base, names = rest
    passed, parts = call(
        passed_kernel,
        [((N, width), BF), ((ALL, 2 * E), BF)],
        (coef, table_rows, grads, inputs.reshape(N, width)),
        MIBS[5],
    )
    wide = 256 * steps
    (answer,) = call(
        answer_kernel, [((ALL, wide), BF)], (coef_got, base, back, parts, names), MIBS[6]
    )
    answered = exchange(answer.reshape(E, ROWS, wide), "expert").reshape(ALL, wide)
    hidden_grads, grad_router = call(
        combine_kernel, [((N, K, inner), BF), ((E, width // E), F32)], (answered, turned), MIBS[7]
    )
    return (
        passed.reshape(1, 2, T, width),
        hidden_grads.reshape(1, 2, T, K, inner),
        grad_router.T[None],
    )


def solution(mesh):
    placed = (
        P("pipe", None, "expert", None),
        P("pipe", None, "expert", None, None),
        P("pipe", None, "expert", None),
        P("pipe", None),
        P("pipe", None, None, None),
        P("pipe", "expert", None, None),
        P(None, "expert", None),
    )
    return jax.shard_map(
        on_device,
        mesh=mesh,
        in_specs=placed,
        out_specs=(
            P("pipe", None, "expert", None),
            P("pipe", None, "expert", None, None),
            P("pipe", "expert", None),
        ),
        check_vma=False,
    )
```

```python
import functools

import jax
import jax.numpy as jnp
from jax import lax
from jax.experimental import pallas as pl
from jax.experimental.pallas import tpu as pltpu
from jax.sharding import PartitionSpec as P

BF = jnp.bfloat16
F32 = jnp.float32
I32 = jnp.int32
NN = (((1,), (0,)), ((), ()))
NT = (((1,), (1,)), ((), ()))
TN = (((0,), (0,)), ((), ()))
VM = pl.BlockSpec(memory_space=pltpu.VMEM)
HB = pl.BlockSpec(memory_space=pltpu.HBM)
SM = pl.BlockSpec(memory_space=pltpu.SMEM)

N, T, K, E, HALF = 128, 64, 4, 32, 12
ROWS = 2 * HALF
ALL = E * ROWS
W = 256
MIBS = (62, 20, 24, 12, 12, 16, 16, 20)
LATER = 224


def dot(a, b, dims):
    return lax.dot_general(a, b, dims, preferred_element_type=F32)


def iota(shape, dim):
    return lax.broadcasted_iota(I32, shape, dim)


def one(mask):
    return jnp.where(mask, 1.0, 0.0).astype(BF)


def divided(x, by):
    return ((x.astype(F32) + 0.5) * (1.0 / by)).astype(I32)


def split(x):
    high = x.astype(BF)
    return high, (x - high.astype(F32)).astype(BF)


def slot_codes(ids_ref):
    named = []
    for k in range(K):
        row = jnp.concatenate([ids_ref[0, k : k + 1, :], ids_ref[1, k : k + 1, :]], axis=1)
        named.append(row == iota((E, N), 0))
    marks = sum(jnp.where(hit, 1.0, 0.0) for hit in named).astype(BF)
    first, second = iota((N, N), 0), iota((N, N), 1)
    earlier = one((first < second) & ((first >> 6) == (second >> 6)))
    place = dot(marks, earlier, NN) + (HALF * (iota((E, N), 1) >> 6)).astype(F32)
    return [jnp.where(hit, place, -1.0) for hit in named]


def token_major(codes):
    lane = iota((N, N * K), 1)
    spread = one((lane >> 2) == iota((N, N * K), 0))
    which = iota((E, N * K), 1) & (K - 1)
    out = jnp.zeros((E, N * K), F32)
    for k in range(K):
        out = jnp.where(which == k, dot(codes[k].astype(BF), spread, NN), out)
    return out


def rows_by_slots(code):
    expand = one(divided(iota((ALL, E), 0), ROWS) == iota((ALL, E), 1))
    row = iota((ALL, code.shape[1]), 0)
    inner = (row - ROWS * divided(row, ROWS)).astype(F32)
    return one(dot(expand, code.astype(BF), NN) == inner)


def slots_by_rows(code):
    expand = one(divided(iota((E, ALL), 1), ROWS) == iota((E, ALL), 0))
    row = iota((code.shape[1], ALL), 1)
    inner = (row - ROWS * divided(row, ROWS)).astype(F32)
    return one(dot(code.astype(BF), expand, TN) == inner)


def first_half(rows, width, start=0):
    row = iota((rows, width), 0) + start
    return (row - ROWS * divided(row, ROWS)) < HALF


def dispatch_kernel(ids_ref, hid_hbm, grad_hbm, out_hbm, hid_ref, grad_ref, out_ref, sems):
    loads = [
        pltpu.make_async_copy(grad_hbm, grad_ref, sems.at[0]),
        pltpu.make_async_copy(hid_hbm, hid_ref, sems.at[1]),
    ]
    for load in loads:
        load.start()
    codes = slot_codes(ids_ref)
    tokens = rows_by_slots(functools.reduce(jnp.maximum, codes))
    pick = rows_by_slots(token_major(codes))
    for load in loads:
        load.wait()
    width = grad_ref.shape[1]
    stores = []
    for start in range(0, width, 256):
        cols = slice(start, min(start + 256, width))
        size = cols.stop - start
        grad = dot(tokens, grad_ref[:, cols], NN)
        hid = dot(pick, hid_ref[:, :, cols].reshape(N * K, size), NN)
        first = 2 * ROWS * (start // 128)
        for lanes in range(0, size, 128):
            at = 2 * ROWS * ((start + lanes) // 128)
            cut = min(lanes + 128, size)
            left = grad[:, lanes:cut].reshape(E, ROWS, cut - lanes)
            right = hid[:, lanes:cut].reshape(E, ROWS, cut - lanes)
            if cut - lanes == 128:
                out_ref[:, at : at + ROWS, :] = left.astype(BF)
                out_ref[:, at + ROWS : at + 2 * ROWS, :] = right.astype(BF)
                last = at + 2 * ROWS
            else:
                tail = [
                    left[:, 0:16],
                    jnp.concatenate([left[:, 16:24], right[:, 0:8]], axis=1),
                    right[:, 8:24],
                    jnp.zeros((E, 16, 32), F32),
                ]
                out_ref[:, at : at + 16, :] = jnp.concatenate(tail, axis=2).astype(BF)
                last = at + 16
        part = pl.ds(first, last - first)
        store = pltpu.make_async_copy(
            out_ref.at[:, part, :], out_hbm.at[:, part, :], sems.at[2 + len(stores)]
        )
        store.start()
        stores.append(store)
    for store in stores:
        store.wait()


def tables_kernel(*refs):
    held, down_ref, tab_ref, back_ref, ids_ref = refs[:8], refs[8], refs[9], refs[10], refs[11]
    for b in range(8):
        for m in range(2):
            tab_ref[m * W + b * E : m * W + (b + 1) * E, :] = held[b][m * E : (m + 1) * E, :]
    rows = jnp.concatenate([held[b][2 * E : 2 * E + 8, 0:N].astype(F32) for b in range(8)], axis=0)
    for j in range(K):
        for b in range(8):
            ids_ref[8 * j + b : 8 * j + b + 1, :] = rows[8 * b + j : 8 * b + j + 1, :]
    for m in range(2):
        back_ref[m * W : (m + 1) * W, :] = dot(
            tab_ref[m * W : (m + 1) * W, :], down_ref[...], NT
        ).astype(BF)


def expert_kernel(got_ref, down_ref, back_ref, base_ref, out_ref, grad_ref, hid_ref):
    inner = down_ref.shape[0]
    full = 128 * (inner // 128)
    for lanes in range(0, full, 128):
        at = 2 * ROWS * (lanes // 128)
        cols = slice(lanes, lanes + 128)
        grad_ref[:, cols] = got_ref[:, at : at + ROWS, :].reshape(ALL, 128)
        hid_ref[:, cols] = got_ref[:, at + ROWS : at + 2 * ROWS, :].reshape(ALL, 128)
    at = 2 * ROWS * (full // 128)
    tail = got_ref[:, at : at + 16, :].astype(F32)
    middle = tail[:, :, 32:64]
    grad = jnp.concatenate([tail[:, :, 0:32], middle[:, 0:8]], axis=1)
    hid = jnp.concatenate([middle[:, 8:16], tail[:, :, 64:96]], axis=1)
    grad_ref[:, full:inner] = grad.astype(BF).reshape(ALL, 32)
    hid_ref[:, full:inner] = hid.astype(BF).reshape(ALL, 32)
    total = jnp.zeros((ALL, 1), F32)
    for start in range(0, inner, 256):
        cols = slice(start, min(start + 256, inner))
        base = dot(grad_ref[...], down_ref[cols, :], NT)
        base_ref[:, cols] = base.astype(BF)
        total = total + jnp.sum(hid_ref[:, cols].astype(F32) * base, axis=1, keepdims=True)
    high, low = split(total)
    left = dot(hid_ref[...], back_ref[0:W, :], NT)
    right = dot(hid_ref[...], back_ref[W : 2 * W, :], NT)
    proj = jnp.where(first_half(ALL, W), left, right)
    lane = iota((ALL, W), 1)
    tail = jnp.where(lane == LATER, high.astype(F32), low.astype(F32))
    tail = jnp.where(lane < LATER + 2, tail, 0.0)
    out_ref[...] = jnp.where(lane < LATER, proj, tail).astype(BF)


def id_masks(ids_ref):
    spread = one(divided(iota((8, W), 1), E) == iota((8, W), 0))
    lane = iota((N, W), 1) & (E - 1)
    masks = []
    for j in range(K):
        wide = dot(ids_ref[8 * j : 8 * j + 8, :].astype(BF), spread, TN)
        masks.append(wide == lane.astype(F32))
    return masks, spread


def blocks_kernel(got_ref, row_ref, ids_ref, gate_ref, out_ref):
    pick = slots_by_rows(jnp.concatenate(slot_codes(row_ref), axis=1))
    slots = dot(pick, got_ref[...], NN)
    gates = [gate_ref[:, k : k + 1] for k in range(K)]
    parts = [slots[k * N : (k + 1) * N] for k in range(K)]
    lane = iota((N, W), 1)
    full = []
    for part in parts:
        dots = part[:, LATER : LATER + 1] + part[:, LATER + 1 : LATER + 2]
        full.append(jnp.where(lane < LATER, part, dots))
    mean = sum(gates[k] * full[k] for k in range(K))
    masks, spread = id_masks(ids_ref)
    rows = []
    for k in range(K):
        value = gates[k] * (full[k] - mean)
        high, low = split(value)
        for j in range(K):
            source = jnp.where(masks[j] & (lane < LATER), high.astype(F32), 0.0)
            if j < 2:
                extra = high if j == 0 else low
                source = jnp.where(lane == LATER, extra.astype(F32), source)
            rows.append(source.astype(BF))
    packed = dot(spread, jnp.concatenate(rows, axis=0), NT).astype(BF)
    for d in range(8):
        out_ref[d] = packed


def solve_kernel(at_ref, got_ref, row_ref, ids_ref, gate_ref, out_ref, coef_ref):
    at = at_ref[0]
    depth = iota((8, K * N), 0)
    found = jnp.zeros((8, K * N), F32)
    for back in range(7, -1, -1):
        where = jnp.minimum(at + back, 7)
        valid = (at + back <= 7).astype(F32)
        block = got_ref[where].astype(F32)
        fresh = []
        for k in range(K):
            part = block[:, k * K * N : (k + 1) * K * N]
            fixed = part[7:8, 0:N] + part[7:8, N : 2 * N]
            terms = jnp.sum(part * found, axis=0, keepdims=True)
            total = fixed
            for j in range(K):
                total = total + terms[:, j * N : (j + 1) * N]
            fresh.append(total * valid)
        fresh = jnp.concatenate(fresh, axis=1)
        if back:
            found = jnp.where(depth == 0, fresh, pltpu.roll(found, 1, 0))
        else:
            found = jnp.where(depth == 7, fresh, found)
    masks, spread = id_masks(ids_ref)
    high, low = split(found)
    coef = jnp.zeros((N, W), F32)
    for j in range(K):
        cut = slice(j * N, (j + 1) * N)
        wide = dot(high[:, cut], spread, TN) + dot(low[:, cut], spread, TN)
        coef = jnp.where(masks[j], wide, coef)
    coef_ref[...] = coef.astype(BF)
    same = one(iota((32, 32), 0) == iota((32, 32), 1))
    tall_high = jnp.concatenate([high[:, j * N : (j + 1) * N] for j in range(K)], axis=0)
    tall_low = jnp.concatenate([low[:, j * N : (j + 1) * N] for j in range(K)], axis=0)
    short = dot(tall_high, same, TN) + dot(tall_low, same, TN)
    names = dot(ids_ref[...].astype(BF), same, TN)
    col = iota((N, 32), 1)
    rows = []
    for k in range(K):
        gate = gate_ref[:, k : k + 1]
        up, rest = split(gate)
        value = jnp.where(col == 7, up.astype(F32), gate * short)
        value = jnp.where(col == 15, rest.astype(F32), value)
        rows.append(jnp.concatenate([value, names], axis=1).astype(BF))
    pick = rows_by_slots(jnp.concatenate(slot_codes(row_ref), axis=1))
    sent = dot(pick, jnp.concatenate(rows, axis=0), NN).reshape(E, ROWS, 64)
    out_ref[:, :, 0:64] = sent[:, 0:16].astype(BF)
    rest = jnp.concatenate([sent[:, 16:24], jnp.zeros((E, 8, 64), F32)], axis=1)
    out_ref[:, :, 64:128] = rest.astype(BF)


def passed_kernel(coef_ref, tab_ref, grad_ref, acts_ref, pass_ref, part_ref):
    for m in range(2):
        rows = slice(m * T, (m + 1) * T)
        moved = dot(coef_ref[rows, :], tab_ref[m * W : (m + 1) * W, :], NN)
        pass_ref[rows, :] = (grad_ref[rows, :].astype(F32) + moved).astype(BF)
    own = coef_ref[:, LATER:W]
    width = acts_ref.shape[1]
    router = (dot(acts_ref[...], own, TN) / T).astype(BF)
    each = width // E
    ahead = jnp.concatenate([router[ROWS:], router[:ROWS]], axis=0)
    col = iota((ALL, width), 1)
    peer = divided(iota((ALL, 1), 0), ROWS)
    source = iota((ALL, 1), 0) + (each - ROWS) * peer
    select = one(source == col)
    part_ref[:, 0:E] = dot(select, router, NN).astype(BF)
    part_ref[:, E : 2 * E] = dot(select, ahead, NN).astype(BF)


def section_columns(j):
    row, col = iota((W, 32), 0), iota((W, 32), 1)
    return one((row < LATER) & ((row >> 5) + 8 * j == col))


def answer_kernel(got_ref, base_ref, back_ref, part_ref, out_ref):
    width = base_ref.shape[1]
    got = got_ref[...].astype(F32)
    got = jnp.concatenate([got[:, :, 0:64], got[:, 0:8, 64:128]], axis=1).reshape(ALL, 64)
    gate = got[:, 7:8] + got[:, 15:16]
    got = got.astype(BF)
    spread = one((iota((8, W), 1) >> 5) == iota((8, W), 0))
    lane = (iota((ALL, W), 1) & (E - 1)).astype(F32)
    coef = jnp.zeros((ALL, W), F32)
    for j in range(K):
        named = dot(got[:, 32 + 8 * j : 40 + 8 * j], spread, NN) == lane
        coef = jnp.where(named, coef + dot(got[:, 0:32], section_columns(j), NT), coef)
    half = first_half(ALL, W)
    left = jnp.where(half, coef, 0.0).astype(BF)
    right = jnp.where(half, 0.0, coef).astype(BF)
    for start in range(0, width, 256):
        cols = slice(start, min(start + 256, width))
        moved = dot(left, back_ref[0:W, cols], NN) + dot(right, back_ref[W : 2 * W, cols], NN)
        out_ref[:, cols] = (gate * base_ref[:, cols].astype(F32) + moved).astype(BF)
    out_ref[:, width : width + 2 * E] = part_ref[...]
    out_ref[:, width + 2 * E :] = jnp.zeros((ALL, out_ref.shape[1] - width - 2 * E), BF)


def combine_kernel(got_ref, ids_ref, out_ref, router_ref):
    pick = slots_by_rows(token_major(slot_codes(ids_ref)))
    width = out_ref.shape[2]
    for start in range(0, width, 256):
        cols = slice(start, min(start + 256, width))
        own = dot(pick, got_ref[:, cols], NN).astype(BF)
        out_ref[:, :, cols] = own.reshape(N, K, cols.stop - start)
    parts = got_ref[:, width : width + 2 * E].astype(F32).reshape(E, ROWS, 2 * E)
    total = jnp.sum(parts, axis=0)
    each = width // E
    turn = iota((E, 2 * E), 1) - iota((E, 2 * E), 0)
    flipped = [jnp.zeros((E, ROWS), F32)] * 2
    for _ in range(3):
        piece = total.astype(BF)
        total = total - piece.astype(F32)
        flipped = [flipped[q] + dot(one(turn == q * E), piece, NT) for q in range(2)]
    router_ref[:, 0:ROWS] = flipped[0]
    router_ref[:, ROWS:each] = flipped[1][:, 0 : each - ROWS]


def call(body, shapes, args, mib, smem=0, scratch=(), sems=0, far=(), far_out=()):
    ins = [SM] * smem + [VM] * (len(args) - smem)
    ins = [HB if i in far else spec for i, spec in enumerate(ins)]
    held = [pltpu.VMEM(s, d) for s, d in scratch]
    if sems:
        held.append(pltpu.SemaphoreType.DMA((sems,)))
    return pl.pallas_call(
        body,
        out_shape=[jax.ShapeDtypeStruct(s, d) for s, d in shapes],
        in_specs=ins,
        out_specs=[HB if i in far_out else VM for i in range(len(shapes))],
        scratch_shapes=held,
        compiler_params=pltpu.CompilerParams(vmem_limit_bytes=mib << 20),
    )(*args)


def exchange(x, axis):
    return lax.all_to_all(x, axis, split_axis=0, concat_axis=0, tiled=True)


def on_device(acts, hidden, ids, version, router, down, grad_top):
    pipe = lax.axis_size("pipe")
    section = lax.axis_index("pipe")
    width = acts.shape[-1]
    inner = hidden.shape[-1]
    inputs = acts[0]
    routes = ids[0]
    mats = down[0, 0]
    grads = grad_top.reshape(N, width)
    turned = routes.transpose(0, 2, 1)
    tall = 2 * ROWS * (inner // 128) + 16

    steps = pl.cdiv(inner, 256)

    (sent,) = call(
        dispatch_kernel,
        [((E, tall, 128), BF)],
        (turned, hidden[0].reshape(N, K, inner), grads),
        MIBS[0],
        scratch=[((N, K, inner), BF), ((N, width), BF), ((E, tall, 128), BF)],
        sems=2 + steps,
        far=(1, 2),
        far_out=(0,),
    )
    arrived = exchange(sent, "expert")

    picked_version = version[0][:, None, None] == 1
    tables = jnp.where(picked_version, router[0, 1][None], router[0, 0][None])
    flipped = tables.transpose(0, 2, 1).reshape(2 * E, width)
    id_rows = jnp.pad(
        turned.transpose(1, 0, 2).reshape(K, N).astype(BF), ((0, 8 - K), (0, width - N))
    )
    own = jnp.concatenate([flipped, id_rows], axis=0)
    held = [
        lax.ppermute(own, "pipe", [(i, i - by) for i in range(by, pipe)]) for by in range(1, pipe)
    ] + [own]
    table_rows, back, id_all = call(
        tables_kernel,
        [((2 * W, width), BF), ((2 * W, inner), BF), ((K * 8, N), F32)],
        (*held, mats),
        MIBS[1],
    )

    logits = jnp.einsum("mtd,mde->mte", inputs, tables, preferred_element_type=F32)
    labels = jnp.arange(E, dtype=I32)
    picked = routes[:, :, :, None] == labels
    chosen = jnp.sum(jnp.where(picked, logits[:, :, None, :], 0.0), axis=3)
    scores = jnp.exp(chosen)
    gating = (scores / jnp.sum(scores, axis=2, keepdims=True)).reshape(N, K)

    base, proj = call(
        expert_kernel,
        [((ALL, inner), BF), ((ALL, W), BF)],
        (arrived, mats, back),
        MIBS[2],
        scratch=[((ALL, width), BF), ((ALL, inner), BF)],
    )
    rest = (gating, turned, id_all, section.reshape(1), grads, inputs, table_rows, back, base)
    proj, rest = lax.optimization_barrier((proj, rest))
    returned = exchange(proj.reshape(E, ROWS, W), "expert").reshape(ALL, W)
    returned, rest = lax.optimization_barrier((returned, rest))
    gating, turned, id_all, where, grads, inputs, table_rows, back, base = rest
    (blocks,) = call(
        blocks_kernel,
        [((8, 8, K * K * N), BF)],
        (returned, turned, id_all, gating),
        MIBS[3],
    )
    blocks, rest = lax.optimization_barrier((blocks, rest))
    gathered = exchange(blocks, "pipe")
    gathered, rest = lax.optimization_barrier((gathered, rest))
    gating, turned, id_all, where, grads, inputs, table_rows, back, base = rest
    coef_sent, coef = call(
        solve_kernel,
        [((E, 16, 128), BF), ((N, W), BF)],
        (where, gathered, turned, id_all, gating),
        MIBS[4],
        smem=1,
    )
    coef_sent, coef, rest = lax.optimization_barrier((coef_sent, coef, rest))
    coef_got = exchange(coef_sent, "expert")
    coef_got, coef, rest = lax.optimization_barrier((coef_got, coef, rest))
    gating, turned, id_all, where, grads, inputs, table_rows, back, base = rest
    passed, parts = call(
        passed_kernel,
        [((N, width), BF), ((ALL, 2 * E), BF)],
        (coef, table_rows, grads, inputs.reshape(N, width)),
        MIBS[5],
    )
    wide = 256 * steps
    (answer,) = call(
        answer_kernel, [((ALL, wide), BF)], (coef_got, base, back, parts), MIBS[6]
    )
    answered = exchange(answer.reshape(E, ROWS, wide), "expert").reshape(ALL, wide)
    hidden_grads, grad_router = call(
        combine_kernel, [((N, K, inner), BF), ((E, width // E), F32)], (answered, turned), MIBS[7]
    )
    return (
        passed.reshape(1, 2, T, width),
        hidden_grads.reshape(1, 2, T, K, inner),
        grad_router.T[None],
    )


def solution(mesh):
    placed = (
        P("pipe", None, "expert", None),
        P("pipe", None, "expert", None, None),
        P("pipe", None, "expert", None),
        P("pipe", None),
        P("pipe", None, None, None),
        P("pipe", "expert", None, None),
        P(None, "expert", None),
    )
    return jax.shard_map(
        on_device,
        mesh=mesh,
        in_specs=placed,
        out_specs=(
            P("pipe", None, "expert", None),
            P("pipe", None, "expert", None, None),
            P("pipe", "expert", None),
        ),
        check_vma=False,
    )
```

```python
import functools

import jax
import jax.numpy as jnp
from jax import lax
from jax.experimental import pallas as pl
from jax.experimental.pallas import tpu as pltpu
from jax.sharding import PartitionSpec as P

BF = jnp.bfloat16
F32 = jnp.float32
I32 = jnp.int32
NN = (((1,), (0,)), ((), ()))
NT = (((1,), (1,)), ((), ()))
TN = (((0,), (0,)), ((), ()))
VM = pl.BlockSpec(memory_space=pltpu.VMEM)
HB = pl.BlockSpec(memory_space=pltpu.HBM)
SM = pl.BlockSpec(memory_space=pltpu.SMEM)

N, T, K, E, HALF = 128, 64, 4, 32, 12
ROWS = 2 * HALF
ALL = E * ROWS
W = 256
MIBS = (62, 20, 60, 12, 12, 16, 16, 20)
LATER = 224


def dot(a, b, dims):
    return lax.dot_general(a, b, dims, preferred_element_type=F32)


def iota(shape, dim):
    return lax.broadcasted_iota(I32, shape, dim)


def one(mask):
    return jnp.where(mask, 1.0, 0.0).astype(BF)


def divided(x, by):
    return ((x.astype(F32) + 0.5) * (1.0 / by)).astype(I32)


def split(x):
    high = x.astype(BF)
    return high, (x - high.astype(F32)).astype(BF)


def slot_codes(ids_ref):
    named = []
    for k in range(K):
        row = jnp.concatenate([ids_ref[0, k : k + 1, :], ids_ref[1, k : k + 1, :]], axis=1)
        named.append(row == iota((E, N), 0))
    marks = sum(jnp.where(hit, 1.0, 0.0) for hit in named).astype(BF)
    first, second = iota((N, N), 0), iota((N, N), 1)
    earlier = one((first < second) & ((first >> 6) == (second >> 6)))
    place = dot(marks, earlier, NN) + (HALF * (iota((E, N), 1) >> 6)).astype(F32)
    return [jnp.where(hit, place, -1.0) for hit in named]


def token_major(codes):
    lane = iota((N, N * K), 1)
    spread = one((lane >> 2) == iota((N, N * K), 0))
    which = iota((E, N * K), 1) & (K - 1)
    out = jnp.zeros((E, N * K), F32)
    for k in range(K):
        out = jnp.where(which == k, dot(codes[k].astype(BF), spread, NN), out)
    return out


def rows_by_slots(code):
    expand = one(divided(iota((ALL, E), 0), ROWS) == iota((ALL, E), 1))
    row = iota((ALL, code.shape[1]), 0)
    inner = (row - ROWS * divided(row, ROWS)).astype(F32)
    return one(dot(expand, code.astype(BF), NN) == inner)


def slots_by_rows(code):
    expand = one(divided(iota((E, ALL), 1), ROWS) == iota((E, ALL), 0))
    row = iota((code.shape[1], ALL), 1)
    inner = (row - ROWS * divided(row, ROWS)).astype(F32)
    return one(dot(code.astype(BF), expand, TN) == inner)


def first_half(rows, width, start=0):
    row = iota((rows, width), 0) + start
    return (row - ROWS * divided(row, ROWS)) < HALF


def dispatch_kernel(ids_ref, hid_hbm, grad_hbm, out_hbm, hid_ref, grad_ref, out_ref, sems):
    loads = [
        pltpu.make_async_copy(grad_hbm, grad_ref, sems.at[0]),
        pltpu.make_async_copy(hid_hbm, hid_ref, sems.at[1]),
    ]
    for load in loads:
        load.start()
    codes = slot_codes(ids_ref)
    tokens = rows_by_slots(functools.reduce(jnp.maximum, codes))
    width = grad_ref.shape[1]
    full = 128 * (width // 128)
    last = 2 * ROWS * (full // 128)
    loads[0].wait()
    tail = None
    for start in range(0, width, 256):
        cols = slice(start, min(start + 256, width))
        grad = dot(tokens, grad_ref[:, cols], NN)
        for lanes in range(start, min(cols.stop, full), 128):
            tile = grad[:, lanes - start : lanes - start + 128].reshape(E, ROWS, 128)
            at = 2 * ROWS * (lanes // 128)
            out_ref[:, at : at + ROWS, :] = tile.astype(BF)
        if cols.stop > full:
            tail = grad[:, full - start :].reshape(E, ROWS, width - full)
    pick = rows_by_slots(token_major(codes))
    loads[1].wait()
    stores = []
    for start in range(0, width, 256):
        cols = slice(start, min(start + 256, width))
        size = cols.stop - start
        hid = dot(pick, hid_ref[:, :, cols].reshape(N * K, size), NN)
        for lanes in range(start, min(cols.stop, full), 128):
            tile = hid[:, lanes - start : lanes - start + 128].reshape(E, ROWS, 128)
            at = 2 * ROWS * (lanes // 128) + ROWS
            out_ref[:, at : at + ROWS, :] = tile.astype(BF)
        first = 2 * ROWS * (start // 128)
        stop = min(first + 4 * ROWS, last)
        if cols.stop > full:
            right = hid[:, full - start :].reshape(E, ROWS, width - full)
            parts = [
                tail[:, 0:16],
                jnp.concatenate([tail[:, 16:24], right[:, 0:8]], axis=1),
                right[:, 8:24],
                jnp.zeros((E, 16, 32), F32),
            ]
            out_ref[:, last : last + 16, :] = jnp.concatenate(parts, axis=2).astype(BF)
            stop = last + 16
        part = pl.ds(first, stop - first)
        store = pltpu.make_async_copy(
            out_ref.at[:, part, :], out_hbm.at[:, part, :], sems.at[2 + len(stores)]
        )
        store.start()
        stores.append(store)
    for store in stores:
        store.wait()


def tables_kernel(*refs):
    held, down_ref, tab_ref, back_ref, ids_ref = refs[:8], refs[8], refs[9], refs[10], refs[11]
    for b in range(8):
        for m in range(2):
            tab_ref[m * W + b * E : m * W + (b + 1) * E, :] = held[b][m * E : (m + 1) * E, :]
    rows = jnp.concatenate([held[b][2 * E : 2 * E + 8, 0:N].astype(F32) for b in range(8)], axis=0)
    for j in range(K):
        for b in range(8):
            ids_ref[8 * j + b : 8 * j + b + 1, :] = rows[8 * b + j : 8 * b + j + 1, :]
    for m in range(2):
        back_ref[m * W : (m + 1) * W, :] = dot(
            tab_ref[m * W : (m + 1) * W, :], down_ref[...], NT
        ).astype(BF)


def expert_kernel(
    got_ref, down_hbm, back_ref, base_ref, out_ref, grad_ref, hid_ref, down_ref, sems
):
    inner = down_ref.shape[0]
    loads = []
    for start in range(0, inner, 256):
        rows = pl.ds(start, min(256, inner - start))
        load = pltpu.make_async_copy(
            down_hbm.at[rows, :], down_ref.at[rows, :], sems.at[len(loads)]
        )
        load.start()
        loads.append(load)
    full = 128 * (inner // 128)
    for lanes in range(0, full, 128):
        at = 2 * ROWS * (lanes // 128)
        cols = slice(lanes, lanes + 128)
        grad_ref[:, cols] = got_ref[:, at : at + ROWS, :].reshape(ALL, 128)
        hid_ref[:, cols] = got_ref[:, at + ROWS : at + 2 * ROWS, :].reshape(ALL, 128)
    at = 2 * ROWS * (full // 128)
    tail = got_ref[:, at : at + 16, :].astype(F32)
    middle = tail[:, :, 32:64]
    grad = jnp.concatenate([tail[:, :, 0:32], middle[:, 0:8]], axis=1)
    hid = jnp.concatenate([middle[:, 8:16], tail[:, :, 64:96]], axis=1)
    grad_ref[:, full:inner] = grad.astype(BF).reshape(ALL, 32)
    hid_ref[:, full:inner] = hid.astype(BF).reshape(ALL, 32)
    total = jnp.zeros((ALL, 1), F32)
    for start in range(0, inner, 256):
        cols = slice(start, min(start + 256, inner))
        loads[start // 256].wait()
        base = dot(grad_ref[...], down_ref[cols, :], NT)
        base_ref[:, cols] = base.astype(BF)
        total = total + jnp.sum(hid_ref[:, cols].astype(F32) * base, axis=1, keepdims=True)
    high, low = split(total)
    left = dot(hid_ref[...], back_ref[0:W, :], NT)
    right = dot(hid_ref[...], back_ref[W : 2 * W, :], NT)
    proj = jnp.where(first_half(ALL, W), left, right)
    lane = iota((ALL, W), 1)
    tail = jnp.where(lane == LATER, high.astype(F32), low.astype(F32))
    tail = jnp.where(lane < LATER + 2, tail, 0.0)
    out_ref[...] = jnp.where(lane < LATER, proj, tail).astype(BF)


def picks_kernel(ids_ref, first_ref, second_ref, third_ref):
    codes = slot_codes(ids_ref)
    wide = jnp.concatenate(codes, axis=1)
    first_ref[...] = slots_by_rows(wide)
    second_ref[...] = rows_by_slots(wide)
    third_ref[...] = slots_by_rows(token_major(codes))


def id_masks(ids_ref):
    spread = one(divided(iota((8, W), 1), E) == iota((8, W), 0))
    lane = iota((N, W), 1) & (E - 1)
    masks = []
    for j in range(K):
        wide = dot(ids_ref[8 * j : 8 * j + 8, :].astype(BF), spread, TN)
        masks.append(wide == lane.astype(F32))
    return masks, spread


def blocks_kernel(got_ref, pick_ref, ids_ref, gate_ref, out_ref):
    slots = dot(pick_ref[...], got_ref[...], NN)
    gates = [gate_ref[:, k : k + 1] for k in range(K)]
    parts = [slots[k * N : (k + 1) * N] for k in range(K)]
    lane = iota((N, W), 1)
    full = []
    for part in parts:
        dots = part[:, LATER : LATER + 1] + part[:, LATER + 1 : LATER + 2]
        full.append(jnp.where(lane < LATER, part, dots))
    mean = sum(gates[k] * full[k] for k in range(K))
    masks, spread = id_masks(ids_ref)
    rows = []
    for k in range(K):
        value = gates[k] * (full[k] - mean)
        high, low = split(value)
        for j in range(K):
            source = jnp.where(masks[j] & (lane < LATER), high.astype(F32), 0.0)
            if j < 2:
                extra = high if j == 0 else low
                source = jnp.where(lane == LATER, extra.astype(F32), source)
            rows.append(source.astype(BF))
    packed = dot(spread, jnp.concatenate(rows, axis=0), NT).astype(BF)
    for d in range(8):
        out_ref[d] = packed


def solve_kernel(at_ref, got_ref, pick_ref, ids_ref, gate_ref, out_ref, coef_ref):
    at = at_ref[0]
    depth = iota((8, K * N), 0)
    found = jnp.zeros((8, K * N), F32)
    for back in range(7, -1, -1):
        where = jnp.minimum(at + back, 7)
        valid = (at + back <= 7).astype(F32)
        block = got_ref[where].astype(F32)
        fresh = []
        for k in range(K):
            part = block[:, k * K * N : (k + 1) * K * N]
            fixed = part[7:8, 0:N] + part[7:8, N : 2 * N]
            terms = jnp.sum(part * found, axis=0, keepdims=True)
            total = fixed
            for j in range(K):
                total = total + terms[:, j * N : (j + 1) * N]
            fresh.append(total * valid)
        fresh = jnp.concatenate(fresh, axis=1)
        if back:
            found = jnp.where(depth == 0, fresh, pltpu.roll(found, 1, 0))
        else:
            found = jnp.where(depth == 7, fresh, found)
    masks, spread = id_masks(ids_ref)
    high, low = split(found)
    coef = jnp.zeros((N, W), F32)
    for j in range(K):
        cut = slice(j * N, (j + 1) * N)
        wide = dot(high[:, cut], spread, TN) + dot(low[:, cut], spread, TN)
        coef = jnp.where(masks[j], wide, coef)
    coef_ref[...] = coef.astype(BF)
    same = one(iota((32, 32), 0) == iota((32, 32), 1))
    tall_high = jnp.concatenate([high[:, j * N : (j + 1) * N] for j in range(K)], axis=0)
    tall_low = jnp.concatenate([low[:, j * N : (j + 1) * N] for j in range(K)], axis=0)
    short = dot(tall_high, same, TN) + dot(tall_low, same, TN)
    names = dot(ids_ref[...].astype(BF), same, TN)
    col = iota((N, 32), 1)
    rows = []
    for k in range(K):
        gate = gate_ref[:, k : k + 1]
        up, rest = split(gate)
        value = jnp.where(col == 7, up.astype(F32), gate * short)
        value = jnp.where(col == 15, rest.astype(F32), value)
        rows.append(jnp.concatenate([value, names], axis=1).astype(BF))
    sent = dot(pick_ref[...], jnp.concatenate(rows, axis=0), NN).reshape(E, ROWS, 64)
    out_ref[:, :, 0:64] = sent[:, 0:16].astype(BF)
    rest = jnp.concatenate([sent[:, 16:24], jnp.zeros((E, 8, 64), F32)], axis=1)
    out_ref[:, :, 64:128] = rest.astype(BF)


def passed_kernel(coef_ref, tab_ref, grad_ref, acts_ref, pass_ref, part_ref):
    for m in range(2):
        rows = slice(m * T, (m + 1) * T)
        moved = dot(coef_ref[rows, :], tab_ref[m * W : (m + 1) * W, :], NN)
        pass_ref[rows, :] = (grad_ref[rows, :].astype(F32) + moved).astype(BF)
    own = coef_ref[:, LATER:W]
    width = acts_ref.shape[1]
    router = (dot(acts_ref[...], own, TN) / T).astype(BF)
    each = width // E
    ahead = jnp.concatenate([router[ROWS:], router[:ROWS]], axis=0)
    col = iota((ALL, width), 1)
    peer = divided(iota((ALL, 1), 0), ROWS)
    source = iota((ALL, 1), 0) + (each - ROWS) * peer
    select = one(source == col)
    part_ref[:, 0:E] = dot(select, router, NN).astype(BF)
    part_ref[:, E : 2 * E] = dot(select, ahead, NN).astype(BF)


def section_columns(j):
    row, col = iota((W, 32), 0), iota((W, 32), 1)
    return one((row < LATER) & ((row >> 5) + 8 * j == col))


def answer_kernel(got_ref, base_ref, back_ref, part_ref, out_ref):
    width = base_ref.shape[1]
    got = got_ref[...].astype(F32)
    got = jnp.concatenate([got[:, :, 0:64], got[:, 0:8, 64:128]], axis=1).reshape(ALL, 64)
    gate = got[:, 7:8] + got[:, 15:16]
    got = got.astype(BF)
    spread = one((iota((8, W), 1) >> 5) == iota((8, W), 0))
    lane = (iota((ALL, W), 1) & (E - 1)).astype(F32)
    coef = jnp.zeros((ALL, W), F32)
    for j in range(K):
        named = dot(got[:, 32 + 8 * j : 40 + 8 * j], spread, NN) == lane
        coef = jnp.where(named, coef + dot(got[:, 0:32], section_columns(j), NT), coef)
    half = first_half(ALL, W)
    left = jnp.where(half, coef, 0.0).astype(BF)
    right = jnp.where(half, 0.0, coef).astype(BF)
    for start in range(0, width, 256):
        cols = slice(start, min(start + 256, width))
        moved = dot(left, back_ref[0:W, cols], NN) + dot(right, back_ref[W : 2 * W, cols], NN)
        out_ref[:, cols] = (gate * base_ref[:, cols].astype(F32) + moved).astype(BF)
    out_ref[:, width : width + 2 * E] = part_ref[...]
    out_ref[:, width + 2 * E :] = jnp.zeros((ALL, out_ref.shape[1] - width - 2 * E), BF)


def combine_kernel(got_ref, pick_ref, out_ref, router_ref):
    width = out_ref.shape[2]
    for start in range(0, width, 256):
        cols = slice(start, min(start + 256, width))
        own = dot(pick_ref[...], got_ref[:, cols], NN).astype(BF)
        out_ref[:, :, cols] = own.reshape(N, K, cols.stop - start)
    parts = got_ref[:, width : width + 2 * E].astype(F32).reshape(E, ROWS, 2 * E)
    total = jnp.sum(parts, axis=0)
    each = width // E
    turn = iota((E, 2 * E), 1) - iota((E, 2 * E), 0)
    flipped = [jnp.zeros((E, ROWS), F32)] * 2
    for _ in range(3):
        piece = total.astype(BF)
        total = total - piece.astype(F32)
        flipped = [flipped[q] + dot(one(turn == q * E), piece, NT) for q in range(2)]
    router_ref[:, 0:ROWS] = flipped[0]
    router_ref[:, ROWS:each] = flipped[1][:, 0 : each - ROWS]


def call(body, shapes, args, mib, smem=0, scratch=(), sems=0, far=(), far_out=()):
    ins = [SM] * smem + [VM] * (len(args) - smem)
    ins = [HB if i in far else spec for i, spec in enumerate(ins)]
    held = [pltpu.VMEM(s, d) for s, d in scratch]
    if sems:
        held.append(pltpu.SemaphoreType.DMA((sems,)))
    return pl.pallas_call(
        body,
        out_shape=[jax.ShapeDtypeStruct(s, d) for s, d in shapes],
        in_specs=ins,
        out_specs=[HB if i in far_out else VM for i in range(len(shapes))],
        scratch_shapes=held,
        compiler_params=pltpu.CompilerParams(vmem_limit_bytes=mib << 20),
    )(*args)


def exchange(x, axis):
    return lax.all_to_all(x, axis, split_axis=0, concat_axis=0, tiled=True)


def on_device(acts, hidden, ids, version, router, down, grad_top):
    pipe = lax.axis_size("pipe")
    section = lax.axis_index("pipe")
    width = acts.shape[-1]
    inner = hidden.shape[-1]
    inputs = acts[0]
    routes = ids[0]
    mats = down[0, 0]
    grads = grad_top.reshape(N, width)
    turned = routes.transpose(0, 2, 1)
    tall = 2 * ROWS * (inner // 128) + 16

    steps = pl.cdiv(inner, 256)

    (sent,) = call(
        dispatch_kernel,
        [((E, tall, 128), BF)],
        (turned, hidden[0].reshape(N, K, inner), grads),
        MIBS[0],
        scratch=[((N, K, inner), BF), ((N, width), BF), ((E, tall, 128), BF)],
        sems=2 + steps,
        far=(1, 2),
        far_out=(0,),
    )
    arrived = exchange(sent, "expert")

    picked_version = version[0][:, None, None] == 1
    tables = jnp.where(picked_version, router[0, 1][None], router[0, 0][None])
    flipped = tables.transpose(0, 2, 1).reshape(2 * E, width)
    id_rows = jnp.pad(
        turned.transpose(1, 0, 2).reshape(K, N).astype(BF), ((0, 8 - K), (0, width - N))
    )
    own = jnp.concatenate([flipped, id_rows], axis=0)
    held = [
        lax.ppermute(own, "pipe", [(i, i - by) for i in range(by, pipe)]) for by in range(1, pipe)
    ] + [own]
    table_rows, back, id_all = call(
        tables_kernel,
        [((2 * W, width), BF), ((2 * W, inner), BF), ((K * 8, N), F32)],
        (*held, mats),
        MIBS[1],
    )

    picks = call(
        picks_kernel,
        [((N * K, ALL), BF), ((ALL, N * K), BF), ((N * K, ALL), BF)],
        (turned,),
        12,
    )
    logits = jnp.einsum("mtd,mde->mte", inputs, tables, preferred_element_type=F32)
    labels = jnp.arange(E, dtype=I32)
    picked = routes[:, :, :, None] == labels
    chosen = jnp.sum(jnp.where(picked, logits[:, :, None, :], 0.0), axis=3)
    scores = jnp.exp(chosen)
    gating = (scores / jnp.sum(scores, axis=2, keepdims=True)).reshape(N, K)

    base, proj = call(
        expert_kernel,
        [((ALL, inner), BF), ((ALL, W), BF)],
        (arrived, mats, back),
        MIBS[2],
        scratch=[((ALL, width), BF), ((ALL, inner), BF), ((inner, width), BF)],
        sems=steps,
        far=(1,),
    )
    rest = (gating, picks, id_all, section.reshape(1), grads, inputs, table_rows, back, base)
    proj, rest = lax.optimization_barrier((proj, rest))
    returned = exchange(proj.reshape(E, ROWS, W), "expert").reshape(ALL, W)
    returned, rest = lax.optimization_barrier((returned, rest))
    gating, picks, id_all, where, grads, inputs, table_rows, back, base = rest
    (blocks,) = call(
        blocks_kernel,
        [((8, 8, K * K * N), BF)],
        (returned, picks[0], id_all, gating),
        MIBS[3],
    )
    blocks, rest = lax.optimization_barrier((blocks, rest))
    gathered = exchange(blocks, "pipe")
    gathered, rest = lax.optimization_barrier((gathered, rest))
    gating, picks, id_all, where, grads, inputs, table_rows, back, base = rest
    coef_sent, coef = call(
        solve_kernel,
        [((E, 16, 128), BF), ((N, W), BF)],
        (where, gathered, picks[1], id_all, gating),
        MIBS[4],
        smem=1,
    )
    coef_sent, coef, rest = lax.optimization_barrier((coef_sent, coef, rest))
    coef_got = exchange(coef_sent, "expert")
    coef_got, coef, rest = lax.optimization_barrier((coef_got, coef, rest))
    gating, picks, id_all, where, grads, inputs, table_rows, back, base = rest
    passed, parts = call(
        passed_kernel,
        [((N, width), BF), ((ALL, 2 * E), BF)],
        (coef, table_rows, grads, inputs.reshape(N, width)),
        MIBS[5],
    )
    wide = 256 * steps
    (answer,) = call(
        answer_kernel, [((ALL, wide), BF)], (coef_got, base, back, parts), MIBS[6]
    )
    answered = exchange(answer.reshape(E, ROWS, wide), "expert").reshape(ALL, wide)
    hidden_grads, grad_router = call(
        combine_kernel, [((N, K, inner), BF), ((E, width // E), F32)], (answered, picks[2]), MIBS[7]
    )
    return (
        passed.reshape(1, 2, T, width),
        hidden_grads.reshape(1, 2, T, K, inner),
        grad_router.T[None],
    )


def solution(mesh):
    placed = (
        P("pipe", None, "expert", None),
        P("pipe", None, "expert", None, None),
        P("pipe", None, "expert", None),
        P("pipe", None),
        P("pipe", None, None, None),
        P("pipe", "expert", None, None),
        P(None, "expert", None),
    )
    return jax.shard_map(
        on_device,
        mesh=mesh,
        in_specs=placed,
        out_specs=(
            P("pipe", None, "expert", None),
            P("pipe", None, "expert", None, None),
            P("pipe", "expert", None),
        ),
        check_vma=False,
    )
```

```python
import functools

import jax
import jax.numpy as jnp
from jax import lax
from jax.experimental import pallas as pl
from jax.experimental.pallas import tpu as pltpu
from jax.sharding import PartitionSpec as P

BF = jnp.bfloat16
F32 = jnp.float32
I32 = jnp.int32
NN = (((1,), (0,)), ((), ()))
NT = (((1,), (1,)), ((), ()))
TN = (((0,), (0,)), ((), ()))
VM = pl.BlockSpec(memory_space=pltpu.VMEM)
HB = pl.BlockSpec(memory_space=pltpu.HBM)
SM = pl.BlockSpec(memory_space=pltpu.SMEM)

N, T, K, E, HALF = 128, 64, 4, 32, 12
ROWS = 2 * HALF
ALL = E * ROWS
W = 256
MIBS = (62, 20, 24, 12, 12, 16, 20, 20)
LATER = 224


def dot(a, b, dims):
    return lax.dot_general(a, b, dims, preferred_element_type=F32)


def iota(shape, dim):
    return lax.broadcasted_iota(I32, shape, dim)


def one(mask):
    return jnp.where(mask, 1.0, 0.0).astype(BF)


def divided(x, by):
    return ((x.astype(F32) + 0.5) * (1.0 / by)).astype(I32)


def split(x):
    high = x.astype(BF)
    return high, (x - high.astype(F32)).astype(BF)


def slot_codes(ids_ref):
    named = []
    for k in range(K):
        row = jnp.concatenate([ids_ref[0, k : k + 1, :], ids_ref[1, k : k + 1, :]], axis=1)
        named.append(row == iota((E, N), 0))
    marks = sum(jnp.where(hit, 1.0, 0.0) for hit in named).astype(BF)
    first, second = iota((N, N), 0), iota((N, N), 1)
    earlier = one((first < second) & ((first >> 6) == (second >> 6)))
    place = dot(marks, earlier, NN) + (HALF * (iota((E, N), 1) >> 6)).astype(F32)
    return [jnp.where(hit, place, -1.0) for hit in named]


def token_major(codes):
    lane = iota((N, N * K), 1)
    spread = one((lane >> 2) == iota((N, N * K), 0))
    which = iota((E, N * K), 1) & (K - 1)
    out = jnp.zeros((E, N * K), F32)
    for k in range(K):
        out = jnp.where(which == k, dot(codes[k].astype(BF), spread, NN), out)
    return out


def rows_by_slots(code):
    expand = one(divided(iota((ALL, E), 0), ROWS) == iota((ALL, E), 1))
    row = iota((ALL, code.shape[1]), 0)
    inner = (row - ROWS * divided(row, ROWS)).astype(F32)
    return one(dot(expand, code.astype(BF), NN) == inner)


def slots_by_rows(code):
    expand = one(divided(iota((E, ALL), 1), ROWS) == iota((E, ALL), 0))
    row = iota((code.shape[1], ALL), 1)
    inner = (row - ROWS * divided(row, ROWS)).astype(F32)
    return one(dot(code.astype(BF), expand, TN) == inner)


def first_half(rows, width, start=0):
    row = iota((rows, width), 0) + start
    return (row - ROWS * divided(row, ROWS)) < HALF


def dispatch_kernel(ids_ref, hid_hbm, grad_hbm, out_hbm, hid_ref, grad_ref, out_ref, sems):
    loads = [
        pltpu.make_async_copy(grad_hbm, grad_ref, sems.at[0]),
        pltpu.make_async_copy(hid_hbm, hid_ref, sems.at[1]),
    ]
    for load in loads:
        load.start()
    codes = slot_codes(ids_ref)
    tokens = rows_by_slots(functools.reduce(jnp.maximum, codes))
    pick = rows_by_slots(token_major(codes))
    for load in loads:
        load.wait()
    width = grad_ref.shape[1]
    stores = []
    for start in range(0, width, 256):
        cols = slice(start, min(start + 256, width))
        size = cols.stop - start
        grad = dot(tokens, grad_ref[:, cols], NN)
        hid = dot(pick, hid_ref[:, :, cols].reshape(N * K, size), NN)
        first = 2 * ROWS * (start // 128)
        for lanes in range(0, size, 128):
            at = 2 * ROWS * ((start + lanes) // 128)
            cut = min(lanes + 128, size)
            left = grad[:, lanes:cut].reshape(E, ROWS, cut - lanes)
            right = hid[:, lanes:cut].reshape(E, ROWS, cut - lanes)
            if cut - lanes == 128:
                out_ref[:, at : at + ROWS, :] = left.astype(BF)
                out_ref[:, at + ROWS : at + 2 * ROWS, :] = right.astype(BF)
                last = at + 2 * ROWS
            else:
                tail = [
                    left[:, 0:16],
                    jnp.concatenate([left[:, 16:24], right[:, 0:8]], axis=1),
                    right[:, 8:24],
                    jnp.zeros((E, 16, 32), F32),
                ]
                out_ref[:, at : at + 16, :] = jnp.concatenate(tail, axis=2).astype(BF)
                last = at + 16
        part = pl.ds(first, last - first)
        store = pltpu.make_async_copy(
            out_ref.at[:, part, :], out_hbm.at[:, part, :], sems.at[2 + len(stores)]
        )
        store.start()
        stores.append(store)
    for store in stores:
        store.wait()


def tables_kernel(*refs):
    held, down_ref, tab_ref, back_ref, ids_ref = refs[:8], refs[8], refs[9], refs[10], refs[11]
    for b in range(8):
        for m in range(2):
            tab_ref[m * W + b * E : m * W + (b + 1) * E, :] = held[b][m * E : (m + 1) * E, :]
    rows = jnp.concatenate([held[b][2 * E : 2 * E + 8, 0:N].astype(F32) for b in range(8)], axis=0)
    for j in range(K):
        for b in range(8):
            ids_ref[8 * j + b : 8 * j + b + 1, :] = rows[8 * b + j : 8 * b + j + 1, :]
    for m in range(2):
        back_ref[m * W : (m + 1) * W, :] = dot(
            tab_ref[m * W : (m + 1) * W, :], down_ref[...], NT
        ).astype(BF)


def expert_kernel(got_ref, down_ref, back_ref, base_ref, out_ref, grad_ref, hid_ref):
    inner = down_ref.shape[0]
    full = 128 * (inner // 128)
    for lanes in range(0, full, 128):
        at = 2 * ROWS * (lanes // 128)
        cols = slice(lanes, lanes + 128)
        grad_ref[:, cols] = got_ref[:, at : at + ROWS, :].reshape(ALL, 128)
        hid_ref[:, cols] = got_ref[:, at + ROWS : at + 2 * ROWS, :].reshape(ALL, 128)
    at = 2 * ROWS * (full // 128)
    tail = got_ref[:, at : at + 16, :].astype(F32)
    middle = tail[:, :, 32:64]
    grad = jnp.concatenate([tail[:, :, 0:32], middle[:, 0:8]], axis=1)
    hid = jnp.concatenate([middle[:, 8:16], tail[:, :, 64:96]], axis=1)
    grad_ref[:, full:inner] = grad.astype(BF).reshape(ALL, 32)
    hid_ref[:, full:inner] = hid.astype(BF).reshape(ALL, 32)
    total = jnp.zeros((ALL, 1), F32)
    for start in range(0, inner, 256):
        cols = slice(start, min(start + 256, inner))
        base = dot(grad_ref[...], down_ref[cols, :], NT)
        base_ref[:, cols] = base.astype(BF)
        total = total + jnp.sum(hid_ref[:, cols].astype(F32) * base, axis=1, keepdims=True)
    high, low = split(total)
    left = dot(hid_ref[...], back_ref[0:W, :], NT)
    right = dot(hid_ref[...], back_ref[W : 2 * W, :], NT)
    proj = jnp.where(first_half(ALL, W), left, right)
    lane = iota((ALL, W), 1)
    tail = jnp.where(lane == LATER, high.astype(F32), low.astype(F32))
    tail = jnp.where(lane < LATER + 2, tail, 0.0)
    out_ref[...] = jnp.where(lane < LATER, proj, tail).astype(BF)


def picks_kernel(ids_ref, first_ref, second_ref, third_ref):
    codes = slot_codes(ids_ref)
    wide = jnp.concatenate(codes, axis=1)
    first_ref[...] = slots_by_rows(wide)
    second_ref[...] = rows_by_slots(wide)
    third_ref[...] = slots_by_rows(token_major(codes))


def id_masks(ids_ref):
    spread = one(divided(iota((8, W), 1), E) == iota((8, W), 0))
    lane = iota((N, W), 1) & (E - 1)
    masks = []
    for j in range(K):
        wide = dot(ids_ref[8 * j : 8 * j + 8, :].astype(BF), spread, TN)
        masks.append(wide == lane.astype(F32))
    return masks, spread


def blocks_kernel(got_ref, pick_ref, ids_ref, gate_ref, out_ref):
    slots = dot(pick_ref[...], got_ref[...], NN)
    gates = [gate_ref[:, k : k + 1] for k in range(K)]
    parts = [slots[k * N : (k + 1) * N] for k in range(K)]
    lane = iota((N, W), 1)
    full = []
    for part in parts:
        dots = part[:, LATER : LATER + 1] + part[:, LATER + 1 : LATER + 2]
        full.append(jnp.where(lane < LATER, part, dots))
    mean = sum(gates[k] * full[k] for k in range(K))
    masks, spread = id_masks(ids_ref)
    rows = []
    for k in range(K):
        value = gates[k] * (full[k] - mean)
        high, low = split(value)
        for j in range(K):
            source = jnp.where(masks[j] & (lane < LATER), high.astype(F32), 0.0)
            if j < 2:
                extra = high if j == 0 else low
                source = jnp.where(lane == LATER, extra.astype(F32), source)
            rows.append(source.astype(BF))
    packed = dot(spread, jnp.concatenate(rows, axis=0), NT).astype(BF)
    for d in range(8):
        out_ref[d] = packed


def solve_kernel(at_ref, got_ref, pick_ref, ids_ref, gate_ref, out_ref, coef_ref):
    at = at_ref[0]
    depth = iota((8, K * N), 0)
    found = jnp.zeros((8, K * N), F32)
    for back in range(7, -1, -1):
        where = jnp.minimum(at + back, 7)
        valid = (at + back <= 7).astype(F32)
        block = got_ref[where].astype(F32)
        fresh = []
        for k in range(K):
            part = block[:, k * K * N : (k + 1) * K * N]
            fixed = part[7:8, 0:N] + part[7:8, N : 2 * N]
            terms = jnp.sum(part * found, axis=0, keepdims=True)
            total = fixed
            for j in range(K):
                total = total + terms[:, j * N : (j + 1) * N]
            fresh.append(total * valid)
        fresh = jnp.concatenate(fresh, axis=1)
        if back:
            found = jnp.where(depth == 0, fresh, pltpu.roll(found, 1, 0))
        else:
            found = jnp.where(depth == 7, fresh, found)
    masks, spread = id_masks(ids_ref)
    high, low = split(found)
    coef = jnp.zeros((N, W), F32)
    for j in range(K):
        cut = slice(j * N, (j + 1) * N)
        wide = dot(high[:, cut], spread, TN) + dot(low[:, cut], spread, TN)
        coef = jnp.where(masks[j], wide, coef)
    coef_ref[...] = coef.astype(BF)
    same = one(iota((32, 32), 0) == iota((32, 32), 1))
    tall_high = jnp.concatenate([high[:, j * N : (j + 1) * N] for j in range(K)], axis=0)
    tall_low = jnp.concatenate([low[:, j * N : (j + 1) * N] for j in range(K)], axis=0)
    short = dot(tall_high, same, TN) + dot(tall_low, same, TN)
    names = dot(ids_ref[...].astype(BF), same, TN)
    col = iota((N, 32), 1)
    rows = []
    for k in range(K):
        gate = gate_ref[:, k : k + 1]
        up, rest = split(gate)
        value = jnp.where(col == 7, up.astype(F32), gate * short)
        value = jnp.where(col == 15, rest.astype(F32), value)
        rows.append(jnp.concatenate([value, names], axis=1).astype(BF))
    sent = dot(pick_ref[...], jnp.concatenate(rows, axis=0), NN).reshape(E, ROWS, 64)
    out_ref[:, :, 0:64] = sent[:, 0:16].astype(BF)
    rest = jnp.concatenate([sent[:, 16:24], jnp.zeros((E, 8, 64), F32)], axis=1)
    out_ref[:, :, 64:128] = rest.astype(BF)


def section_columns(j):
    row, col = iota((W, 32), 0), iota((W, 32), 1)
    return one((row < LATER) & ((row >> 5) + 8 * j == col))


def answer_kernel(
    got_ref, base_ref, back_ref, coef_ref, tab_ref, grad_ref, acts_ref, out_ref, pass_hbm, pass_ref, sems
):
    for m in range(2):
        rows = slice(m * T, (m + 1) * T)
        moved = dot(coef_ref[rows, :], tab_ref[m * W : (m + 1) * W, :], NN)
        pass_ref[rows, :] = (grad_ref[rows, :].astype(F32) + moved).astype(BF)
    store = pltpu.make_async_copy(pass_ref, pass_hbm, sems.at[0])
    store.start()
    own = coef_ref[:, LATER:W]
    width = acts_ref.shape[1]
    router = (dot(acts_ref[...], own, TN) / T).astype(BF)
    each = width // E
    ahead = jnp.concatenate([router[ROWS:], router[:ROWS]], axis=0)
    col = iota((ALL, width), 1)
    peer = divided(iota((ALL, 1), 0), ROWS)
    source = iota((ALL, 1), 0) + (each - ROWS) * peer
    select = one(source == col)
    out_ref[:, width : width + E] = dot(select, router, NN).astype(BF)
    out_ref[:, width + E : width + 2 * E] = dot(select, ahead, NN).astype(BF)
    out_ref[:, width + 2 * E :] = jnp.zeros((ALL, out_ref.shape[1] - width - 2 * E), BF)
    got = got_ref[...].astype(F32)
    got = jnp.concatenate([got[:, :, 0:64], got[:, 0:8, 64:128]], axis=1).reshape(ALL, 64)
    gate = got[:, 7:8] + got[:, 15:16]
    got = got.astype(BF)
    spread = one((iota((8, W), 1) >> 5) == iota((8, W), 0))
    lane = (iota((ALL, W), 1) & (E - 1)).astype(F32)
    coef = jnp.zeros((ALL, W), F32)
    for j in range(K):
        named = dot(got[:, 32 + 8 * j : 40 + 8 * j], spread, NN) == lane
        coef = jnp.where(named, coef + dot(got[:, 0:32], section_columns(j), NT), coef)
    half = first_half(ALL, W)
    left = jnp.where(half, coef, 0.0).astype(BF)
    right = jnp.where(half, 0.0, coef).astype(BF)
    for start in range(0, width, 256):
        cols = slice(start, min(start + 256, width))
        moved = dot(left, back_ref[0:W, cols], NN) + dot(right, back_ref[W : 2 * W, cols], NN)
        out_ref[:, cols] = (gate * base_ref[:, cols].astype(F32) + moved).astype(BF)
    store.wait()


def combine_kernel(got_ref, pick_ref, out_ref, router_ref):
    width = out_ref.shape[2]
    for start in range(0, width, 256):
        cols = slice(start, min(start + 256, width))
        own = dot(pick_ref[...], got_ref[:, cols], NN).astype(BF)
        out_ref[:, :, cols] = own.reshape(N, K, cols.stop - start)
    parts = got_ref[:, width : width + 2 * E].astype(F32).reshape(E, ROWS, 2 * E)
    total = jnp.sum(parts, axis=0)
    each = width // E
    turn = iota((E, 2 * E), 1) - iota((E, 2 * E), 0)
    flipped = [jnp.zeros((E, ROWS), F32)] * 2
    for _ in range(3):
        piece = total.astype(BF)
        total = total - piece.astype(F32)
        flipped = [flipped[q] + dot(one(turn == q * E), piece, NT) for q in range(2)]
    router_ref[:, 0:ROWS] = flipped[0]
    router_ref[:, ROWS:each] = flipped[1][:, 0 : each - ROWS]


def call(body, shapes, args, mib, smem=0, scratch=(), sems=0, far=(), far_out=()):
    ins = [SM] * smem + [VM] * (len(args) - smem)
    ins = [HB if i in far else spec for i, spec in enumerate(ins)]
    held = [pltpu.VMEM(s, d) for s, d in scratch]
    if sems:
        held.append(pltpu.SemaphoreType.DMA((sems,)))
    return pl.pallas_call(
        body,
        out_shape=[jax.ShapeDtypeStruct(s, d) for s, d in shapes],
        in_specs=ins,
        out_specs=[HB if i in far_out else VM for i in range(len(shapes))],
        scratch_shapes=held,
        compiler_params=pltpu.CompilerParams(vmem_limit_bytes=mib << 20),
    )(*args)


def exchange(x, axis):
    return lax.all_to_all(x, axis, split_axis=0, concat_axis=0, tiled=True)


def on_device(acts, hidden, ids, version, router, down, grad_top):
    pipe = lax.axis_size("pipe")
    section = lax.axis_index("pipe")
    width = acts.shape[-1]
    inner = hidden.shape[-1]
    inputs = acts[0]
    routes = ids[0]
    mats = down[0, 0]
    grads = grad_top.reshape(N, width)
    turned = routes.transpose(0, 2, 1)
    tall = 2 * ROWS * (inner // 128) + 16

    steps = pl.cdiv(inner, 256)

    (sent,) = call(
        dispatch_kernel,
        [((E, tall, 128), BF)],
        (turned, hidden[0].reshape(N, K, inner), grads),
        MIBS[0],
        scratch=[((N, K, inner), BF), ((N, width), BF), ((E, tall, 128), BF)],
        sems=2 + steps,
        far=(1, 2),
        far_out=(0,),
    )
    arrived = exchange(sent, "expert")

    picked_version = version[0][:, None, None] == 1
    tables = jnp.where(picked_version, router[0, 1][None], router[0, 0][None])
    flipped = tables.transpose(0, 2, 1).reshape(2 * E, width)
    id_rows = jnp.pad(
        turned.transpose(1, 0, 2).reshape(K, N).astype(BF), ((0, 8 - K), (0, width - N))
    )
    own = jnp.concatenate([flipped, id_rows], axis=0)
    held = [
        lax.ppermute(own, "pipe", [(i, i - by) for i in range(by, pipe)]) for by in range(1, pipe)
    ] + [own]
    table_rows, back, id_all = call(
        tables_kernel,
        [((2 * W, width), BF), ((2 * W, inner), BF), ((K * 8, N), F32)],
        (*held, mats),
        MIBS[1],
    )

    picks = call(
        picks_kernel,
        [((N * K, ALL), BF), ((ALL, N * K), BF), ((N * K, ALL), BF)],
        (turned,),
        12,
    )
    logits = jnp.einsum("mtd,mde->mte", inputs, tables, preferred_element_type=F32)
    labels = jnp.arange(E, dtype=I32)
    picked = routes[:, :, :, None] == labels
    chosen = jnp.sum(jnp.where(picked, logits[:, :, None, :], 0.0), axis=3)
    scores = jnp.exp(chosen)
    gating = (scores / jnp.sum(scores, axis=2, keepdims=True)).reshape(N, K)

    base, proj = call(
        expert_kernel,
        [((ALL, inner), BF), ((ALL, W), BF)],
        (arrived, mats, back),
        MIBS[2],
        scratch=[((ALL, width), BF), ((ALL, inner), BF)],
    )
    rest = (gating, picks, id_all, section.reshape(1), grads, inputs, table_rows, back, base)
    proj, rest = lax.optimization_barrier((proj, rest))
    returned = exchange(proj.reshape(E, ROWS, W), "expert").reshape(ALL, W)
    returned, rest = lax.optimization_barrier((returned, rest))
    gating, picks, id_all, where, grads, inputs, table_rows, back, base = rest
    (blocks,) = call(
        blocks_kernel,
        [((8, 8, K * K * N), BF)],
        (returned, picks[0], id_all, gating),
        MIBS[3],
    )
    blocks, rest = lax.optimization_barrier((blocks, rest))
    gathered = exchange(blocks, "pipe")
    gathered, rest = lax.optimization_barrier((gathered, rest))
    gating, picks, id_all, where, grads, inputs, table_rows, back, base = rest
    coef_sent, coef = call(
        solve_kernel,
        [((E, 16, 128), BF), ((N, W), BF)],
        (where, gathered, picks[1], id_all, gating),
        MIBS[4],
        smem=1,
    )
    coef_sent, coef, rest = lax.optimization_barrier((coef_sent, coef, rest))
    coef_got = exchange(coef_sent, "expert")
    coef_got, coef, rest = lax.optimization_barrier((coef_got, coef, rest))
    gating, picks, id_all, where, grads, inputs, table_rows, back, base = rest
    wide = 256 * steps
    answer, passed = call(
        answer_kernel,
        [((ALL, wide), BF), ((N, width), BF)],
        (coef_got, base, back, coef, table_rows, grads, inputs.reshape(N, width)),
        MIBS[6],
        scratch=[((N, width), BF)],
        sems=1,
        far_out=(1,),
    )
    answered = exchange(answer.reshape(E, ROWS, wide), "expert").reshape(ALL, wide)
    hidden_grads, grad_router = call(
        combine_kernel, [((N, K, inner), BF), ((E, width // E), F32)], (answered, picks[2]), MIBS[7]
    )
    return (
        passed.reshape(1, 2, T, width),
        hidden_grads.reshape(1, 2, T, K, inner),
        grad_router.T[None],
    )


def solution(mesh):
    placed = (
        P("pipe", None, "expert", None),
        P("pipe", None, "expert", None, None),
        P("pipe", None, "expert", None),
        P("pipe", None),
        P("pipe", None, None, None),
        P("pipe", "expert", None, None),
        P(None, "expert", None),
    )
    return jax.shard_map(
        on_device,
        mesh=mesh,
        in_specs=placed,
        out_specs=(
            P("pipe", None, "expert", None),
            P("pipe", None, "expert", None, None),
            P("pipe", "expert", None),
        ),
        check_vma=False,
    )
```

```python
import functools

import jax
import jax.numpy as jnp
from jax import lax
from jax.experimental import pallas as pl
from jax.experimental.pallas import tpu as pltpu
from jax.sharding import PartitionSpec as P

BF = jnp.bfloat16
F32 = jnp.float32
I32 = jnp.int32
NN = (((1,), (0,)), ((), ()))
NT = (((1,), (1,)), ((), ()))
TN = (((0,), (0,)), ((), ()))
VM = pl.BlockSpec(memory_space=pltpu.VMEM)
HB = pl.BlockSpec(memory_space=pltpu.HBM)
SM = pl.BlockSpec(memory_space=pltpu.SMEM)

N, T, K, E, HALF = 128, 64, 4, 32, 12
ROWS = 2 * HALF
ALL = E * ROWS
W = 256
MIBS = (62, 20, 24, 12, 12, 16, 20, 20)
LATER = 224


def dot(a, b, dims):
    return lax.dot_general(a, b, dims, preferred_element_type=F32)


def iota(shape, dim):
    return lax.broadcasted_iota(I32, shape, dim)


def one(mask):
    return jnp.where(mask, 1.0, 0.0).astype(BF)


def divided(x, by):
    return ((x.astype(F32) + 0.5) * (1.0 / by)).astype(I32)


def split(x):
    high = x.astype(BF)
    return high, (x - high.astype(F32)).astype(BF)


def slot_codes(ids_ref):
    named = []
    for k in range(K):
        row = jnp.concatenate([ids_ref[0, k : k + 1, :], ids_ref[1, k : k + 1, :]], axis=1)
        named.append(row == iota((E, N), 0))
    marks = sum(jnp.where(hit, 1.0, 0.0) for hit in named).astype(BF)
    first, second = iota((N, N), 0), iota((N, N), 1)
    earlier = one((first < second) & ((first >> 6) == (second >> 6)))
    place = dot(marks, earlier, NN) + (HALF * (iota((E, N), 1) >> 6)).astype(F32)
    return [jnp.where(hit, place, -1.0) for hit in named]


def token_major(codes):
    lane = iota((N, N * K), 1)
    spread = one((lane >> 2) == iota((N, N * K), 0))
    which = iota((E, N * K), 1) & (K - 1)
    out = jnp.zeros((E, N * K), F32)
    for k in range(K):
        out = jnp.where(which == k, dot(codes[k].astype(BF), spread, NN), out)
    return out


def rows_by_slots(code):
    expand = one(divided(iota((ALL, E), 0), ROWS) == iota((ALL, E), 1))
    row = iota((ALL, code.shape[1]), 0)
    inner = (row - ROWS * divided(row, ROWS)).astype(F32)
    return one(dot(expand, code.astype(BF), NN) == inner)


def slots_by_rows(code):
    expand = one(divided(iota((E, ALL), 1), ROWS) == iota((E, ALL), 0))
    row = iota((code.shape[1], ALL), 1)
    inner = (row - ROWS * divided(row, ROWS)).astype(F32)
    return one(dot(code.astype(BF), expand, TN) == inner)


def first_half(rows, width, start=0):
    row = iota((rows, width), 0) + start
    return (row - ROWS * divided(row, ROWS)) < HALF


def dispatch_kernel(ids_ref, hid_hbm, grad_hbm, out_hbm, hid_ref, grad_ref, out_ref, sems):
    loads = [
        pltpu.make_async_copy(grad_hbm, grad_ref, sems.at[0]),
        pltpu.make_async_copy(hid_hbm, hid_ref, sems.at[1]),
    ]
    for load in loads:
        load.start()
    codes = slot_codes(ids_ref)
    tokens = rows_by_slots(functools.reduce(jnp.maximum, codes))
    pick = rows_by_slots(token_major(codes))
    for load in loads:
        load.wait()
    width = grad_ref.shape[1]
    stores = []
    for start in range(0, width, 256):
        cols = slice(start, min(start + 256, width))
        size = cols.stop - start
        grad = dot(tokens, grad_ref[:, cols], NN)
        hid = dot(pick, hid_ref[:, :, cols].reshape(N * K, size), NN)
        first = 2 * ROWS * (start // 128)
        for lanes in range(0, size, 128):
            at = 2 * ROWS * ((start + lanes) // 128)
            cut = min(lanes + 128, size)
            left = grad[:, lanes:cut].reshape(E, ROWS, cut - lanes)
            right = hid[:, lanes:cut].reshape(E, ROWS, cut - lanes)
            if cut - lanes == 128:
                out_ref[:, at : at + ROWS, :] = left.astype(BF)
                out_ref[:, at + ROWS : at + 2 * ROWS, :] = right.astype(BF)
                last = at + 2 * ROWS
            else:
                tail = [
                    left[:, 0:16],
                    jnp.concatenate([left[:, 16:24], right[:, 0:8]], axis=1),
                    right[:, 8:24],
                    jnp.zeros((E, 16, 32), F32),
                ]
                out_ref[:, at : at + 16, :] = jnp.concatenate(tail, axis=2).astype(BF)
                last = at + 16
        part = pl.ds(first, last - first)
        store = pltpu.make_async_copy(
            out_ref.at[:, part, :], out_hbm.at[:, part, :], sems.at[2 + len(stores)]
        )
        store.start()
        stores.append(store)
    for store in stores:
        store.wait()


def tables_kernel(*refs):
    held, down_ref, tab_ref, back_ref, ids_ref = refs[:8], refs[8], refs[9], refs[10], refs[11]
    for b in range(8):
        for m in range(2):
            tab_ref[m * W + b * E : m * W + (b + 1) * E, :] = held[b][m * E : (m + 1) * E, :]
    rows = jnp.concatenate([held[b][2 * E : 2 * E + 8, 0:N].astype(F32) for b in range(8)], axis=0)
    for j in range(K):
        for b in range(8):
            ids_ref[8 * j + b : 8 * j + b + 1, :] = rows[8 * b + j : 8 * b + j + 1, :]
    for m in range(2):
        back_ref[m * W : (m + 1) * W, :] = dot(
            tab_ref[m * W : (m + 1) * W, :], down_ref[...], NT
        ).astype(BF)


def expert_kernel(got_ref, down_ref, back_ref, base_ref, out_ref, grad_ref, hid_ref):
    inner = down_ref.shape[0]
    full = 128 * (inner // 128)
    for lanes in range(0, full, 128):
        at = 2 * ROWS * (lanes // 128)
        cols = slice(lanes, lanes + 128)
        grad_ref[:, cols] = got_ref[:, at : at + ROWS, :].reshape(ALL, 128)
        hid_ref[:, cols] = got_ref[:, at + ROWS : at + 2 * ROWS, :].reshape(ALL, 128)
    at = 2 * ROWS * (full // 128)
    tail = got_ref[:, at : at + 16, :].astype(F32)
    middle = tail[:, :, 32:64]
    grad = jnp.concatenate([tail[:, :, 0:32], middle[:, 0:8]], axis=1)
    hid = jnp.concatenate([middle[:, 8:16], tail[:, :, 64:96]], axis=1)
    grad_ref[:, full:inner] = grad.astype(BF).reshape(ALL, 32)
    hid_ref[:, full:inner] = hid.astype(BF).reshape(ALL, 32)
    total = jnp.zeros((ALL, 1), F32)
    for start in range(0, inner, 256):
        cols = slice(start, min(start + 256, inner))
        base = dot(grad_ref[...], down_ref[cols, :], NT)
        base_ref[:, cols] = base.astype(BF)
        total = total + jnp.sum(hid_ref[:, cols].astype(F32) * base, axis=1, keepdims=True)
    high, low = split(total)
    left = dot(hid_ref[...], back_ref[0:W, :], NT)
    right = dot(hid_ref[...], back_ref[W : 2 * W, :], NT)
    proj = jnp.where(first_half(ALL, W), left, right)
    lane = iota((ALL, W), 1)
    tail = jnp.where(lane == LATER, high.astype(F32), low.astype(F32))
    tail = jnp.where(lane < LATER + 2, tail, 0.0)
    out_ref[...] = jnp.where(lane < LATER, proj, tail).astype(BF)


def picks_kernel(ids_ref, first_ref, second_ref, third_ref, router_ref):
    codes = slot_codes(ids_ref)
    wide = jnp.concatenate(codes, axis=1)
    first_ref[...] = slots_by_rows(wide)
    second_ref[...] = rows_by_slots(wide)
    third_ref[...] = slots_by_rows(token_major(codes))
    width = router_ref.shape[1]
    peer = divided(iota((ALL, 1), 0), ROWS)
    source = iota((ALL, 1), 0) + (width // E - ROWS) * peer
    router_ref[...] = one(source == iota((ALL, width), 1))


def id_masks(ids_ref):
    spread = one(divided(iota((8, W), 1), E) == iota((8, W), 0))
    lane = iota((N, W), 1) & (E - 1)
    masks = []
    for j in range(K):
        wide = dot(ids_ref[8 * j : 8 * j + 8, :].astype(BF), spread, TN)
        masks.append(wide == lane.astype(F32))
    return masks, spread


def blocks_kernel(got_ref, pick_ref, ids_ref, gate_ref, out_ref):
    slots = dot(pick_ref[...], got_ref[...], NN)
    gates = [gate_ref[:, k : k + 1] for k in range(K)]
    parts = [slots[k * N : (k + 1) * N] for k in range(K)]
    lane = iota((N, W), 1)
    full = []
    for part in parts:
        dots = part[:, LATER : LATER + 1] + part[:, LATER + 1 : LATER + 2]
        full.append(jnp.where(lane < LATER, part, dots))
    mean = sum(gates[k] * full[k] for k in range(K))
    masks, spread = id_masks(ids_ref)
    rows = []
    for k in range(K):
        value = gates[k] * (full[k] - mean)
        high, low = split(value)
        for j in range(K):
            source = jnp.where(masks[j] & (lane < LATER), high.astype(F32), 0.0)
            if j < 2:
                extra = high if j == 0 else low
                source = jnp.where(lane == LATER, extra.astype(F32), source)
            rows.append(source.astype(BF))
    packed = dot(spread, jnp.concatenate(rows, axis=0), NT).astype(BF)
    for d in range(8):
        out_ref[d] = packed


def solve_kernel(at_ref, got_ref, pick_ref, ids_ref, gate_ref, out_ref, coef_ref):
    at = at_ref[0]
    depth = iota((8, K * N), 0)
    found = jnp.zeros((8, K * N), F32)
    for back in range(7, -1, -1):
        where = jnp.minimum(at + back, 7)
        valid = (at + back <= 7).astype(F32)
        block = got_ref[where].astype(F32)
        fresh = []
        for k in range(K):
            part = block[:, k * K * N : (k + 1) * K * N]
            fixed = part[7:8, 0:N] + part[7:8, N : 2 * N]
            terms = jnp.sum(part * found, axis=0, keepdims=True)
            total = fixed
            for j in range(K):
                total = total + terms[:, j * N : (j + 1) * N]
            fresh.append(total * valid)
        fresh = jnp.concatenate(fresh, axis=1)
        if back:
            found = jnp.where(depth == 0, fresh, pltpu.roll(found, 1, 0))
        else:
            found = jnp.where(depth == 7, fresh, found)
    masks, spread = id_masks(ids_ref)
    high, low = split(found)
    coef = jnp.zeros((N, W), F32)
    for j in range(K):
        cut = slice(j * N, (j + 1) * N)
        wide = dot(high[:, cut], spread, TN) + dot(low[:, cut], spread, TN)
        coef = jnp.where(masks[j], wide, coef)
    coef_ref[...] = coef.astype(BF)
    same = one(iota((32, 32), 0) == iota((32, 32), 1))
    tall_high = jnp.concatenate([high[:, j * N : (j + 1) * N] for j in range(K)], axis=0)
    tall_low = jnp.concatenate([low[:, j * N : (j + 1) * N] for j in range(K)], axis=0)
    short = dot(tall_high, same, TN) + dot(tall_low, same, TN)
    names = dot(ids_ref[...].astype(BF), same, TN)
    col = iota((N, 32), 1)
    rows = []
    for k in range(K):
        gate = gate_ref[:, k : k + 1]
        up, rest = split(gate)
        value = jnp.where(col == 7, up.astype(F32), gate * short)
        value = jnp.where(col == 15, rest.astype(F32), value)
        rows.append(jnp.concatenate([value, names], axis=1).astype(BF))
    sent = dot(pick_ref[...], jnp.concatenate(rows, axis=0), NN).reshape(E, ROWS, 64)
    out_ref[:, :, 0:64] = sent[:, 0:16].astype(BF)
    rest = jnp.concatenate([sent[:, 16:24], jnp.zeros((E, 8, 64), F32)], axis=1)
    out_ref[:, :, 64:128] = rest.astype(BF)


def section_columns(j):
    row, col = iota((W, 32), 0), iota((W, 32), 1)
    return one((row < LATER) & ((row >> 5) + 8 * j == col))


def answer_kernel(
    got_ref, base_ref, back_ref, coef_ref, tab_ref, grad_ref, acts_ref, select_ref,
    out_ref, pass_hbm, pass_ref, sems,
):
    for m in range(2):
        rows = slice(m * T, (m + 1) * T)
        moved = dot(coef_ref[rows, :], tab_ref[m * W : (m + 1) * W, :], NN)
        pass_ref[rows, :] = (grad_ref[rows, :].astype(F32) + moved).astype(BF)
    store = pltpu.make_async_copy(pass_ref, pass_hbm, sems.at[0])
    store.start()
    own = coef_ref[:, LATER:W]
    width = acts_ref.shape[1]
    router = (dot(acts_ref[...], own, TN) / T).astype(BF)
    ahead = jnp.concatenate([router[ROWS:], router[:ROWS]], axis=0)
    select = select_ref[...]
    out_ref[:, width : width + E] = dot(select, router, NN).astype(BF)
    out_ref[:, width + E : width + 2 * E] = dot(select, ahead, NN).astype(BF)
    out_ref[:, width + 2 * E :] = jnp.zeros((ALL, out_ref.shape[1] - width - 2 * E), BF)
    got = got_ref[...].astype(F32)
    got = jnp.concatenate([got[:, :, 0:64], got[:, 0:8, 64:128]], axis=1).reshape(ALL, 64)
    gate = got[:, 7:8] + got[:, 15:16]
    got = got.astype(BF)
    spread = one((iota((8, W), 1) >> 5) == iota((8, W), 0))
    lane = (iota((ALL, W), 1) & (E - 1)).astype(F32)
    coef = jnp.zeros((ALL, W), F32)
    for j in range(K):
        named = dot(got[:, 32 + 8 * j : 40 + 8 * j], spread, NN) == lane
        coef = jnp.where(named, coef + dot(got[:, 0:32], section_columns(j), NT), coef)
    half = first_half(ALL, W)
    left = jnp.where(half, coef, 0.0).astype(BF)
    right = jnp.where(half, 0.0, coef).astype(BF)
    for start in range(0, width, 256):
        cols = slice(start, min(start + 256, width))
        moved = dot(left, back_ref[0:W, cols], NN) + dot(right, back_ref[W : 2 * W, cols], NN)
        out_ref[:, cols] = (gate * base_ref[:, cols].astype(F32) + moved).astype(BF)
    store.wait()


def combine_kernel(got_ref, pick_ref, out_ref, router_ref):
    width = out_ref.shape[2]
    for start in range(0, width, 256):
        cols = slice(start, min(start + 256, width))
        own = dot(pick_ref[...], got_ref[:, cols], NN).astype(BF)
        out_ref[:, :, cols] = own.reshape(N, K, cols.stop - start)
    parts = got_ref[:, width : width + 2 * E].astype(F32).reshape(E, ROWS, 2 * E)
    total = jnp.sum(parts, axis=0)
    each = width // E
    turn = iota((E, 2 * E), 1) - iota((E, 2 * E), 0)
    flipped = [jnp.zeros((E, ROWS), F32)] * 2
    for _ in range(3):
        piece = total.astype(BF)
        total = total - piece.astype(F32)
        flipped = [flipped[q] + dot(one(turn == q * E), piece, NT) for q in range(2)]
    router_ref[:, 0:ROWS] = flipped[0]
    router_ref[:, ROWS:each] = flipped[1][:, 0 : each - ROWS]


def call(body, shapes, args, mib, smem=0, scratch=(), sems=0, far=(), far_out=()):
    ins = [SM] * smem + [VM] * (len(args) - smem)
    ins = [HB if i in far else spec for i, spec in enumerate(ins)]
    held = [pltpu.VMEM(s, d) for s, d in scratch]
    if sems:
        held.append(pltpu.SemaphoreType.DMA((sems,)))
    return pl.pallas_call(
        body,
        out_shape=[jax.ShapeDtypeStruct(s, d) for s, d in shapes],
        in_specs=ins,
        out_specs=[HB if i in far_out else VM for i in range(len(shapes))],
        scratch_shapes=held,
        compiler_params=pltpu.CompilerParams(vmem_limit_bytes=mib << 20),
    )(*args)


def exchange(x, axis):
    return lax.all_to_all(x, axis, split_axis=0, concat_axis=0, tiled=True)


def on_device(acts, hidden, ids, version, router, down, grad_top):
    pipe = lax.axis_size("pipe")
    section = lax.axis_index("pipe")
    width = acts.shape[-1]
    inner = hidden.shape[-1]
    inputs = acts[0]
    routes = ids[0]
    mats = down[0, 0]
    grads = grad_top.reshape(N, width)
    turned = routes.transpose(0, 2, 1)
    tall = 2 * ROWS * (inner // 128) + 16

    steps = pl.cdiv(inner, 256)

    (sent,) = call(
        dispatch_kernel,
        [((E, tall, 128), BF)],
        (turned, hidden[0].reshape(N, K, inner), grads),
        MIBS[0],
        scratch=[((N, K, inner), BF), ((N, width), BF), ((E, tall, 128), BF)],
        sems=2 + steps,
        far=(1, 2),
        far_out=(0,),
    )
    arrived = exchange(sent, "expert")

    picked_version = version[0][:, None, None] == 1
    tables = jnp.where(picked_version, router[0, 1][None], router[0, 0][None])
    flipped = tables.transpose(0, 2, 1).reshape(2 * E, width)
    id_rows = jnp.pad(
        turned.transpose(1, 0, 2).reshape(K, N).astype(BF), ((0, 8 - K), (0, width - N))
    )
    own = jnp.concatenate([flipped, id_rows], axis=0)
    held = [
        lax.ppermute(own, "pipe", [(i, i - by) for i in range(by, pipe)]) for by in range(1, pipe)
    ] + [own]
    table_rows, back, id_all = call(
        tables_kernel,
        [((2 * W, width), BF), ((2 * W, inner), BF), ((K * 8, N), F32)],
        (*held, mats),
        MIBS[1],
    )

    picks = call(
        picks_kernel,
        [((N * K, ALL), BF), ((ALL, N * K), BF), ((N * K, ALL), BF), ((ALL, width), BF)],
        (turned,),
        12,
    )
    logits = jnp.einsum("mtd,mde->mte", inputs, tables, preferred_element_type=F32)
    labels = jnp.arange(E, dtype=I32)
    picked = routes[:, :, :, None] == labels
    chosen = jnp.sum(jnp.where(picked, logits[:, :, None, :], 0.0), axis=3)
    scores = jnp.exp(chosen)
    gating = (scores / jnp.sum(scores, axis=2, keepdims=True)).reshape(N, K)

    base, proj = call(
        expert_kernel,
        [((ALL, inner), BF), ((ALL, W), BF)],
        (arrived, mats, back),
        MIBS[2],
        scratch=[((ALL, width), BF), ((ALL, inner), BF)],
    )
    rest = (gating, picks, id_all, section.reshape(1), grads, inputs, table_rows, back, base)
    proj, rest = lax.optimization_barrier((proj, rest))
    returned = exchange(proj.reshape(E, ROWS, W), "expert").reshape(ALL, W)
    returned, rest = lax.optimization_barrier((returned, rest))
    gating, picks, id_all, where, grads, inputs, table_rows, back, base = rest
    (blocks,) = call(
        blocks_kernel,
        [((8, 8, K * K * N), BF)],
        (returned, picks[0], id_all, gating),
        MIBS[3],
    )
    blocks, rest = lax.optimization_barrier((blocks, rest))
    gathered = exchange(blocks, "pipe")
    gathered, rest = lax.optimization_barrier((gathered, rest))
    gating, picks, id_all, where, grads, inputs, table_rows, back, base = rest
    coef_sent, coef = call(
        solve_kernel,
        [((E, 16, 128), BF), ((N, W), BF)],
        (where, gathered, picks[1], id_all, gating),
        MIBS[4],
        smem=1,
    )
    coef_sent, coef, rest = lax.optimization_barrier((coef_sent, coef, rest))
    coef_got = exchange(coef_sent, "expert")
    coef_got, coef, rest = lax.optimization_barrier((coef_got, coef, rest))
    gating, picks, id_all, where, grads, inputs, table_rows, back, base = rest
    wide = 256 * steps
    answer, passed = call(
        answer_kernel,
        [((ALL, wide), BF), ((N, width), BF)],
        (coef_got, base, back, coef, table_rows, grads, inputs.reshape(N, width), picks[3]),
        MIBS[6],
        scratch=[((N, width), BF)],
        sems=1,
        far_out=(1,),
    )
    answered = exchange(answer.reshape(E, ROWS, wide), "expert").reshape(ALL, wide)
    hidden_grads, grad_router = call(
        combine_kernel, [((N, K, inner), BF), ((E, width // E), F32)], (answered, picks[2]), MIBS[7]
    )
    return (
        passed.reshape(1, 2, T, width),
        hidden_grads.reshape(1, 2, T, K, inner),
        grad_router.T[None],
    )


def solution(mesh):
    placed = (
        P("pipe", None, "expert", None),
        P("pipe", None, "expert", None, None),
        P("pipe", None, "expert", None),
        P("pipe", None),
        P("pipe", None, None, None),
        P("pipe", "expert", None, None),
        P(None, "expert", None),
    )
    return jax.shard_map(
        on_device,
        mesh=mesh,
        in_specs=placed,
        out_specs=(
            P("pipe", None, "expert", None),
            P("pipe", None, "expert", None, None),
            P("pipe", "expert", None),
        ),
        check_vma=False,
    )
```
